256 devices in a mesh: ctx: 32 (over z, y), tp: 8 (over x, core).
Axes of the slice: x: 4, y: 4, z: 8, core: 2. Of those that a mesh axis runs over, the one named last changes fastest.
Arguments:
- tokens: bfloat16 [24576, 4096], P(('ctx', 'tp')), may hold values from -6 to 6
- norm_gain: float32 [4096], replicated, may hold values from 0.1 to 1.9
- w_qkv: bfloat16 [4096, 8192], P('ctx', 'tp'), may hold values from -0.09375 to 0.09375
- w_out: bfloat16 [4096, 4096], P('tp', 'ctx'), may hold values from -0.09375 to 0.09375
- head_gain: float32 [4096], P('tp'), may hold values from 0.1 to 1.9
- input_codes: int32 [8, 24576], P('tp', 'ctx'), may hold values from -4 to 4
- forget_codes: int32 [8, 24576], P('tp', 'ctx'), may hold values from -24 to 4
- forget_bias: float32 [8], P('tp'), may hold values from 3 to 13.5, as said below
- document_begin_flags: int32 [24576], P('ctx'), may hold values 0 or 1
Outputs:
- mixed: bfloat16 [24576, 4096], P(('ctx', 'tp'))
The draws below stay inside these ranges and needn't reach their ends.
Inputs may be any that keep to these rules, and one draw needn't show every extreme that they name: `forget_bias`: a bias for each head.
All inputs are finite; a program needn't handle non-finite values. No bound on the sum of `document_begin_flags` on one device may be relied on, other than what follows from the above.
Results may differ from the reference program's by a relative error of at most 0.017.
Values may be sent and summed in bfloat16 or wider, within the bound.
A program may use at most 64 MiB of HBM per device.

```python
import jax
import jax.numpy as jnp
from jax import lax

D = 4096
H = 8
DK = 256
DV = 512
TOK_DEV = 768
HEADS_DEV = 1
STREAM_LENGTH = 24576
N_TP = 8


def draw_forget_codes(key, part):
    perturbation_seed, segment_seed_handle, spike_seed_handle = jax.random.split(key, 3)
    blocks = STREAM_LENGTH // TOK_DEV
    jitter = jax.random.randint(perturbation_seed, (H, STREAM_LENGTH), -2, 3, dtype=jnp.int32)
    offsets = jax.random.randint(segment_seed_handle, (H, blocks), -2, 3, dtype=jnp.int32)
    spread = jnp.repeat(offsets, TOK_DEV, axis=1)
    destination_places = jax.random.randint(spike_seed_handle, (3,), 0, STREAM_LENGTH, dtype=jnp.int32)
    position = jnp.arange(STREAM_LENGTH, dtype=jnp.int32)
    bursting = jnp.any(position[None, :] == destination_places[:, None], axis=0)
    return jnp.where(bursting[None, :], jnp.int32(-24), jitter + spread)


def draw_forget_bias(key, part):
    order_key, slow_key, fast_key = jax.random.split(key, 3)
    ranking = jax.random.permutation(order_key, H)
    slow_count = H // 2
    slowness = ranking < slow_count
    slow_value = jax.random.uniform(slow_key, (H,), jnp.float32, 12.0, 13.5)
    fast_value = jax.random.uniform(fast_key, (H,), jnp.float32, 3.0, 4.0)
    return jnp.where(slowness, slow_value, fast_value)


def with_ends(drawn, stream_key, low, high):
    longest = drawn.shape.index(max(drawn.shape))
    spots = []
    for shift in (0, 1):
        where = [jax.random.randint(jax.random.fold_in(stream_key, axis), (), 0, length) for axis, length in enumerate(drawn.shape)]
        where[longest] = (where[longest] + shift) % drawn.shape[longest]
        spots.append(tuple(where))
    return drawn.at[spots[0]].set(low).at[spots[1]].set(high)


def level_of(own_key, dims, cuts, smallest, top_value):
    level, own = 1.0, jax.random.fold_in(own_key, 6)
    for dim, shards_of in cuts:
        heights = jnp.exp(jax.random.uniform(jax.random.fold_in(own, dim), (shards_of,), jnp.float32, smallest / len(cuts), top_value / len(cuts)))
        level = level * jnp.repeat(heights, dims[dim] // shards_of).reshape([-1 if axis == dim else 1 for axis in range(len(dims))])
    return level


def gaussian(own_key, dims, deviation, bound, shards=(), kind=jnp.bfloat16):
    loudness = level_of(own_key, dims, shards, -0.22, 0.18) if shards else 1.0
    values = jax.random.normal(own_key, dims, jnp.float32) * deviation * loudness
    return jnp.minimum(jnp.maximum(values, -bound), bound).astype(kind)


def setup_inputs(seed: int = 0) -> dict:
    key_of = jax.random.split(jax.random.key(seed), 10)
    tokens = gaussian(key_of[0], (STREAM_LENGTH, D), 1.0, 6.0, ((0, 256),))
    norm_gain = jnp.clip(1.0 + 0.18 * jax.random.normal(key_of[1], (D,), jnp.float32), 0.1, 1.9)
    w_qkv = gaussian(key_of[2], (D, H * (2 * DK + DV)), D ** -0.5, 0.09375, ((0, 32), (1, 8)))
    w_out = gaussian(key_of[3], (H * DV, D), (H * DV) ** -0.5, 0.09375, ((0, 8), (1, 32)))
    head_gain = jnp.clip(1.0 + 0.18 * jax.random.normal(key_of[4], (H * DV,), jnp.float32), 0.1, 1.9)
    input_codes = with_ends(jax.random.randint(key_of[5], (H, STREAM_LENGTH), -4, 5), jax.random.fold_in(key_of[5], 1), -4, 4).astype(jnp.int32)
    forget_codes = draw_forget_codes(jax.random.fold_in(key_of[9], 71), 0)
    forget_bias = draw_forget_bias(jax.random.fold_in(key_of[9], 71), 0)
    document_begin_flags = with_ends((jax.random.randint(key_of[8], (STREAM_LENGTH,), 0, 8 * TOK_DEV) < 1).astype(jnp.int32), jax.random.fold_in(key_of[8], 1), 0, 1)
    return dict(tokens=tokens, norm_gain=norm_gain, w_qkv=w_qkv, w_out=w_out, head_gain=head_gain, input_codes=input_codes, forget_codes=forget_codes, forget_bias=forget_bias, document_begin_flags=document_begin_flags)


EPSILON = 1e-06
FORGET_STEP = 0.5
INPUT_STEP = 0.5

def rms_rows(embedded_entries, norm_gain):
    token_float = embedded_entries.astype(jnp.float32)
    moment = lax.optimization_barrier(jnp.mean(token_float * token_float, axis=1, keepdims=True))
    return (token_float * lax.rsqrt(moment + EPSILON) * norm_gain).astype(jnp.bfloat16)

def local_terms(queries, key_rows, values, log_forget, input_gate, starts):
    length = queries.shape[0]
    scaling = queries.shape[1] ** (-0.5)
    segment = jnp.cumsum(starts)
    levels = jnp.cumsum(log_forget)
    position = jnp.arange(length)
    allowed = (position[:, None] >= position[None, :]) & (segment[:, None] == segment[None, :])
    decays = jnp.where(allowed, jnp.exp(jnp.minimum(levels[:, None] - levels[None, :], 0.0) + input_gate[None, :]), 0.0)
    scores = jnp.dot(queries, key_rows.T, preferred_element_type=jnp.float32) * scaling
    weights = (scores * decays).astype(jnp.bfloat16)
    inner_part = jnp.dot(weights, values, preferred_element_type=jnp.float32)
    last_level = levels[-1]
    last_seg = segment[-1]
    keeping = jnp.where(segment == last_seg, jnp.exp(last_level - levels + input_gate), 0.0)
    weighted = (key_rows.astype(jnp.float32) * keeping[:, None]).astype(jnp.bfloat16)
    local_state = lax.dot_general(weighted, values, (((0,), (0,)), ((), ())), preferred_element_type=jnp.float32)
    passing = jnp.where(last_seg == 0, jnp.exp(last_level), 0.0)
    carried = jnp.where(segment == 0, jnp.exp(levels), 0.0) * scaling
    return (inner_part, local_state, passing, carried)

def apply_state(queries, carried, incoming):
    lifted = queries.astype(jnp.float32) * carried[:, None]
    return jnp.dot(lifted, incoming, precision=lax.Precision.HIGHEST, preferred_element_type=jnp.float32)

def head_norm(head_out, gain):
    centre = lax.optimization_barrier(jnp.mean(head_out, axis=1, keepdims=True))
    shifted = head_out - centre
    spread = lax.optimization_barrier(jnp.mean(shifted * shifted, axis=1, keepdims=True))
    return (shifted * lax.rsqrt(spread + EPSILON) * gain).astype(jnp.bfloat16)

def reference(tokens, norm_gain, w_qkv, w_out, head_gain, input_codes, forget_codes, forget_bias, document_begin_flags):
    normed = rms_rows(tokens, norm_gain)
    stride = 2 * DK + DV
    blocks = STREAM_LENGTH // TOK_DEV

    def one_head(inputs):
        attention_slot_number, input_row, forget_row, bias_value, gain_row = inputs
        columns = lax.dynamic_slice_in_dim(w_qkv, attention_slot_number * stride, stride, 1)
        rows_combined = jnp.dot(normed, columns, preferred_element_type=jnp.float32).astype(jnp.bfloat16)
        queries = rows_combined[:, :DK].reshape(blocks, TOK_DEV, DK)
        key_rows = rows_combined[:, DK:2 * DK].reshape(blocks, TOK_DEV, DK)
        values = rows_combined[:, 2 * DK:].reshape(blocks, TOK_DEV, DV)
        log_forget = jax.nn.log_sigmoid(FORGET_STEP * forget_row.astype(jnp.float32) + bias_value)
        input_gate = INPUT_STEP * input_row.astype(jnp.float32)

        def advance(state, block_data):
            query_block, key_block, value_block, forget_block, gate_block, start_block = block_data
            inner_part, local_state, passing, carried = local_terms(query_block, key_block, value_block, forget_block, gate_block, start_block)
            head_out = inner_part + apply_state(query_block, carried, state)
            return (passing * state + local_state, head_out)
        initial = jnp.zeros((DK, DV), jnp.float32)
        block_data = (queries, key_rows, values, log_forget.reshape(blocks, TOK_DEV), input_gate.reshape(blocks, TOK_DEV), document_begin_flags.reshape(blocks, TOK_DEV))
        _, outputs = lax.scan(advance, initial, block_data)
        return head_norm(outputs.reshape(STREAM_LENGTH, DV), gain_row)
    indices = jnp.arange(H, dtype=jnp.int32)
    heads_normed = lax.map(one_head, (indices, input_codes, forget_codes, forget_bias, head_gain.reshape(H, DV)))
    running = tokens.astype(jnp.float32)
    for group in range(N_TP):
        group_heads = heads_normed[group * HEADS_DEV:(group + 1) * HEADS_DEV]
        flattened = jnp.transpose(group_heads, (1, 0, 2)).reshape(STREAM_LENGTH, HEADS_DEV * DV)
        group_rows = w_out[group * HEADS_DEV * DV:(group + 1) * HEADS_DEV * DV]
        group_part = jnp.dot(flattened, group_rows, preferred_element_type=jnp.float32).astype(jnp.bfloat16)
        group_part = lax.optimization_barrier(group_part)
        running = running + group_part.astype(jnp.float32)
    return running.astype(jnp.bfloat16)
```

```python
import jax
import jax.numpy as jnp
from jax import lax
from jax.sharding import PartitionSpec as P

DK = 256
DV = 512


EPSILON = 1e-06
FORGET_STEP = 0.5
INPUT_STEP = 0.5


def carried_in(passing, state, axis):
    count = lax.axis_size(axis)
    if count == 1:
        return jnp.zeros_like(state)

    def shifted(part, k, kind):
        pairs = [(i, i + k) for i in range(count - k)]
        return lax.ppermute(part.astype(kind), axis, pairs).astype(jnp.float32)

    decay = shifted(passing, 1, jnp.float32)
    total = shifted(state, 1, jnp.bfloat16)
    if count > 2:
        decay_far = shifted(passing, 2, jnp.float32)
        total_far = shifted(state, 2, jnp.bfloat16)
        total = decay[:, None, None] * total_far + total
        decay = decay * decay_far
    k = 2
    while k < count:
        decay_far = shifted(decay, k, jnp.float32)
        total_far = shifted(total, k, jnp.bfloat16)
        total = decay[:, None, None] * total_far + total
        decay = decay * decay_far
        k *= 2
    return total


def rms_rows(embedded_entries, norm_gain):
    token_float = embedded_entries.astype(jnp.float32)
    moment = jnp.mean(token_float * token_float, axis=1, keepdims=True)
    return (token_float * lax.rsqrt(moment + EPSILON) * norm_gain).astype(jnp.bfloat16)


def local_terms(queries, key_rows, values, log_forget, input_gate, starts):
    length = queries.shape[0]
    scaling = queries.shape[1] ** (-0.5)
    segment = jnp.cumsum(starts)
    levels = jnp.cumsum(log_forget)
    position = jnp.arange(length)
    allowed = (position[:, None] >= position[None, :]) & (segment[:, None] == segment[None, :])
    decays = jnp.where(
        allowed,
        jnp.exp(jnp.minimum(levels[:, None] - levels[None, :], 0.0) + input_gate[None, :]),
        0.0,
    )
    scores = jnp.dot(queries, key_rows.T, preferred_element_type=jnp.float32) * scaling
    weights = (scores * decays).astype(jnp.bfloat16)
    inner_part = jnp.dot(weights, values, preferred_element_type=jnp.float32)
    last_level = levels[-1]
    last_seg = segment[-1]
    keeping = jnp.where(segment == last_seg, jnp.exp(last_level - levels + input_gate), 0.0)
    weighted = (key_rows.astype(jnp.float32) * keeping[:, None]).astype(jnp.bfloat16)
    local_state = lax.dot_general(
        weighted, values, (((0,), (0,)), ((), ())), preferred_element_type=jnp.float32
    )
    passing = jnp.where(last_seg == 0, jnp.exp(last_level), 0.0)
    carried = jnp.where(segment == 0, jnp.exp(levels), 0.0) * scaling
    return (inner_part, local_state, passing, carried)


def apply_state(queries, carried, incoming):
    lifted = queries.astype(jnp.float32) * carried[:, None]
    return jnp.dot(
        lifted, incoming, precision=lax.Precision.HIGHEST, preferred_element_type=jnp.float32
    )


def head_norm(head_out, gain):
    centre = jnp.mean(head_out, axis=1, keepdims=True)
    shifted = head_out - centre
    spread = jnp.mean(shifted * shifted, axis=1, keepdims=True)
    return (shifted * lax.rsqrt(spread + EPSILON) * gain).astype(jnp.bfloat16)


def local(
    tokens,
    norm_gain,
    w_qkv,
    w_out,
    head_gain,
    input_codes,
    forget_codes,
    forget_bias,
    document_begin_flags,
):
    normed = rms_rows(tokens, norm_gain)
    every_row_list = lax.all_gather(normed, "tp", axis=0, tiled=True)
    parameter_collection = lax.all_gather(w_qkv, "ctx", axis=0, tiled=True)
    rows_combined = jnp.dot(
        every_row_list, parameter_collection, preferred_element_type=jnp.float32
    )
    rows_combined = rows_combined.astype(jnp.bfloat16)
    heads_here = forget_bias.shape[0]
    stride = 2 * DK + DV
    query_list, inner_list, state_list, passing_list, carried_list = ([], [], [], [], [])
    attention_slot_number = 0
    offset = attention_slot_number * stride
    queries = rows_combined[:, offset : offset + DK]
    key_rows = rows_combined[:, offset + DK : offset + 2 * DK]
    values = rows_combined[:, offset + 2 * DK : offset + stride]
    log_forget = jax.nn.log_sigmoid(
        FORGET_STEP * forget_codes[attention_slot_number].astype(jnp.float32)
        + forget_bias[attention_slot_number]
    )
    input_gate = INPUT_STEP * input_codes[attention_slot_number].astype(jnp.float32)
    inner_part, local_state, passing, carried = local_terms(
        queries, key_rows, values, log_forget, input_gate, document_begin_flags
    )
    query_list.append(queries)
    inner_list.append(inner_part)
    state_list.append(local_state)
    passing_list.append(passing)
    carried_list.append(carried)
    incoming = carried_in(jnp.stack(passing_list), jnp.stack(state_list), "ctx")
    attention_slot_number = 0
    head_out = inner_list[attention_slot_number] + apply_state(
        query_list[attention_slot_number],
        carried_list[attention_slot_number],
        incoming[attention_slot_number],
    )
    normed_heads = head_norm(head_out, head_gain)
    out_columns = lax.all_gather(w_out, "ctx", axis=1, tiled=True)
    summed = lax.psum_scatter(
        jnp.dot(normed_heads, out_columns, preferred_element_type=jnp.float32).astype(jnp.bfloat16),
        "tp",
        scatter_dimension=0,
        tiled=True,
    ).astype(jnp.float32)
    return (tokens.astype(jnp.float32) + summed).astype(jnp.bfloat16)


def solution(mesh):
    placed = (
        P(("ctx", "tp"), None),
        P(),
        P("ctx", "tp"),
        P("tp", "ctx"),
        P("tp"),
        P("tp", "ctx"),
        P("tp", "ctx"),
        P("tp"),
        P("ctx"),
    )
    return jax.shard_map(
        local, mesh=mesh, in_specs=placed, out_specs=P(("ctx", "tp"), None), check_vma=False
    )
```

```python
import jax
import jax.numpy as jnp
from jax import lax
from jax.sharding import PartitionSpec as P

DK = 256
DV = 512


EPSILON = 1e-06
FORGET_STEP = 0.5
INPUT_STEP = 0.5


def carried_in(passing, state, axis):
    count = lax.axis_size(axis)
    if count == 1:
        return jnp.zeros_like(state)
    heads, rows, width = state.shape
    pad = 16

    def shifted(decay, total, k):
        high = decay.astype(jnp.bfloat16)
        low = (decay - high.astype(jnp.float32)).astype(jnp.bfloat16)
        extra = jnp.zeros((heads, pad, width), jnp.bfloat16)
        extra = extra.at[:, 0, 0].set(high).at[:, 0, 1].set(low)
        message = jnp.concatenate([total.astype(jnp.bfloat16), extra], axis=1)
        pairs = [(i, i + k) for i in range(count - k)]
        got = lax.ppermute(message, axis, pairs)
        got_decay = got[:, rows, 0].astype(jnp.float32) + got[:, rows, 1].astype(jnp.float32)
        return got_decay, got[:, :rows].astype(jnp.float32)

    decay, total = shifted(passing, state, 1)
    if count > 2:
        decay_far, total_far = shifted(passing, state, 2)
        total = decay[:, None, None] * total_far + total
        decay = decay * decay_far
    k = 2
    while k < count:
        decay_far, total_far = shifted(decay, total, k)
        total = decay[:, None, None] * total_far + total
        decay = decay * decay_far
        k *= 2
    return total


def rms_rows(embedded_entries, norm_gain):
    token_float = embedded_entries.astype(jnp.float32)
    moment = jnp.mean(token_float * token_float, axis=1, keepdims=True)
    return (token_float * lax.rsqrt(moment + EPSILON) * norm_gain).astype(jnp.bfloat16)


def local_terms(queries, key_rows, values, log_forget, input_gate, starts):
    length = queries.shape[0]
    scaling = queries.shape[1] ** (-0.5)
    segment = jnp.cumsum(starts)
    levels = jnp.cumsum(log_forget)
    position = jnp.arange(length)
    allowed = (position[:, None] >= position[None, :]) & (segment[:, None] == segment[None, :])
    decays = jnp.where(
        allowed,
        jnp.exp(jnp.minimum(levels[:, None] - levels[None, :], 0.0) + input_gate[None, :]),
        0.0,
    )
    scores = jnp.dot(queries, key_rows.T, preferred_element_type=jnp.float32) * scaling
    weights = (scores * decays).astype(jnp.bfloat16)
    inner_part = jnp.dot(weights, values, preferred_element_type=jnp.float32)
    last_level = levels[-1]
    last_seg = segment[-1]
    keeping = jnp.where(segment == last_seg, jnp.exp(last_level - levels + input_gate), 0.0)
    weighted = (key_rows.astype(jnp.float32) * keeping[:, None]).astype(jnp.bfloat16)
    local_state = lax.dot_general(
        weighted, values, (((0,), (0,)), ((), ())), preferred_element_type=jnp.float32
    )
    passing = jnp.where(last_seg == 0, jnp.exp(last_level), 0.0)
    carried = jnp.where(segment == 0, jnp.exp(levels), 0.0) * scaling
    return (inner_part, local_state, passing, carried)


def apply_state(queries, carried, incoming):
    lifted = queries.astype(jnp.float32) * carried[:, None]
    return jnp.dot(
        lifted, incoming, precision=lax.Precision.HIGHEST, preferred_element_type=jnp.float32
    )


def head_norm(head_out, gain):
    centre = jnp.mean(head_out, axis=1, keepdims=True)
    shifted = head_out - centre
    spread = jnp.mean(shifted * shifted, axis=1, keepdims=True)
    return (shifted * lax.rsqrt(spread + EPSILON) * gain).astype(jnp.bfloat16)


def local(
    tokens,
    norm_gain,
    w_qkv,
    w_out,
    head_gain,
    input_codes,
    forget_codes,
    forget_bias,
    document_begin_flags,
):
    normed = rms_rows(tokens, norm_gain)
    every_row_list = lax.all_gather(normed, "tp", axis=0, tiled=True)
    parameter_collection = lax.all_gather(w_qkv, "ctx", axis=0, tiled=True)
    rows_combined = jnp.dot(
        every_row_list, parameter_collection, preferred_element_type=jnp.float32
    )
    rows_combined = rows_combined.astype(jnp.bfloat16)
    heads_here = forget_bias.shape[0]
    stride = 2 * DK + DV
    query_list, inner_list, state_list, passing_list, carried_list = ([], [], [], [], [])
    attention_slot_number = 0
    offset = attention_slot_number * stride
    queries = rows_combined[:, offset : offset + DK]
    key_rows = rows_combined[:, offset + DK : offset + 2 * DK]
    values = rows_combined[:, offset + 2 * DK : offset + stride]
    log_forget = jax.nn.log_sigmoid(
        FORGET_STEP * forget_codes[attention_slot_number].astype(jnp.float32)
        + forget_bias[attention_slot_number]
    )
    input_gate = INPUT_STEP * input_codes[attention_slot_number].astype(jnp.float32)
    inner_part, local_state, passing, carried = local_terms(
        queries, key_rows, values, log_forget, input_gate, document_begin_flags
    )
    query_list.append(queries)
    inner_list.append(inner_part)
    state_list.append(local_state)
    passing_list.append(passing)
    carried_list.append(carried)
    incoming = carried_in(jnp.stack(passing_list), jnp.stack(state_list), "ctx")
    attention_slot_number = 0
    head_out = inner_list[attention_slot_number] + apply_state(
        query_list[attention_slot_number],
        carried_list[attention_slot_number],
        incoming[attention_slot_number],
    )
    normed_heads = head_norm(head_out, head_gain)
    out_columns = lax.all_gather(w_out, "ctx", axis=1, tiled=True)
    summed = lax.psum_scatter(
        jnp.dot(normed_heads, out_columns, preferred_element_type=jnp.float32).astype(jnp.bfloat16),
        "tp",
        scatter_dimension=0,
        tiled=True,
    ).astype(jnp.float32)
    return (tokens.astype(jnp.float32) + summed).astype(jnp.bfloat16)


def solution(mesh):
    placed = (
        P(("ctx", "tp"), None),
        P(),
        P("ctx", "tp"),
        P("tp", "ctx"),
        P("tp"),
        P("tp", "ctx"),
        P("tp", "ctx"),
        P("tp"),
        P("ctx"),
    )
    return jax.shard_map(
        local, mesh=mesh, in_specs=placed, out_specs=P(("ctx", "tp"), None), check_vma=False
    )
```

```python
import jax
import jax.numpy as jnp
from jax import lax
from jax.sharding import PartitionSpec as P

DK = 256
DV = 512


EPSILON = 1e-06
FORGET_STEP = 0.5
INPUT_STEP = 0.5


def carried_in(passing, state, axis):
    count = lax.axis_size(axis)
    if count == 1:
        return jnp.zeros_like(state)
    heads, rows, width = state.shape
    pad = 16

    def shifted(decay, total, k):
        high = decay.astype(jnp.bfloat16)
        low = (decay - high.astype(jnp.float32)).astype(jnp.bfloat16)
        extra = jnp.zeros((heads, pad, width), jnp.bfloat16)
        extra = extra.at[:, 0, 0].set(high).at[:, 0, 1].set(low)
        message = jnp.concatenate([total.astype(jnp.bfloat16), extra], axis=1)
        pairs = [(i, i + k) for i in range(count - k)]
        got = lax.ppermute(message, axis, pairs)
        got_decay = got[:, rows, 0].astype(jnp.float32) + got[:, rows, 1].astype(jnp.float32)
        return got_decay, got[:, :rows].astype(jnp.float32)

    decay, total = shifted(passing, state, 1)
    if count > 2:
        decay_far, total_far = shifted(passing, state, 2)
        total = decay[:, None, None] * total_far + total
        decay = decay * decay_far
    k = 2
    while k < count:
        decay_far, total_far = shifted(decay, total, k)
        total = decay[:, None, None] * total_far + total
        decay = decay * decay_far
        k *= 2
    return total


def rms_rows(embedded_entries, norm_gain):
    token_float = embedded_entries.astype(jnp.float32)
    moment = jnp.mean(token_float * token_float, axis=1, keepdims=True)
    return (token_float * lax.rsqrt(moment + EPSILON) * norm_gain).astype(jnp.bfloat16)


def local_terms(queries, key_rows, values, log_forget, input_gate, starts):
    length = queries.shape[0]
    scaling = queries.shape[1] ** (-0.5)
    segment = jnp.cumsum(starts)
    levels = jnp.cumsum(log_forget)
    position = jnp.arange(length)
    allowed = (position[:, None] >= position[None, :]) & (segment[:, None] == segment[None, :])
    decays = jnp.where(
        allowed,
        jnp.exp(jnp.minimum(levels[:, None] - levels[None, :], 0.0) + input_gate[None, :]),
        0.0,
    )
    scores = jnp.dot(queries, key_rows.T, preferred_element_type=jnp.float32) * scaling
    weights = (scores * decays).astype(jnp.bfloat16)
    inner_part = jnp.dot(weights, values, preferred_element_type=jnp.float32)
    last_level = levels[-1]
    last_seg = segment[-1]
    keeping = jnp.where(segment == last_seg, jnp.exp(last_level - levels + input_gate), 0.0)
    weighted = (key_rows.astype(jnp.float32) * keeping[:, None]).astype(jnp.bfloat16)
    local_state = lax.dot_general(
        weighted, values, (((0,), (0,)), ((), ())), preferred_element_type=jnp.float32
    )
    passing = jnp.where(last_seg == 0, jnp.exp(last_level), 0.0)
    carried = jnp.where(segment == 0, jnp.exp(levels), 0.0) * scaling
    return (inner_part, local_state, passing, carried)


def apply_state(queries, carried, incoming):
    lifted = queries.astype(jnp.float32) * carried[:, None]
    return jnp.dot(
        lifted, incoming, precision=lax.Precision.HIGHEST, preferred_element_type=jnp.float32
    )


def head_norm(head_out, gain):
    centre = jnp.mean(head_out, axis=1, keepdims=True)
    shifted = head_out - centre
    spread = jnp.mean(shifted * shifted, axis=1, keepdims=True)
    return (shifted * lax.rsqrt(spread + EPSILON) * gain).astype(jnp.bfloat16)


def local(
    tokens,
    norm_gain,
    w_qkv,
    w_out,
    head_gain,
    input_codes,
    forget_codes,
    forget_bias,
    document_begin_flags,
):
    normed = rms_rows(tokens, norm_gain)
    group = lax.axis_size("tp")
    copies = jnp.broadcast_to(normed[None], (group,) + normed.shape)
    every_row_list = lax.all_to_all(copies, "tp", 0, 0, tiled=True).reshape(-1, normed.shape[1])
    parameter_collection = lax.all_gather(w_qkv, "ctx", axis=0, tiled=True)
    rows_combined = jnp.dot(
        every_row_list, parameter_collection, preferred_element_type=jnp.float32
    )
    rows_combined = rows_combined.astype(jnp.bfloat16)
    heads_here = forget_bias.shape[0]
    stride = 2 * DK + DV
    query_list, inner_list, state_list, passing_list, carried_list = ([], [], [], [], [])
    attention_slot_number = 0
    offset = attention_slot_number * stride
    queries = rows_combined[:, offset : offset + DK]
    key_rows = rows_combined[:, offset + DK : offset + 2 * DK]
    values = rows_combined[:, offset + 2 * DK : offset + stride]
    log_forget = jax.nn.log_sigmoid(
        FORGET_STEP * forget_codes[attention_slot_number].astype(jnp.float32)
        + forget_bias[attention_slot_number]
    )
    input_gate = INPUT_STEP * input_codes[attention_slot_number].astype(jnp.float32)
    inner_part, local_state, passing, carried = local_terms(
        queries, key_rows, values, log_forget, input_gate, document_begin_flags
    )
    query_list.append(queries)
    inner_list.append(inner_part)
    state_list.append(local_state)
    passing_list.append(passing)
    carried_list.append(carried)
    incoming = carried_in(jnp.stack(passing_list), jnp.stack(state_list), "ctx")
    attention_slot_number = 0
    head_out = inner_list[attention_slot_number] + apply_state(
        query_list[attention_slot_number],
        carried_list[attention_slot_number],
        incoming[attention_slot_number],
    )
    normed_heads = head_norm(head_out, head_gain)
    out_columns = lax.all_gather(w_out, "ctx", axis=1, tiled=True)
    summed = lax.psum_scatter(
        jnp.dot(normed_heads, out_columns, preferred_element_type=jnp.float32).astype(jnp.bfloat16),
        "tp",
        scatter_dimension=0,
        tiled=True,
    ).astype(jnp.float32)
    return (tokens.astype(jnp.float32) + summed).astype(jnp.bfloat16)


def solution(mesh):
    placed = (
        P(("ctx", "tp"), None),
        P(),
        P("ctx", "tp"),
        P("tp", "ctx"),
        P("tp"),
        P("tp", "ctx"),
        P("tp", "ctx"),
        P("tp"),
        P("ctx"),
    )
    return jax.shard_map(
        local, mesh=mesh, in_specs=placed, out_specs=P(("ctx", "tp"), None), check_vma=False
    )
```

```python
import jax
import jax.numpy as jnp
from jax import lax
from jax.sharding import PartitionSpec as P

DK = 256
DV = 512


EPSILON = 1e-06
FORGET_STEP = 0.5
INPUT_STEP = 0.5


def carried_in(passing, state, axis):
    count = lax.axis_size(axis)
    if count == 1:
        return jnp.zeros_like(state)
    heads, rows, width = state.shape
    pad = 16

    def shifted(decay, total, k):
        high = decay.astype(jnp.bfloat16)
        low = (decay - high.astype(jnp.float32)).astype(jnp.bfloat16)
        extra = jnp.zeros((heads, pad, width), jnp.bfloat16)
        extra = extra.at[:, 0, 0].set(high).at[:, 0, 1].set(low)
        message = jnp.concatenate([total.astype(jnp.bfloat16), extra], axis=1)
        pairs = [(i, i + k) for i in range(count - k)]
        got = lax.ppermute(message, axis, pairs)
        got_decay = got[:, rows, 0].astype(jnp.float32) + got[:, rows, 1].astype(jnp.float32)
        return got_decay, got[:, :rows].astype(jnp.float32)

    decay, total = shifted(passing, state, 1)
    if count > 2:
        decay_far, total_far = shifted(passing, state, 2)
        total = decay[:, None, None] * total_far + total
        decay = decay * decay_far
    k = 2
    while k < count:
        decay_far, total_far = shifted(decay, total, k)
        total = decay[:, None, None] * total_far + total
        decay = decay * decay_far
        k *= 2
    return total


def rms_rows(embedded_entries, norm_gain):
    token_float = embedded_entries.astype(jnp.float32)
    moment = jnp.mean(token_float * token_float, axis=1, keepdims=True)
    return (token_float * lax.rsqrt(moment + EPSILON) * norm_gain).astype(jnp.bfloat16)


def local_terms(queries, key_rows, values, log_forget, input_gate, starts):
    length = queries.shape[0]
    scaling = queries.shape[1] ** (-0.5)
    segment = jnp.cumsum(starts)
    levels = jnp.cumsum(log_forget)
    position = jnp.arange(length)
    allowed = (position[:, None] >= position[None, :]) & (segment[:, None] == segment[None, :])
    decays = jnp.where(
        allowed,
        jnp.exp(jnp.minimum(levels[:, None] - levels[None, :], 0.0) + input_gate[None, :]),
        0.0,
    )
    scores = jnp.dot(queries, key_rows.T, preferred_element_type=jnp.float32) * scaling
    weights = (scores * decays).astype(jnp.bfloat16)
    inner_part = jnp.dot(weights, values, preferred_element_type=jnp.float32)
    last_level = levels[-1]
    last_seg = segment[-1]
    keeping = jnp.where(segment == last_seg, jnp.exp(last_level - levels + input_gate), 0.0)
    weighted = (key_rows.astype(jnp.float32) * keeping[:, None]).astype(jnp.bfloat16)
    local_state = lax.dot_general(
        weighted, values, (((0,), (0,)), ((), ())), preferred_element_type=jnp.float32
    )
    passing = jnp.where(last_seg == 0, jnp.exp(last_level), 0.0)
    carried = jnp.where(segment == 0, jnp.exp(levels), 0.0) * scaling
    return (inner_part, local_state, passing, carried)


def apply_state(queries, carried, incoming):
    lifted = queries.astype(jnp.float32) * carried[:, None]
    return jnp.dot(
        lifted, incoming, precision=lax.Precision.HIGHEST, preferred_element_type=jnp.float32
    )


def head_norm(head_out, gain):
    centre = jnp.mean(head_out, axis=1, keepdims=True)
    shifted = head_out - centre
    spread = jnp.mean(shifted * shifted, axis=1, keepdims=True)
    return (shifted * lax.rsqrt(spread + EPSILON) * gain).astype(jnp.bfloat16)


def local(
    tokens,
    norm_gain,
    w_qkv,
    w_out,
    head_gain,
    input_codes,
    forget_codes,
    forget_bias,
    document_begin_flags,
):
    normed = rms_rows(tokens, norm_gain)
    group = lax.axis_size("tp")
    copies = jnp.broadcast_to(normed[None], (group,) + normed.shape)
    every_row_list = lax.all_to_all(copies, "tp", 0, 0, tiled=True).reshape(-1, normed.shape[1])
    parameter_collection = lax.all_gather(w_qkv, "ctx", axis=0, tiled=True)
    rows_combined = jnp.dot(
        every_row_list, parameter_collection, preferred_element_type=jnp.float32
    )
    rows_combined = rows_combined.astype(jnp.bfloat16)
    heads_here = forget_bias.shape[0]
    stride = 2 * DK + DV
    query_list, inner_list, state_list, passing_list, carried_list = ([], [], [], [], [])
    attention_slot_number = 0
    offset = attention_slot_number * stride
    queries = rows_combined[:, offset : offset + DK]
    key_rows = rows_combined[:, offset + DK : offset + 2 * DK]
    values = rows_combined[:, offset + 2 * DK : offset + stride]
    log_forget = jax.nn.log_sigmoid(
        FORGET_STEP * forget_codes[attention_slot_number].astype(jnp.float32)
        + forget_bias[attention_slot_number]
    )
    input_gate = INPUT_STEP * input_codes[attention_slot_number].astype(jnp.float32)
    inner_part, local_state, passing, carried = local_terms(
        queries, key_rows, values, log_forget, input_gate, document_begin_flags
    )
    query_list.append(queries)
    inner_list.append(inner_part)
    state_list.append(local_state)
    passing_list.append(passing)
    carried_list.append(carried)
    incoming = carried_in(jnp.stack(passing_list), jnp.stack(state_list), "ctx")
    attention_slot_number = 0
    head_out = inner_list[attention_slot_number] + apply_state(
        query_list[attention_slot_number],
        carried_list[attention_slot_number],
        incoming[attention_slot_number],
    )
    normed_heads = head_norm(head_out, head_gain)
    out_rows = lax.all_gather(w_out.T, "ctx", axis=0, tiled=True)
    projected = lax.dot_general(
        normed_heads, out_rows, (((1,), (1,)), ((), ())), preferred_element_type=jnp.float32
    )
    summed = lax.psum_scatter(
        projected.astype(jnp.bfloat16),
        "tp",
        scatter_dimension=0,
        tiled=True,
    ).astype(jnp.float32)
    return (tokens.astype(jnp.float32) + summed).astype(jnp.bfloat16)


def solution(mesh):
    placed = (
        P(("ctx", "tp"), None),
        P(),
        P("ctx", "tp"),
        P("tp", "ctx"),
        P("tp"),
        P("tp", "ctx"),
        P("tp", "ctx"),
        P("tp"),
        P("ctx"),
    )
    return jax.shard_map(
        local, mesh=mesh, in_specs=placed, out_specs=P(("ctx", "tp"), None), check_vma=False
    )
```

```python
import jax
import jax.numpy as jnp
from jax import lax
from jax.sharding import PartitionSpec as P

DK = 256
DV = 512


EPSILON = 1e-06
FORGET_STEP = 0.5
INPUT_STEP = 0.5


def carried_in(passing, state, axis):
    count = lax.axis_size(axis)
    if count == 1:
        return jnp.zeros_like(state)
    heads, rows, width = state.shape
    pad = 16

    def shifted(decay, total, k):
        high = decay.astype(jnp.bfloat16)
        low = (decay - high.astype(jnp.float32)).astype(jnp.bfloat16)
        extra = jnp.zeros((heads, pad, width), jnp.bfloat16)
        extra = extra.at[:, 0, 0].set(high).at[:, 0, 1].set(low)
        message = jnp.concatenate([total.astype(jnp.bfloat16), extra], axis=1)
        pairs = [(i, i + k) for i in range(count - k)]
        got = lax.ppermute(message, axis, pairs)
        got_decay = got[:, rows, 0].astype(jnp.float32) + got[:, rows, 1].astype(jnp.float32)
        return got_decay, got[:, :rows].astype(jnp.float32)

    decay, total = shifted(passing, state, 1)
    if count > 2:
        decay_far, total_far = shifted(passing, state, 2)
        total = decay[:, None, None] * total_far + total
        decay = decay * decay_far
    k = 2
    while k < count:
        decay_far, total_far = shifted(decay, total, k)
        total = decay[:, None, None] * total_far + total
        decay = decay * decay_far
        k *= 2
    return total


def rms_rows(embedded_entries, norm_gain):
    token_float = embedded_entries.astype(jnp.float32)
    moment = jnp.mean(token_float * token_float, axis=1, keepdims=True)
    return (token_float * lax.rsqrt(moment + EPSILON) * norm_gain).astype(jnp.bfloat16)


def local_terms(queries, key_rows, values, log_forget, input_gate, starts):
    length = queries.shape[0]
    scaling = queries.shape[1] ** (-0.5)
    segment = jnp.cumsum(starts)
    levels = jnp.cumsum(log_forget)
    position = jnp.arange(length)
    allowed = (position[:, None] >= position[None, :]) & (segment[:, None] == segment[None, :])
    decays = jnp.where(
        allowed,
        jnp.exp(jnp.minimum(levels[:, None] - levels[None, :], 0.0) + input_gate[None, :]),
        0.0,
    )
    scores = jnp.dot(queries, key_rows.T, preferred_element_type=jnp.float32) * scaling
    weights = (scores * decays).astype(jnp.bfloat16)
    inner_part = jnp.dot(weights, values, preferred_element_type=jnp.float32)
    last_level = levels[-1]
    last_seg = segment[-1]
    keeping = jnp.where(segment == last_seg, jnp.exp(last_level - levels + input_gate), 0.0)
    weighted = (key_rows.astype(jnp.float32) * keeping[:, None]).astype(jnp.bfloat16)
    local_state = lax.dot_general(
        weighted, values, (((0,), (0,)), ((), ())), preferred_element_type=jnp.float32
    )
    passing = jnp.where(last_seg == 0, jnp.exp(last_level), 0.0)
    carried = jnp.where(segment == 0, jnp.exp(levels), 0.0) * scaling
    return (inner_part, local_state, passing, carried)


def apply_state(queries, carried, incoming):
    lifted = queries.astype(jnp.float32) * carried[:, None]
    return jnp.dot(
        lifted, incoming, precision=lax.Precision.HIGHEST, preferred_element_type=jnp.float32
    )


def head_norm(head_out, gain):
    centre = jnp.mean(head_out, axis=1, keepdims=True)
    shifted = head_out - centre
    spread = jnp.mean(shifted * shifted, axis=1, keepdims=True)
    return (shifted * lax.rsqrt(spread + EPSILON) * gain).astype(jnp.bfloat16)


def local(
    tokens,
    norm_gain,
    w_qkv,
    w_out,
    head_gain,
    input_codes,
    forget_codes,
    forget_bias,
    document_begin_flags,
):
    normed = rms_rows(tokens, norm_gain)
    group = lax.axis_size("tp")
    copies = jnp.broadcast_to(normed[None], (group,) + normed.shape)
    every_row_list = lax.all_to_all(copies, "tp", 0, 0, tiled=True).reshape(-1, normed.shape[1])
    parameter_collection = lax.all_gather(w_qkv, "ctx", axis=0, tiled=True)
    rows_combined = jnp.dot(
        every_row_list, parameter_collection, preferred_element_type=jnp.float32
    )
    rows_combined = rows_combined.astype(jnp.bfloat16)
    heads_here = forget_bias.shape[0]
    stride = 2 * DK + DV
    query_list, inner_list, state_list, passing_list, carried_list = ([], [], [], [], [])
    attention_slot_number = 0
    offset = attention_slot_number * stride
    queries = rows_combined[:, offset : offset + DK]
    key_rows = rows_combined[:, offset + DK : offset + 2 * DK]
    values = rows_combined[:, offset + 2 * DK : offset + stride]
    log_forget = jax.nn.log_sigmoid(
        FORGET_STEP * forget_codes[attention_slot_number].astype(jnp.float32)
        + forget_bias[attention_slot_number]
    )
    input_gate = INPUT_STEP * input_codes[attention_slot_number].astype(jnp.float32)
    inner_part, local_state, passing, carried = local_terms(
        queries, key_rows, values, log_forget, input_gate, document_begin_flags
    )
    query_list.append(queries)
    inner_list.append(inner_part)
    state_list.append(local_state)
    passing_list.append(passing)
    carried_list.append(carried)
    incoming = carried_in(jnp.stack(passing_list), jnp.stack(state_list), "ctx")
    attention_slot_number = 0
    head_out = inner_list[attention_slot_number] + apply_state(
        query_list[attention_slot_number],
        carried_list[attention_slot_number],
        incoming[attention_slot_number],
    )
    normed_heads = head_norm(head_out, head_gain)
    blocks = lax.axis_size("ctx")
    out_copies = jnp.broadcast_to(w_out.T[None], (blocks,) + w_out.T.shape)
    out_rows = lax.all_to_all(out_copies, "ctx", 0, 0, tiled=True).reshape(-1, w_out.shape[0])
    projected = lax.dot_general(
        normed_heads, out_rows, (((1,), (1,)), ((), ())), preferred_element_type=jnp.float32
    )
    summed = lax.psum_scatter(
        projected.astype(jnp.bfloat16),
        "tp",
        scatter_dimension=0,
        tiled=True,
    ).astype(jnp.float32)
    return (tokens.astype(jnp.float32) + summed).astype(jnp.bfloat16)


def solution(mesh):
    placed = (
        P(("ctx", "tp"), None),
        P(),
        P("ctx", "tp"),
        P("tp", "ctx"),
        P("tp"),
        P("tp", "ctx"),
        P("tp", "ctx"),
        P("tp"),
        P("ctx"),
    )
    return jax.shard_map(
        local, mesh=mesh, in_specs=placed, out_specs=P(("ctx", "tp"), None), check_vma=False
    )
```

```python
import functools

import jax
import jax.numpy as jnp
from jax import lax
from jax.experimental import pallas as pl
from jax.experimental.pallas import tpu as pltpu
from jax.sharding import PartitionSpec as P

DK = 256
DV = 512


EPSILON = 1e-06
FORGET_STEP = 0.5
INPUT_STEP = 0.5


MESH_ID = pl.DeviceIdType.MESH
DECAY_ROWS = 16


def scan_shifts(count):
    shifts = [1] + ([2] if count > 2 else [])
    k = 2
    while k < count:
        shifts.append(k)
        k *= 2
    return shifts


def scan_kernel(count, shifts, state_ref, decay_ref, out_ref, send_buf, recv_buf, acc_total, acc_decay, send_sems, recv_sems):
    me = lax.axis_index("ctx")
    tp = lax.axis_index("tp")
    rows = state_ref.shape[0]

    barrier = pltpu.get_barrier_semaphore()
    partners = sorted(set(shifts))
    for s in partners:
        for peer in (lax.rem(me + s, count), lax.rem(me + count - s, count)):
            pl.semaphore_signal(barrier, 1, device_id=(peer, tp), device_id_type=MESH_ID)
    pl.semaphore_wait(barrier, 2 * len(partners))

    def pack(slot, total, decay):
        high = decay.astype(jnp.bfloat16)
        send_buf[slot, :rows, :] = total.astype(jnp.bfloat16)
        send_buf[slot, rows : rows + DECAY_ROWS, :] = high
        send_buf[slot, rows + DECAY_ROWS :, :] = (decay - high.astype(jnp.float32)).astype(jnp.bfloat16)

    def copy(j, source_slot, peer):
        return pltpu.make_async_remote_copy(
            src_ref=send_buf.at[source_slot],
            dst_ref=recv_buf.at[j],
            send_sem=send_sems.at[j],
            recv_sem=recv_sems.at[j],
            device_id=(peer, tp),
            device_id_type=MESH_ID,
        )

    def send(j, source_slot):
        @pl.when(me + shifts[j] < count)
        def _():
            copy(j, source_slot, me + shifts[j]).start()

    def absorb(j, source_slot):
        @pl.when(me - shifts[j] >= 0)
        def _():
            copy(j, source_slot, me - shifts[j]).wait_recv()
            got = recv_buf[j]
            far_total = got[:rows].astype(jnp.float32)
            far_decay = got[rows : rows + DECAY_ROWS].astype(jnp.float32) + got[
                rows + DECAY_ROWS :
            ].astype(jnp.float32)
            decay = acc_decay[...]
            acc_total[...] = decay[0:1, :] * far_total + acc_total[...]
            acc_decay[...] = decay * far_decay

    acc_total[...] = jnp.zeros_like(acc_total)
    acc_decay[...] = jnp.ones_like(acc_decay)
    pack(0, state_ref[...], decay_ref[...])
    first = min(2, len(shifts))
    for j in range(first):
        send(j, 0)
    for j in range(first):
        absorb(j, 0)
    for j in range(first, len(shifts)):
        pack(j - 1, acc_total[...], acc_decay[...])
        send(j, j - 1)
        absorb(j, j - 1)
    out_ref[...] = acc_total[...]
    for j in range(len(shifts)):
        @pl.when(me + shifts[j] < count)
        def _():
            copy(j, 0 if j < first else j - 1, me + shifts[j]).wait_send()


def carried_in(passing, state, axis):
    count = lax.axis_size(axis)
    if count == 1:
        return jnp.zeros_like(state)
    shifts = scan_shifts(count)
    rows, width = state.shape
    decay = jnp.broadcast_to(passing.reshape(1, 1), (DECAY_ROWS, width)).astype(jnp.float32)
    message = (len(shifts), rows + 2 * DECAY_ROWS, width)
    return pl.pallas_call(
        functools.partial(scan_kernel, count, shifts),
        out_shape=jax.ShapeDtypeStruct((rows, width), jnp.float32),
        in_specs=[pl.BlockSpec(memory_space=pltpu.VMEM)] * 2,
        out_specs=pl.BlockSpec(memory_space=pltpu.VMEM),
        scratch_shapes=[
            pltpu.VMEM(message, jnp.bfloat16),
            pltpu.VMEM(message, jnp.bfloat16),
            pltpu.VMEM((rows, width), jnp.float32),
            pltpu.VMEM((DECAY_ROWS, width), jnp.float32),
            pltpu.SemaphoreType.DMA((len(shifts),)),
            pltpu.SemaphoreType.DMA((len(shifts),)),
        ],
        compiler_params=pltpu.CompilerParams(collective_id=0, has_side_effects=True),
    )(state.astype(jnp.float32), decay)


def rms_rows(embedded_entries, norm_gain):
    token_float = embedded_entries.astype(jnp.float32)
    moment = jnp.mean(token_float * token_float, axis=1, keepdims=True)
    return (token_float * lax.rsqrt(moment + EPSILON) * norm_gain).astype(jnp.bfloat16)


def local_terms(queries, key_rows, values, log_forget, input_gate, starts):
    length = queries.shape[0]
    scaling = queries.shape[1] ** (-0.5)
    segment = jnp.cumsum(starts)
    levels = jnp.cumsum(log_forget)
    position = jnp.arange(length)
    allowed = (position[:, None] >= position[None, :]) & (segment[:, None] == segment[None, :])
    decays = jnp.where(
        allowed,
        jnp.exp(jnp.minimum(levels[:, None] - levels[None, :], 0.0) + input_gate[None, :]),
        0.0,
    )
    scores = jnp.dot(queries, key_rows.T, preferred_element_type=jnp.float32) * scaling
    weights = (scores * decays).astype(jnp.bfloat16)
    inner_part = jnp.dot(weights, values, preferred_element_type=jnp.float32)
    last_level = levels[-1]
    last_seg = segment[-1]
    keeping = jnp.where(segment == last_seg, jnp.exp(last_level - levels + input_gate), 0.0)
    weighted = (key_rows.astype(jnp.float32) * keeping[:, None]).astype(jnp.bfloat16)
    local_state = lax.dot_general(
        weighted, values, (((0,), (0,)), ((), ())), preferred_element_type=jnp.float32
    )
    passing = jnp.where(last_seg == 0, jnp.exp(last_level), 0.0)
    carried = jnp.where(segment == 0, jnp.exp(levels), 0.0) * scaling
    return (inner_part, local_state, passing, carried)


def apply_state(queries, carried, incoming):
    lifted = queries.astype(jnp.float32) * carried[:, None]
    return jnp.dot(
        lifted, incoming, precision=lax.Precision.HIGHEST, preferred_element_type=jnp.float32
    )


def head_norm(head_out, gain):
    centre = jnp.mean(head_out, axis=1, keepdims=True)
    shifted = head_out - centre
    spread = jnp.mean(shifted * shifted, axis=1, keepdims=True)
    return (shifted * lax.rsqrt(spread + EPSILON) * gain).astype(jnp.bfloat16)


def local(
    tokens,
    norm_gain,
    w_qkv,
    w_out,
    head_gain,
    input_codes,
    forget_codes,
    forget_bias,
    document_begin_flags,
):
    normed = rms_rows(tokens, norm_gain)
    group = lax.axis_size("tp")
    copies = jnp.broadcast_to(normed[None], (group,) + normed.shape)
    every_row_list = lax.all_to_all(copies, "tp", 0, 0, tiled=True).reshape(-1, normed.shape[1])
    width = w_qkv.shape[1]
    both = lax.all_gather(jnp.concatenate([w_qkv, w_out.T], axis=1), "ctx", axis=0, tiled=True)
    parameter_collection = both[:, :width]
    out_rows = both[:, width:]
    rows_combined = jnp.dot(
        every_row_list, parameter_collection, preferred_element_type=jnp.float32
    )
    rows_combined = rows_combined.astype(jnp.bfloat16)
    heads_here = forget_bias.shape[0]
    stride = 2 * DK + DV
    query_list, inner_list, state_list, passing_list, carried_list = ([], [], [], [], [])
    attention_slot_number = 0
    offset = attention_slot_number * stride
    queries = rows_combined[:, offset : offset + DK]
    key_rows = rows_combined[:, offset + DK : offset + 2 * DK]
    values = rows_combined[:, offset + 2 * DK : offset + stride]
    log_forget = jax.nn.log_sigmoid(
        FORGET_STEP * forget_codes[attention_slot_number].astype(jnp.float32)
        + forget_bias[attention_slot_number]
    )
    input_gate = INPUT_STEP * input_codes[attention_slot_number].astype(jnp.float32)
    inner_part, local_state, passing, carried = local_terms(
        queries, key_rows, values, log_forget, input_gate, document_begin_flags
    )
    query_list.append(queries)
    inner_list.append(inner_part)
    state_list.append(local_state)
    passing_list.append(passing)
    carried_list.append(carried)
    incoming = carried_in(passing_list[0], state_list[0], "ctx")[None]
    attention_slot_number = 0
    head_out = inner_list[attention_slot_number] + apply_state(
        query_list[attention_slot_number],
        carried_list[attention_slot_number],
        incoming[attention_slot_number],
    )
    normed_heads = head_norm(head_out, head_gain)
    projected = lax.dot_general(
        normed_heads, out_rows, (((1,), (1,)), ((), ())), preferred_element_type=jnp.float32
    )
    summed = lax.psum_scatter(
        projected.astype(jnp.bfloat16),
        "tp",
        scatter_dimension=0,
        tiled=True,
    ).astype(jnp.float32)
    return (tokens.astype(jnp.float32) + summed).astype(jnp.bfloat16)


def solution(mesh):
    placed = (
        P(("ctx", "tp"), None),
        P(),
        P("ctx", "tp"),
        P("tp", "ctx"),
        P("tp"),
        P("tp", "ctx"),
        P("tp", "ctx"),
        P("tp"),
        P("ctx"),
    )
    return jax.shard_map(
        local, mesh=mesh, in_specs=placed, out_specs=P(("ctx", "tp"), None), check_vma=False
    )
```

```python
import functools

import jax
import jax.numpy as jnp
from jax import lax
from jax.experimental import pallas as pl
from jax.experimental.pallas import tpu as pltpu
from jax.sharding import PartitionSpec as P

DK = 256
DV = 512


EPSILON = 1e-06
FORGET_STEP = 0.5
INPUT_STEP = 0.5


MESH_ID = pl.DeviceIdType.MESH
DECAY_ROWS = 16


def scan_shifts(count):
    shifts = [1] + ([2] if count > 2 else [])
    k = 2
    while k < count:
        shifts.append(k)
        k *= 2
    return shifts


def scan_kernel(count, shifts, state_ref, decay_ref, out_ref, send_buf, recv_buf, acc_total, acc_decay, send_sems, recv_sems):
    rows_of_z = lax.axis_size("cy")
    me = lax.axis_index("cz") * rows_of_z + lax.axis_index("cy")
    tp = lax.axis_index("tp")
    rows = state_ref.shape[0]

    def place(peer):
        return (peer // rows_of_z, peer % rows_of_z, tp)

    barrier = pltpu.get_barrier_semaphore()
    partners = sorted(set(shifts))
    for s in partners:
        for peer in (lax.rem(me + s, count), lax.rem(me + count - s, count)):
            pl.semaphore_signal(barrier, 1, device_id=place(peer), device_id_type=MESH_ID)
    pl.semaphore_wait(barrier, 2 * len(partners))

    def pack(slot, total, decay):
        high = decay.astype(jnp.bfloat16)
        send_buf[slot, :rows, :] = total.astype(jnp.bfloat16)
        send_buf[slot, rows : rows + DECAY_ROWS, :] = high
        send_buf[slot, rows + DECAY_ROWS :, :] = (decay - high.astype(jnp.float32)).astype(jnp.bfloat16)

    def copy(j, source_slot, peer):
        return pltpu.make_async_remote_copy(
            src_ref=send_buf.at[source_slot],
            dst_ref=recv_buf.at[j],
            send_sem=send_sems.at[j],
            recv_sem=recv_sems.at[j],
            device_id=place(peer),
            device_id_type=MESH_ID,
        )

    def send(j, source_slot):
        @pl.when(me + shifts[j] < count)
        def _():
            copy(j, source_slot, me + shifts[j]).start()

    def absorb(j, source_slot):
        @pl.when(me - shifts[j] >= 0)
        def _():
            copy(j, source_slot, me - shifts[j]).wait_recv()
            got = recv_buf[j]
            far_total = got[:rows].astype(jnp.float32)
            far_decay = got[rows : rows + DECAY_ROWS].astype(jnp.float32) + got[
                rows + DECAY_ROWS :
            ].astype(jnp.float32)
            decay = acc_decay[...]
            acc_total[...] = decay[0:1, :] * far_total + acc_total[...]
            acc_decay[...] = decay * far_decay

    acc_total[...] = jnp.zeros_like(acc_total)
    acc_decay[...] = jnp.ones_like(acc_decay)
    pack(0, state_ref[...], decay_ref[...])
    first = min(2, len(shifts))
    for j in range(first):
        send(j, 0)
    for j in range(first):
        absorb(j, 0)
    for j in range(first, len(shifts)):
        pack(j - 1, acc_total[...], acc_decay[...])
        send(j, j - 1)
        absorb(j, j - 1)
    out_ref[...] = acc_total[...]
    for j in range(len(shifts)):
        @pl.when(me + shifts[j] < count)
        def _():
            copy(j, 0 if j < first else j - 1, me + shifts[j]).wait_send()


def carried_in(passing, state):
    count = lax.axis_size("cz") * lax.axis_size("cy")
    if count == 1:
        return jnp.zeros_like(state)
    shifts = scan_shifts(count)
    rows, width = state.shape
    decay = jnp.broadcast_to(passing.reshape(1, 1), (DECAY_ROWS, width)).astype(jnp.float32)
    message = (len(shifts), rows + 2 * DECAY_ROWS, width)
    return pl.pallas_call(
        functools.partial(scan_kernel, count, shifts),
        out_shape=jax.ShapeDtypeStruct((rows, width), jnp.float32),
        in_specs=[pl.BlockSpec(memory_space=pltpu.VMEM)] * 2,
        out_specs=pl.BlockSpec(memory_space=pltpu.VMEM),
        scratch_shapes=[
            pltpu.VMEM(message, jnp.bfloat16),
            pltpu.VMEM(message, jnp.bfloat16),
            pltpu.VMEM((rows, width), jnp.float32),
            pltpu.VMEM((DECAY_ROWS, width), jnp.float32),
            pltpu.SemaphoreType.DMA((len(shifts),)),
            pltpu.SemaphoreType.DMA((len(shifts),)),
        ],
        compiler_params=pltpu.CompilerParams(collective_id=0, has_side_effects=True),
    )(state.astype(jnp.float32), decay)


def rms_rows(embedded_entries, norm_gain):
    token_float = embedded_entries.astype(jnp.float32)
    moment = jnp.mean(token_float * token_float, axis=1, keepdims=True)
    return (token_float * lax.rsqrt(moment + EPSILON) * norm_gain).astype(jnp.bfloat16)


def local_terms(queries, key_rows, values, log_forget, input_gate, starts):
    length = queries.shape[0]
    scaling = queries.shape[1] ** (-0.5)
    segment = jnp.cumsum(starts)
    levels = jnp.cumsum(log_forget)
    position = jnp.arange(length)
    allowed = (position[:, None] >= position[None, :]) & (segment[:, None] == segment[None, :])
    decays = jnp.where(
        allowed,
        jnp.exp(jnp.minimum(levels[:, None] - levels[None, :], 0.0) + input_gate[None, :]),
        0.0,
    )
    scores = jnp.dot(queries, key_rows.T, preferred_element_type=jnp.float32) * scaling
    weights = (scores * decays).astype(jnp.bfloat16)
    inner_part = jnp.dot(weights, values, preferred_element_type=jnp.float32)
    last_level = levels[-1]
    last_seg = segment[-1]
    keeping = jnp.where(segment == last_seg, jnp.exp(last_level - levels + input_gate), 0.0)
    weighted = (key_rows.astype(jnp.float32) * keeping[:, None]).astype(jnp.bfloat16)
    local_state = lax.dot_general(
        weighted, values, (((0,), (0,)), ((), ())), preferred_element_type=jnp.float32
    )
    passing = jnp.where(last_seg == 0, jnp.exp(last_level), 0.0)
    carried = jnp.where(segment == 0, jnp.exp(levels), 0.0) * scaling
    return (inner_part, local_state, passing, carried)


def apply_state(queries, carried, incoming):
    lifted = queries.astype(jnp.float32) * carried[:, None]
    return jnp.dot(
        lifted, incoming, precision=lax.Precision.HIGHEST, preferred_element_type=jnp.float32
    )


def head_norm(head_out, gain):
    centre = jnp.mean(head_out, axis=1, keepdims=True)
    shifted = head_out - centre
    spread = jnp.mean(shifted * shifted, axis=1, keepdims=True)
    return (shifted * lax.rsqrt(spread + EPSILON) * gain).astype(jnp.bfloat16)


def local(
    tokens,
    norm_gain,
    w_qkv,
    w_out,
    head_gain,
    input_codes,
    forget_codes,
    forget_bias,
    document_begin_flags,
):
    normed = rms_rows(tokens, norm_gain)
    group = lax.axis_size("tp")
    copies = jnp.broadcast_to(normed[None], (group,) + normed.shape)
    every_row_list = lax.all_to_all(copies, "tp", 0, 0, tiled=True).reshape(-1, normed.shape[1])
    width = w_qkv.shape[1]
    pieces = jnp.concatenate([w_qkv, w_out.T], axis=1)
    both = lax.all_gather(lax.all_gather(pieces, "cy", axis=0, tiled=True), "cz", axis=0, tiled=True)
    parameter_collection = both[:, :width]
    out_rows = both[:, width:]
    rows_combined = jnp.dot(
        every_row_list, parameter_collection, preferred_element_type=jnp.float32
    )
    rows_combined = rows_combined.astype(jnp.bfloat16)
    heads_here = forget_bias.shape[0]
    stride = 2 * DK + DV
    query_list, inner_list, state_list, passing_list, carried_list = ([], [], [], [], [])
    attention_slot_number = 0
    offset = attention_slot_number * stride
    queries = rows_combined[:, offset : offset + DK]
    key_rows = rows_combined[:, offset + DK : offset + 2 * DK]
    values = rows_combined[:, offset + 2 * DK : offset + stride]
    log_forget = jax.nn.log_sigmoid(
        FORGET_STEP * forget_codes[attention_slot_number].astype(jnp.float32)
        + forget_bias[attention_slot_number]
    )
    input_gate = INPUT_STEP * input_codes[attention_slot_number].astype(jnp.float32)
    inner_part, local_state, passing, carried = local_terms(
        queries, key_rows, values, log_forget, input_gate, document_begin_flags
    )
    query_list.append(queries)
    inner_list.append(inner_part)
    state_list.append(local_state)
    passing_list.append(passing)
    carried_list.append(carried)
    incoming = carried_in(passing_list[0], state_list[0])[None]
    attention_slot_number = 0
    head_out = inner_list[attention_slot_number] + apply_state(
        query_list[attention_slot_number],
        carried_list[attention_slot_number],
        incoming[attention_slot_number],
    )
    normed_heads = head_norm(head_out, head_gain)
    projected = lax.dot_general(
        normed_heads, out_rows, (((1,), (1,)), ((), ())), preferred_element_type=jnp.float32
    )
    summed = lax.psum_scatter(
        projected.astype(jnp.bfloat16),
        "tp",
        scatter_dimension=0,
        tiled=True,
    ).astype(jnp.float32)
    return (tokens.astype(jnp.float32) + summed).astype(jnp.bfloat16)


def solution(mesh):
    z_rows = 4 if mesh.shape["ctx"] % 4 == 0 else 1
    split = jax.sharding.Mesh(
        mesh.devices.reshape(mesh.shape["ctx"] // z_rows, z_rows, mesh.shape["tp"]), ("cz", "cy", "tp")
    )
    blocks = ("cz", "cy")
    placed = (
        P(blocks + ("tp",), None),
        P(),
        P(blocks, "tp"),
        P("tp", blocks),
        P("tp"),
        P("tp", blocks),
        P("tp", blocks),
        P("tp"),
        P(blocks),
    )
    return jax.shard_map(
        local, mesh=split, in_specs=placed, out_specs=P(blocks + ("tp",), None), check_vma=False
    )
```

```python
import functools

import jax
import jax.numpy as jnp
from jax import lax
from jax.experimental import pallas as pl
from jax.experimental.pallas import tpu as pltpu
from jax.sharding import PartitionSpec as P

DK = 256
DV = 512


EPSILON = 1e-06
FORGET_STEP = 0.5
INPUT_STEP = 0.5


MESH_ID = pl.DeviceIdType.MESH
DECAY_ROWS = 16


def scan_shifts(count):
    shifts = [1] + ([2] if count > 2 else [])
    k = 2
    while k < count:
        shifts.append(k)
        k *= 2
    return shifts


def pack(ref, total, decay):
    rows = total.shape[0]
    high = decay.astype(jnp.bfloat16)
    ref[:rows, :] = total.astype(jnp.bfloat16)
    ref[rows : rows + DECAY_ROWS, :] = high
    ref[rows + DECAY_ROWS :, :] = (decay - high.astype(jnp.float32)).astype(jnp.bfloat16)


def absorb(got, rows, acc_total, acc_decay):
    far_total = got[:rows].astype(jnp.float32)
    far_decay = got[rows : rows + DECAY_ROWS].astype(jnp.float32) + got[rows + DECAY_ROWS :].astype(jnp.float32)
    decay = acc_decay[...]
    acc_total[...] = decay[0:1, :] * far_total + acc_total[...]
    acc_decay[...] = decay * far_decay


def scan_kernel(
    ny, nz, zshifts, state_ref, decay_ref, out_ref,
    row_send, row_recv, z_send, z_recv, p_send, p_recv,
    acc_total, acc_decay, quarter_total, quarter_decay, z_total, z_decay,
    row_send_sems, row_recv_sems, z_send_sems, z_recv_sems, p_send_sems, p_recv_sems,
):
    yi = lax.axis_index("cy")
    zi = lax.axis_index("cz")
    tp = lax.axis_index("tp")
    rows, width = state_ref.shape
    quarter = width // ny
    mine = pl.ds(pl.multiple_of(yi * quarter, quarter), quarter)

    barrier = pltpu.get_barrier_semaphore()
    z_partners = sorted(set(zshifts))
    for d in range(1, ny):
        pl.semaphore_signal(barrier, 1, device_id=(zi, lax.rem(yi + d, ny), tp), device_id_type=MESH_ID)
    for s in z_partners:
        for peer in (lax.rem(zi + s, nz), lax.rem(zi + nz - s, nz)):
            pl.semaphore_signal(barrier, 1, device_id=(peer, yi, tp), device_id_type=MESH_ID)
    pl.semaphore_wait(barrier, (ny - 1) + 2 * len(z_partners))

    def row_copy(d, target, slot):
        return pltpu.make_async_remote_copy(
            src_ref=row_send, dst_ref=row_recv.at[slot], send_sem=row_send_sems.at[d],
            recv_sem=row_recv_sems.at[slot], device_id=(zi, target, tp), device_id_type=MESH_ID,
        )

    pack(row_send, state_ref[...], decay_ref[...])
    for d in range(1, ny):
        row_copy(d, lax.rem(yi + d, ny), yi).start()
    for d in range(1, ny):
        source = lax.rem(yi + ny - d, ny)
        row_copy(d, yi, source).wait_recv()

    acc_total[...] = jnp.zeros_like(acc_total)
    acc_decay[...] = jnp.ones_like(acc_decay)
    for d in range(1, ny):
        @pl.when(yi - d >= 0)
        def _():
            absorb(row_recv[yi - d], rows, acc_total, acc_decay)

    quarter_total[...] = jnp.zeros_like(quarter_total)
    quarter_decay[...] = jnp.ones_like(quarter_decay)
    for y in reversed(range(ny)):
        @pl.when(yi == y)
        def _():
            absorb(row_send[:, mine], rows, quarter_total, quarter_decay)

        @pl.when(yi != y)
        def _():
            absorb(row_recv[y, :, mine], rows, quarter_total, quarter_decay)

    def z_copy(j, slot, peer):
        return pltpu.make_async_remote_copy(
            src_ref=z_send.at[slot], dst_ref=z_recv.at[j], send_sem=z_send_sems.at[j],
            recv_sem=z_recv_sems.at[j], device_id=(peer, yi, tp), device_id_type=MESH_ID,
        )

    def z_send_round(j, slot):
        @pl.when(zi + zshifts[j] < nz)
        def _():
            z_copy(j, slot, zi + zshifts[j]).start()

    def z_absorb(j, slot):
        @pl.when(zi - zshifts[j] >= 0)
        def _():
            z_copy(j, slot, zi - zshifts[j]).wait_recv()
            absorb(z_recv[j], rows, z_total, z_decay)

    z_total[...] = jnp.zeros_like(z_total)
    z_decay[...] = jnp.ones_like(z_decay)
    first = min(2, len(zshifts))
    if zshifts:
        pack(z_send.at[0], quarter_total[...], quarter_decay[...])
    for j in range(first):
        z_send_round(j, 0)
    for j in range(first):
        z_absorb(j, 0)
    for j in range(first, len(zshifts)):
        pack(z_send.at[j - 1], z_total[...], z_decay[...])
        z_send_round(j, j - 1)
        z_absorb(j, j - 1)

    def p_copy(d, target, slot):
        return pltpu.make_async_remote_copy(
            src_ref=p_send, dst_ref=p_recv.at[slot], send_sem=p_send_sems.at[d],
            recv_sem=p_recv_sems.at[slot], device_id=(zi, target, tp), device_id_type=MESH_ID,
        )

    p_send[...] = z_total[...].astype(jnp.bfloat16)
    for d in range(1, ny):
        p_copy(d, lax.rem(yi + d, ny), yi).start()
    for d in range(1, ny):
        p_copy(d, yi, lax.rem(yi + ny - d, ny)).wait_recv()
    decay = acc_decay[0:1, :]
    for y in range(ny):
        cols = slice(y * quarter, (y + 1) * quarter)

        @pl.when(yi == y)
        def _():
            out_ref[:, cols] = decay[:, cols] * p_send[...].astype(jnp.float32) + acc_total[:, cols]

        @pl.when(yi != y)
        def _():
            out_ref[:, cols] = decay[:, cols] * p_recv[y].astype(jnp.float32) + acc_total[:, cols]

    for d in range(1, ny):
        row_copy(d, lax.rem(yi + d, ny), yi).wait_send()
        p_copy(d, lax.rem(yi + d, ny), yi).wait_send()
    for j in range(len(zshifts)):
        @pl.when(zi + zshifts[j] < nz)
        def _():
            z_copy(j, 0 if j < first else j - 1, zi + zshifts[j]).wait_send()


def carried_in(passing, state):
    ny, nz = lax.axis_size("cy"), lax.axis_size("cz")
    if ny * nz == 1:
        return jnp.zeros_like(state)
    zshifts = scan_shifts(nz) if nz > 1 else []
    rows, width = state.shape
    quarter = width // ny
    decay = jnp.broadcast_to(passing.reshape(1, 1), (DECAY_ROWS, width)).astype(jnp.float32)
    message = rows + 2 * DECAY_ROWS
    slots = max(len(zshifts), 1)
    return pl.pallas_call(
        functools.partial(scan_kernel, ny, nz, zshifts),
        out_shape=jax.ShapeDtypeStruct((rows, width), jnp.float32),
        in_specs=[pl.BlockSpec(memory_space=pltpu.VMEM)] * 2,
        out_specs=pl.BlockSpec(memory_space=pltpu.VMEM),
        scratch_shapes=[
            pltpu.VMEM((message, width), jnp.bfloat16),
            pltpu.VMEM((ny, message, width), jnp.bfloat16),
            pltpu.VMEM((slots, message, quarter), jnp.bfloat16),
            pltpu.VMEM((slots, message, quarter), jnp.bfloat16),
            pltpu.VMEM((rows, quarter), jnp.bfloat16),
            pltpu.VMEM((ny, rows, quarter), jnp.bfloat16),
            pltpu.VMEM((rows, width), jnp.float32),
            pltpu.VMEM((DECAY_ROWS, width), jnp.float32),
            pltpu.VMEM((rows, quarter), jnp.float32),
            pltpu.VMEM((DECAY_ROWS, quarter), jnp.float32),
            pltpu.VMEM((rows, quarter), jnp.float32),
            pltpu.VMEM((DECAY_ROWS, quarter), jnp.float32),
            pltpu.SemaphoreType.DMA((ny,)),
            pltpu.SemaphoreType.DMA((ny,)),
            pltpu.SemaphoreType.DMA((slots,)),
            pltpu.SemaphoreType.DMA((slots,)),
            pltpu.SemaphoreType.DMA((ny,)),
            pltpu.SemaphoreType.DMA((ny,)),
        ],
        compiler_params=pltpu.CompilerParams(collective_id=0, has_side_effects=True),
    )(state.astype(jnp.float32), decay)


def rms_rows(embedded_entries, norm_gain):
    token_float = embedded_entries.astype(jnp.float32)
    moment = jnp.mean(token_float * token_float, axis=1, keepdims=True)
    return (token_float * lax.rsqrt(moment + EPSILON) * norm_gain).astype(jnp.bfloat16)


def local_terms(queries, key_rows, values, log_forget, input_gate, starts):
    length = queries.shape[0]
    scaling = queries.shape[1] ** (-0.5)
    segment = jnp.cumsum(starts)
    levels = jnp.cumsum(log_forget)
    position = jnp.arange(length)
    allowed = (position[:, None] >= position[None, :]) & (segment[:, None] == segment[None, :])
    decays = jnp.where(
        allowed,
        jnp.exp(jnp.minimum(levels[:, None] - levels[None, :], 0.0) + input_gate[None, :]),
        0.0,
    )
    scores = jnp.dot(queries, key_rows.T, preferred_element_type=jnp.float32) * scaling
    weights = (scores * decays).astype(jnp.bfloat16)
    inner_part = jnp.dot(weights, values, preferred_element_type=jnp.float32)
    last_level = levels[-1]
    last_seg = segment[-1]
    keeping = jnp.where(segment == last_seg, jnp.exp(last_level - levels + input_gate), 0.0)
    weighted = (key_rows.astype(jnp.float32) * keeping[:, None]).astype(jnp.bfloat16)
    local_state = lax.dot_general(
        weighted, values, (((0,), (0,)), ((), ())), preferred_element_type=jnp.float32
    )
    passing = jnp.where(last_seg == 0, jnp.exp(last_level), 0.0)
    carried = jnp.where(segment == 0, jnp.exp(levels), 0.0) * scaling
    return (inner_part, local_state, passing, carried)


def apply_state(queries, carried, incoming):
    lifted = queries.astype(jnp.float32) * carried[:, None]
    return jnp.dot(
        lifted, incoming, precision=lax.Precision.HIGHEST, preferred_element_type=jnp.float32
    )


def head_norm(head_out, gain):
    centre = jnp.mean(head_out, axis=1, keepdims=True)
    shifted = head_out - centre
    spread = jnp.mean(shifted * shifted, axis=1, keepdims=True)
    return (shifted * lax.rsqrt(spread + EPSILON) * gain).astype(jnp.bfloat16)


def local(
    tokens,
    norm_gain,
    w_qkv,
    w_out,
    head_gain,
    input_codes,
    forget_codes,
    forget_bias,
    document_begin_flags,
):
    normed = rms_rows(tokens, norm_gain)
    group = lax.axis_size("tp")
    copies = jnp.broadcast_to(normed[None], (group,) + normed.shape)
    every_row_list = lax.all_to_all(copies, "tp", 0, 0, tiled=True).reshape(-1, normed.shape[1])
    width = w_qkv.shape[1]
    both = lax.all_gather(jnp.concatenate([w_qkv, w_out.T], axis=1), ("cz", "cy"), axis=0, tiled=True)
    parameter_collection = both[:, :width]
    out_rows = both[:, width:]
    rows_combined = jnp.dot(
        every_row_list, parameter_collection, preferred_element_type=jnp.float32
    )
    rows_combined = rows_combined.astype(jnp.bfloat16)
    heads_here = forget_bias.shape[0]
    stride = 2 * DK + DV
    query_list, inner_list, state_list, passing_list, carried_list = ([], [], [], [], [])
    attention_slot_number = 0
    offset = attention_slot_number * stride
    queries = rows_combined[:, offset : offset + DK]
    key_rows = rows_combined[:, offset + DK : offset + 2 * DK]
    values = rows_combined[:, offset + 2 * DK : offset + stride]
    log_forget = jax.nn.log_sigmoid(
        FORGET_STEP * forget_codes[attention_slot_number].astype(jnp.float32)
        + forget_bias[attention_slot_number]
    )
    input_gate = INPUT_STEP * input_codes[attention_slot_number].astype(jnp.float32)
    inner_part, local_state, passing, carried = local_terms(
        queries, key_rows, values, log_forget, input_gate, document_begin_flags
    )
    query_list.append(queries)
    inner_list.append(inner_part)
    state_list.append(local_state)
    passing_list.append(passing)
    carried_list.append(carried)
    incoming = carried_in(passing_list[0], state_list[0])[None]
    attention_slot_number = 0
    head_out = inner_list[attention_slot_number] + apply_state(
        query_list[attention_slot_number],
        carried_list[attention_slot_number],
        incoming[attention_slot_number],
    )
    normed_heads = head_norm(head_out, head_gain)
    projected = lax.dot_general(
        normed_heads, out_rows, (((1,), (1,)), ((), ())), preferred_element_type=jnp.float32
    )
    summed = lax.psum_scatter(
        projected.astype(jnp.bfloat16),
        "tp",
        scatter_dimension=0,
        tiled=True,
    ).astype(jnp.float32)
    return (tokens.astype(jnp.float32) + summed).astype(jnp.bfloat16)


def solution(mesh):
    z_rows = 4 if mesh.shape["ctx"] % 4 == 0 else 1
    split = jax.sharding.Mesh(
        mesh.devices.reshape(mesh.shape["ctx"] // z_rows, z_rows, mesh.shape["tp"]), ("cz", "cy", "tp")
    )
    blocks = ("cz", "cy")
    placed = (
        P(blocks + ("tp",), None),
        P(),
        P(blocks, "tp"),
        P("tp", blocks),
        P("tp"),
        P("tp", blocks),
        P("tp", blocks),
        P("tp"),
        P(blocks),
    )
    return jax.shard_map(
        local, mesh=split, in_specs=placed, out_specs=P(blocks + ("tp",), None), check_vma=False
    )
```

```python
import functools

import jax
import jax.numpy as jnp
from jax import lax
from jax.experimental import pallas as pl
from jax.experimental.pallas import tpu as pltpu
from jax.sharding import PartitionSpec as P

DK = 256
DV = 512


EPSILON = 1e-06
FORGET_STEP = 0.5
INPUT_STEP = 0.5


MESH_ID = pl.DeviceIdType.MESH
DECAY_ROWS = 16


def scan_shifts(count):
    shifts = [1] + ([2] if count > 2 else [])
    k = 2
    while k < count:
        shifts.append(k)
        k *= 2
    return shifts


def pack(ref, total, decay):
    rows = total.shape[0]
    high = decay.astype(jnp.bfloat16)
    ref[:rows, :] = total.astype(jnp.bfloat16)
    ref[rows : rows + DECAY_ROWS, :] = high
    ref[rows + DECAY_ROWS :, :] = (decay - high.astype(jnp.float32)).astype(jnp.bfloat16)


def absorb(got, rows, acc_total, acc_decay):
    far_total = got[:rows].astype(jnp.float32)
    far_decay = got[rows : rows + DECAY_ROWS].astype(jnp.float32) + got[rows + DECAY_ROWS :].astype(jnp.float32)
    decay = acc_decay[...]
    acc_total[...] = decay[0:1, :] * far_total + acc_total[...]
    acc_decay[...] = decay * far_decay


def scan_kernel(
    ny, nz, zshifts, state_ref, decay_ref, out_ref,
    row_send, row_recv, z_send, z_recv, p_send, p_recv,
    acc_total, acc_decay, quarter_total, quarter_decay, z_total, z_decay,
    row_send_sems, row_recv_sems, z_send_sems, z_recv_sems, p_send_sems, p_recv_sems,
):
    yi = lax.axis_index("cy")
    zi = lax.axis_index("cz")
    tp = lax.axis_index("tp")
    rows, width = state_ref.shape
    quarter = width // ny
    mine = pl.ds(pl.multiple_of(yi * quarter, quarter), quarter)

    barrier = pltpu.get_barrier_semaphore()
    z_partners = sorted(set(zshifts))
    for d in range(1, ny):
        pl.semaphore_signal(barrier, 1, device_id=(zi, lax.rem(yi + d, ny), tp), device_id_type=MESH_ID)
    for s in z_partners:
        for peer in (lax.rem(zi + s, nz), lax.rem(zi + nz - s, nz)):
            pl.semaphore_signal(barrier, 1, device_id=(peer, yi, tp), device_id_type=MESH_ID)
    pl.semaphore_wait(barrier, (ny - 1) + 2 * len(z_partners))

    def row_copy(d, target, slot):
        return pltpu.make_async_remote_copy(
            src_ref=row_send, dst_ref=row_recv.at[slot], send_sem=row_send_sems.at[d],
            recv_sem=row_recv_sems.at[slot], device_id=(zi, target, tp), device_id_type=MESH_ID,
        )

    pack(row_send, state_ref[...], decay_ref[...])
    for d in range(1, ny):
        row_copy(d, lax.rem(yi + d, ny), yi).start()
    for d in range(1, ny):
        source = lax.rem(yi + ny - d, ny)
        row_copy(d, yi, source).wait_recv()

    acc_total[...] = jnp.zeros_like(acc_total)
    acc_decay[...] = jnp.ones_like(acc_decay)
    for d in range(1, ny):
        @pl.when(yi - d >= 0)
        def _():
            absorb(row_recv[yi - d], rows, acc_total, acc_decay)

    quarter_total[...] = jnp.zeros_like(quarter_total)
    quarter_decay[...] = jnp.ones_like(quarter_decay)
    for y in reversed(range(ny)):
        @pl.when(yi == y)
        def _():
            absorb(row_send[:, mine], rows, quarter_total, quarter_decay)

        @pl.when(yi != y)
        def _():
            absorb(row_recv[y, :, mine], rows, quarter_total, quarter_decay)

    def z_copy(j, slot, peer):
        return pltpu.make_async_remote_copy(
            src_ref=z_send.at[slot], dst_ref=z_recv.at[j], send_sem=z_send_sems.at[j],
            recv_sem=z_recv_sems.at[j], device_id=(peer, yi, tp), device_id_type=MESH_ID,
        )

    def z_send_round(j, slot):
        @pl.when(zi + zshifts[j] < nz)
        def _():
            z_copy(j, slot, zi + zshifts[j]).start()

    def z_absorb(j, slot):
        @pl.when(zi - zshifts[j] >= 0)
        def _():
            z_copy(j, slot, zi - zshifts[j]).wait_recv()
            absorb(z_recv[j], rows, z_total, z_decay)

    z_total[...] = jnp.zeros_like(z_total)
    z_decay[...] = jnp.ones_like(z_decay)
    first = min(2, len(zshifts))
    if zshifts:
        pack(z_send.at[0], quarter_total[...], quarter_decay[...])
    for j in range(first):
        z_send_round(j, 0)
    for j in range(first):
        z_absorb(j, 0)
    for j in range(first, len(zshifts)):
        pack(z_send.at[j - 1], z_total[...], z_decay[...])
        z_send_round(j, j - 1)
        z_absorb(j, j - 1)

    def p_copy(d, target, slot):
        return pltpu.make_async_remote_copy(
            src_ref=p_send, dst_ref=p_recv.at[slot], send_sem=p_send_sems.at[d],
            recv_sem=p_recv_sems.at[slot], device_id=(zi, target, tp), device_id_type=MESH_ID,
        )

    p_send[...] = z_total[...].astype(jnp.bfloat16)
    for d in range(1, ny):
        p_copy(d, lax.rem(yi + d, ny), yi).start()
    for d in range(1, ny):
        p_copy(d, yi, lax.rem(yi + ny - d, ny)).wait_recv()
    decay = acc_decay[0:1, :]
    for y in range(ny):
        cols = slice(y * quarter, (y + 1) * quarter)

        @pl.when(yi == y)
        def _():
            out_ref[:, cols] = decay[:, cols] * p_send[...].astype(jnp.float32) + acc_total[:, cols]

        @pl.when(yi != y)
        def _():
            out_ref[:, cols] = decay[:, cols] * p_recv[y].astype(jnp.float32) + acc_total[:, cols]

    for d in range(1, ny):
        row_copy(d, lax.rem(yi + d, ny), yi).wait_send()
        p_copy(d, lax.rem(yi + d, ny), yi).wait_send()
    for j in range(len(zshifts)):
        @pl.when(zi + zshifts[j] < nz)
        def _():
            z_copy(j, 0 if j < first else j - 1, zi + zshifts[j]).wait_send()


def ring_steps(n):
    steps = [(s, True) for s in range(1, (n - 1) // 2 + 1)]
    if n % 2 == 0 and n > 1:
        steps.append((n // 2, False))
    return steps


def gather_kernel(ny, nz, piece_ref, out_ref, local_sem, send_sems, recv_sems):
    yi = lax.axis_index("cy")
    zi = lax.axis_index("cz")
    tp = lax.axis_index("tp")
    half = piece_ref.shape[1] // 2
    cols = (pl.ds(0, half), pl.ds(half, half))

    barrier = pltpu.get_barrier_semaphore()
    neighbours = [
        (zi, lax.rem(yi + 1, ny), tp),
        (zi, lax.rem(yi + ny - 1, ny), tp),
        (lax.rem(zi + 1, nz), yi, tp),
        (lax.rem(zi + nz - 1, nz), yi, tp),
    ]
    for peer in neighbours:
        pl.semaphore_signal(barrier, 1, device_id=peer, device_id_type=MESH_ID)
    pl.semaphore_wait(barrier, len(neighbours))

    own = pltpu.make_async_copy(piece_ref, out_ref.at[zi, yi], local_sem.at[0])
    own.start()
    sends = []

    def ring(along_y, group_of, first_src):
        n, me = (ny, yi) if along_y else (nz, zi)
        return dict(n=n, me=me, along_y=along_y, group_of=group_of, first_src=first_src, steps=ring_steps(n), last={})

    def device(r, k):
        return (zi, k, tp) if r["along_y"] else (k, yi, tp)

    def step(r, t):
        if t > len(r["steps"]):
            return
        n, me, group_of = r["n"], r["me"], r["group_of"]
        hop, both = r["steps"][t - 1]
        for sign in (1, -1) if both else (1,):
            if t > 1:
                r["last"].pop(sign).wait_recv()
            origin = lax.rem(me + n - sign * (hop - 1), n)
            target = lax.rem(me + n + sign, n)
            source = lax.rem(me + n - sign, n)
            arrived = lax.rem(me + 2 * n - sign * hop, n)
            idx = len(sends)
            send = pltpu.make_async_remote_copy(
                src_ref=r["first_src"] if t == 1 else group_of(origin), dst_ref=group_of(origin),
                send_sem=send_sems.at[idx], recv_sem=recv_sems.at[idx],
                device_id=device(r, target), device_id_type=MESH_ID,
            )
            incoming = pltpu.make_async_remote_copy(
                src_ref=group_of(arrived), dst_ref=group_of(arrived),
                send_sem=send_sems.at[idx], recv_sem=recv_sems.at[idx],
                device_id=device(r, source), device_id_type=MESH_ID,
            )
            send.start()
            sends.append(send)
            r["last"][sign] = incoming

    def stage(rings):
        for t in range(1, max(len(r["steps"]) for r in rings) + 1):
            for r in rings:
                step(r, t)
        for r in rings:
            for incoming in r["last"].values():
                incoming.wait_recv()

    stage([
        ring(True, lambda k: out_ref.at[zi, k, :, cols[0]], piece_ref.at[:, cols[0]]),
        ring(False, lambda k: out_ref.at[k, yi, :, cols[1]], piece_ref.at[:, cols[1]]),
    ])
    own.wait()
    stage([
        ring(False, lambda k: out_ref.at[k, :, :, cols[0]], out_ref.at[zi, :, :, cols[0]]),
        ring(True, lambda k: out_ref.at[:, k, :, cols[1]], out_ref.at[:, yi, :, cols[1]]),
    ])
    for send in sends:
        send.wait_send()


def gather_blocks(piece):
    ny, nz = lax.axis_size("cy"), lax.axis_size("cz")
    rows, width = piece.shape
    count = sum(2 if both else 1 for _, both in ring_steps(ny)) * 2 + sum(2 if both else 1 for _, both in ring_steps(nz)) * 2
    out = pl.pallas_call(
        functools.partial(gather_kernel, ny, nz),
        out_shape=jax.ShapeDtypeStruct((nz, ny, rows, width), piece.dtype),
        in_specs=[pl.BlockSpec(memory_space=pltpu.VMEM)],
        out_specs=pl.BlockSpec(memory_space=pl.ANY),
        scratch_shapes=[
            pltpu.SemaphoreType.DMA((1,)),
            pltpu.SemaphoreType.DMA((count,)),
            pltpu.SemaphoreType.DMA((count,)),
        ],
        compiler_params=pltpu.CompilerParams(collective_id=1, has_side_effects=True),
    )(piece)
    return out.reshape(nz * ny * rows, width)


def carried_in(passing, state):
    ny, nz = lax.axis_size("cy"), lax.axis_size("cz")
    if ny * nz == 1:
        return jnp.zeros_like(state)
    zshifts = scan_shifts(nz) if nz > 1 else []
    rows, width = state.shape
    quarter = width // ny
    decay = jnp.broadcast_to(passing.reshape(1, 1), (DECAY_ROWS, width)).astype(jnp.float32)
    message = rows + 2 * DECAY_ROWS
    slots = max(len(zshifts), 1)
    return pl.pallas_call(
        functools.partial(scan_kernel, ny, nz, zshifts),
        out_shape=jax.ShapeDtypeStruct((rows, width), jnp.float32),
        in_specs=[pl.BlockSpec(memory_space=pltpu.VMEM)] * 2,
        out_specs=pl.BlockSpec(memory_space=pltpu.VMEM),
        scratch_shapes=[
            pltpu.VMEM((message, width), jnp.bfloat16),
            pltpu.VMEM((ny, message, width), jnp.bfloat16),
            pltpu.VMEM((slots, message, quarter), jnp.bfloat16),
            pltpu.VMEM((slots, message, quarter), jnp.bfloat16),
            pltpu.VMEM((rows, quarter), jnp.bfloat16),
            pltpu.VMEM((ny, rows, quarter), jnp.bfloat16),
            pltpu.VMEM((rows, width), jnp.float32),
            pltpu.VMEM((DECAY_ROWS, width), jnp.float32),
            pltpu.VMEM((rows, quarter), jnp.float32),
            pltpu.VMEM((DECAY_ROWS, quarter), jnp.float32),
            pltpu.VMEM((rows, quarter), jnp.float32),
            pltpu.VMEM((DECAY_ROWS, quarter), jnp.float32),
            pltpu.SemaphoreType.DMA((ny,)),
            pltpu.SemaphoreType.DMA((ny,)),
            pltpu.SemaphoreType.DMA((slots,)),
            pltpu.SemaphoreType.DMA((slots,)),
            pltpu.SemaphoreType.DMA((ny,)),
            pltpu.SemaphoreType.DMA((ny,)),
        ],
        compiler_params=pltpu.CompilerParams(collective_id=0, has_side_effects=True),
    )(state.astype(jnp.float32), decay)


def rms_rows(embedded_entries, norm_gain):
    token_float = embedded_entries.astype(jnp.float32)
    moment = jnp.mean(token_float * token_float, axis=1, keepdims=True)
    return (token_float * lax.rsqrt(moment + EPSILON) * norm_gain).astype(jnp.bfloat16)


def local_terms(queries, key_rows, values, log_forget, input_gate, starts):
    length = queries.shape[0]
    scaling = queries.shape[1] ** (-0.5)
    segment = jnp.cumsum(starts)
    levels = jnp.cumsum(log_forget)
    position = jnp.arange(length)
    allowed = (position[:, None] >= position[None, :]) & (segment[:, None] == segment[None, :])
    decays = jnp.where(
        allowed,
        jnp.exp(jnp.minimum(levels[:, None] - levels[None, :], 0.0) + input_gate[None, :]),
        0.0,
    )
    scores = jnp.dot(queries, key_rows.T, preferred_element_type=jnp.float32) * scaling
    weights = (scores * decays).astype(jnp.bfloat16)
    inner_part = jnp.dot(weights, values, preferred_element_type=jnp.float32)
    last_level = levels[-1]
    last_seg = segment[-1]
    keeping = jnp.where(segment == last_seg, jnp.exp(last_level - levels + input_gate), 0.0)
    weighted = (key_rows.astype(jnp.float32) * keeping[:, None]).astype(jnp.bfloat16)
    local_state = lax.dot_general(
        weighted, values, (((0,), (0,)), ((), ())), preferred_element_type=jnp.float32
    )
    passing = jnp.where(last_seg == 0, jnp.exp(last_level), 0.0)
    carried = jnp.where(segment == 0, jnp.exp(levels), 0.0) * scaling
    return (inner_part, local_state, passing, carried)


def apply_state(queries, carried, incoming):
    lifted = queries.astype(jnp.float32) * carried[:, None]
    return jnp.dot(
        lifted, incoming, precision=lax.Precision.HIGHEST, preferred_element_type=jnp.float32
    )


def head_norm(head_out, gain):
    centre = jnp.mean(head_out, axis=1, keepdims=True)
    shifted = head_out - centre
    spread = jnp.mean(shifted * shifted, axis=1, keepdims=True)
    return (shifted * lax.rsqrt(spread + EPSILON) * gain).astype(jnp.bfloat16)


def local(
    tokens,
    norm_gain,
    w_qkv,
    w_out,
    head_gain,
    input_codes,
    forget_codes,
    forget_bias,
    document_begin_flags,
):
    normed = rms_rows(tokens, norm_gain)
    group = lax.axis_size("tp")
    copies = jnp.broadcast_to(normed[None], (group,) + normed.shape)
    every_row_list = lax.all_to_all(copies, "tp", 0, 0, tiled=True).reshape(-1, normed.shape[1])
    width = w_qkv.shape[1]
    both = gather_blocks(jnp.concatenate([w_qkv, w_out.T], axis=1))
    parameter_collection = both[:, :width]
    out_rows = both[:, width:]
    rows_combined = jnp.dot(
        every_row_list, parameter_collection, preferred_element_type=jnp.float32
    )
    rows_combined = rows_combined.astype(jnp.bfloat16)
    heads_here = forget_bias.shape[0]
    stride = 2 * DK + DV
    query_list, inner_list, state_list, passing_list, carried_list = ([], [], [], [], [])
    attention_slot_number = 0
    offset = attention_slot_number * stride
    queries = rows_combined[:, offset : offset + DK]
    key_rows = rows_combined[:, offset + DK : offset + 2 * DK]
    values = rows_combined[:, offset + 2 * DK : offset + stride]
    log_forget = jax.nn.log_sigmoid(
        FORGET_STEP * forget_codes[attention_slot_number].astype(jnp.float32)
        + forget_bias[attention_slot_number]
    )
    input_gate = INPUT_STEP * input_codes[attention_slot_number].astype(jnp.float32)
    inner_part, local_state, passing, carried = local_terms(
        queries, key_rows, values, log_forget, input_gate, document_begin_flags
    )
    query_list.append(queries)
    inner_list.append(inner_part)
    state_list.append(local_state)
    passing_list.append(passing)
    carried_list.append(carried)
    incoming = carried_in(passing_list[0], state_list[0])[None]
    attention_slot_number = 0
    head_out = inner_list[attention_slot_number] + apply_state(
        query_list[attention_slot_number],
        carried_list[attention_slot_number],
        incoming[attention_slot_number],
    )
    normed_heads = head_norm(head_out, head_gain)
    projected = lax.dot_general(
        normed_heads, out_rows, (((1,), (1,)), ((), ())), preferred_element_type=jnp.float32
    )
    summed = lax.psum_scatter(
        projected.astype(jnp.bfloat16),
        "tp",
        scatter_dimension=0,
        tiled=True,
    ).astype(jnp.float32)
    return (tokens.astype(jnp.float32) + summed).astype(jnp.bfloat16)


def solution(mesh):
    z_rows = 4 if mesh.shape["ctx"] % 4 == 0 else 1
    split = jax.sharding.Mesh(
        mesh.devices.reshape(mesh.shape["ctx"] // z_rows, z_rows, mesh.shape["tp"]), ("cz", "cy", "tp")
    )
    blocks = ("cz", "cy")
    placed = (
        P(blocks + ("tp",), None),
        P(),
        P(blocks, "tp"),
        P("tp", blocks),
        P("tp"),
        P("tp", blocks),
        P("tp", blocks),
        P("tp"),
        P(blocks),
    )
    return jax.shard_map(
        local, mesh=split, in_specs=placed, out_specs=P(blocks + ("tp",), None), check_vma=False
    )
```

```python
import functools

import jax
import jax.numpy as jnp
from jax import lax
from jax.experimental import pallas as pl
from jax.experimental.pallas import tpu as pltpu
from jax.sharding import PartitionSpec as P

DK = 256
DV = 512


EPSILON = 1e-06
FORGET_STEP = 0.5
INPUT_STEP = 0.5


MESH_ID = pl.DeviceIdType.MESH
DECAY_ROWS = 16


def scan_shifts(count):
    shifts = [1] + ([2] if count > 2 else [])
    k = 2
    while k < count:
        shifts.append(k)
        k *= 2
    return shifts


def pack(ref, total, decay):
    rows = total.shape[0]
    high = decay.astype(jnp.bfloat16)
    ref[:rows, :] = total.astype(jnp.bfloat16)
    ref[rows : rows + DECAY_ROWS, :] = high
    ref[rows + DECAY_ROWS :, :] = (decay - high.astype(jnp.float32)).astype(jnp.bfloat16)


def absorb(got, rows, acc_total, acc_decay):
    far_total = got[:rows].astype(jnp.float32)
    far_decay = got[rows : rows + DECAY_ROWS].astype(jnp.float32) + got[rows + DECAY_ROWS :].astype(jnp.float32)
    decay = acc_decay[...]
    acc_total[...] = decay[0:1, :] * far_total + acc_total[...]
    acc_decay[...] = decay * far_decay


def scan_kernel(
    ny, nz, zshifts, state_ref, decay_ref, out_ref,
    row_send, row_recv, z_send, z_recv, p_send, p_recv,
    acc_total, acc_decay, quarter_total, quarter_decay, z_total, z_decay,
    row_send_sems, row_recv_sems, z_send_sems, z_recv_sems, p_send_sems, p_recv_sems,
):
    yi = lax.axis_index("cy")
    zi = lax.axis_index("cz")
    tp = lax.axis_index("tp")
    rows, width = state_ref.shape
    quarter = width // ny
    mine = pl.ds(pl.multiple_of(yi * quarter, quarter), quarter)

    barrier = pltpu.get_barrier_semaphore()
    z_partners = sorted(set(zshifts))
    for d in range(1, ny):
        pl.semaphore_signal(barrier, 1, device_id=(zi, lax.rem(yi + d, ny), tp), device_id_type=MESH_ID)
    for s in z_partners:
        for peer in (lax.rem(zi + s, nz), lax.rem(zi + nz - s, nz)):
            pl.semaphore_signal(barrier, 1, device_id=(peer, yi, tp), device_id_type=MESH_ID)
    pl.semaphore_wait(barrier, (ny - 1) + 2 * len(z_partners))

    def row_copy(d, target, slot):
        return pltpu.make_async_remote_copy(
            src_ref=row_send, dst_ref=row_recv.at[slot], send_sem=row_send_sems.at[d],
            recv_sem=row_recv_sems.at[slot], device_id=(zi, target, tp), device_id_type=MESH_ID,
        )

    pack(row_send, state_ref[...], decay_ref[...])
    for d in range(1, ny):
        row_copy(d, lax.rem(yi + d, ny), yi).start()
    for d in range(1, ny):
        source = lax.rem(yi + ny - d, ny)
        row_copy(d, yi, source).wait_recv()

    acc_total[...] = jnp.zeros_like(acc_total)
    acc_decay[...] = jnp.ones_like(acc_decay)
    for d in range(1, ny):
        @pl.when(yi - d >= 0)
        def _():
            absorb(row_recv[yi - d], rows, acc_total, acc_decay)

    quarter_total[...] = jnp.zeros_like(quarter_total)
    quarter_decay[...] = jnp.ones_like(quarter_decay)
    for y in reversed(range(ny)):
        @pl.when(yi == y)
        def _():
            absorb(row_send[:, mine], rows, quarter_total, quarter_decay)

        @pl.when(yi != y)
        def _():
            absorb(row_recv[y, :, mine], rows, quarter_total, quarter_decay)

    def z_copy(j, slot, peer):
        return pltpu.make_async_remote_copy(
            src_ref=z_send.at[slot], dst_ref=z_recv.at[j], send_sem=z_send_sems.at[j],
            recv_sem=z_recv_sems.at[j], device_id=(peer, yi, tp), device_id_type=MESH_ID,
        )

    def z_send_round(j, slot):
        @pl.when(zi + zshifts[j] < nz)
        def _():
            z_copy(j, slot, zi + zshifts[j]).start()

    def z_absorb(j, slot):
        @pl.when(zi - zshifts[j] >= 0)
        def _():
            z_copy(j, slot, zi - zshifts[j]).wait_recv()
            absorb(z_recv[j], rows, z_total, z_decay)

    z_total[...] = jnp.zeros_like(z_total)
    z_decay[...] = jnp.ones_like(z_decay)
    first = min(2, len(zshifts))
    if zshifts:
        pack(z_send.at[0], quarter_total[...], quarter_decay[...])
    for j in range(first):
        z_send_round(j, 0)
    for j in range(first):
        z_absorb(j, 0)
    for j in range(first, len(zshifts)):
        pack(z_send.at[j - 1], z_total[...], z_decay[...])
        z_send_round(j, j - 1)
        z_absorb(j, j - 1)

    def p_copy(d, target, slot):
        return pltpu.make_async_remote_copy(
            src_ref=p_send, dst_ref=p_recv.at[slot], send_sem=p_send_sems.at[d],
            recv_sem=p_recv_sems.at[slot], device_id=(zi, target, tp), device_id_type=MESH_ID,
        )

    p_send[...] = z_total[...].astype(jnp.bfloat16)
    for d in range(1, ny):
        p_copy(d, lax.rem(yi + d, ny), yi).start()
    for d in range(1, ny):
        p_copy(d, yi, lax.rem(yi + ny - d, ny)).wait_recv()
    decay = acc_decay[0:1, :]
    for y in range(ny):
        cols = slice(y * quarter, (y + 1) * quarter)

        @pl.when(yi == y)
        def _():
            out_ref[:, cols] = decay[:, cols] * p_send[...].astype(jnp.float32) + acc_total[:, cols]

        @pl.when(yi != y)
        def _():
            out_ref[:, cols] = decay[:, cols] * p_recv[y].astype(jnp.float32) + acc_total[:, cols]

    for d in range(1, ny):
        row_copy(d, lax.rem(yi + d, ny), yi).wait_send()
        p_copy(d, lax.rem(yi + d, ny), yi).wait_send()
    for j in range(len(zshifts)):
        @pl.when(zi + zshifts[j] < nz)
        def _():
            z_copy(j, 0 if j < first else j - 1, zi + zshifts[j]).wait_send()


def ring_steps(n):
    steps = [(s, True) for s in range(1, (n - 1) // 2 + 1)]
    if n % 2 == 0 and n > 1:
        steps.append((n // 2, False))
    return steps


def gather_kernel(ny, nz, nt, piece_ref, rows_ref, out_ref, rows_out, local_sem, send_sems, recv_sems):
    yi = lax.axis_index("cy")
    zi = lax.axis_index("cz")
    tp = lax.axis_index("tp")
    half = piece_ref.shape[1] // 2
    cols = (pl.ds(0, half), pl.ds(half, half))

    barrier = pltpu.get_barrier_semaphore()
    neighbours = [
        (zi, lax.rem(yi + 1, ny), tp),
        (zi, lax.rem(yi + ny - 1, ny), tp),
        (lax.rem(zi + 1, nz), yi, tp),
        (lax.rem(zi + nz - 1, nz), yi, tp),
        (zi, yi, lax.rem(tp + 1, nt)),
        (zi, yi, lax.rem(tp + nt - 1, nt)),
    ]
    for peer in neighbours:
        pl.semaphore_signal(barrier, 1, device_id=peer, device_id_type=MESH_ID)
    pl.semaphore_wait(barrier, len(neighbours))

    own = pltpu.make_async_copy(piece_ref, out_ref.at[zi, yi], local_sem.at[0])
    own.start()
    own_rows = pltpu.make_async_copy(rows_ref, rows_out.at[tp], local_sem.at[1])
    own_rows.start()
    sends = []

    def ring(along, group_of, first_src):
        n, me = {"y": (ny, yi), "z": (nz, zi), "t": (nt, tp)}[along]
        return dict(n=n, me=me, along=along, group_of=group_of, first_src=first_src, steps=ring_steps(n), last={})

    def device(r, k):
        return {"y": (zi, k, tp), "z": (k, yi, tp), "t": (zi, yi, k)}[r["along"]]

    def step(r, t):
        if t > len(r["steps"]):
            return
        n, me, group_of = r["n"], r["me"], r["group_of"]
        hop, both = r["steps"][t - 1]
        for sign in (1, -1) if both else (1,):
            if t > 1:
                r["last"].pop(sign).wait_recv()
            origin = lax.rem(me + n - sign * (hop - 1), n)
            target = lax.rem(me + n + sign, n)
            source = lax.rem(me + n - sign, n)
            arrived = lax.rem(me + 2 * n - sign * hop, n)
            idx = len(sends)
            send = pltpu.make_async_remote_copy(
                src_ref=r["first_src"] if t == 1 else group_of(origin), dst_ref=group_of(origin),
                send_sem=send_sems.at[idx], recv_sem=recv_sems.at[idx],
                device_id=device(r, target), device_id_type=MESH_ID,
            )
            incoming = pltpu.make_async_remote_copy(
                src_ref=group_of(arrived), dst_ref=group_of(arrived),
                send_sem=send_sems.at[idx], recv_sem=recv_sems.at[idx],
                device_id=device(r, source), device_id_type=MESH_ID,
            )
            send.start()
            sends.append(send)
            r["last"][sign] = incoming

    def stage(rings):
        for t in range(1, max(len(r["steps"]) for r in rings) + 1):
            for r in rings:
                step(r, t)
        for r in rings:
            for incoming in r["last"].values():
                incoming.wait_recv()

    stage([
        ring("y", lambda k: out_ref.at[zi, k, :, cols[0]], piece_ref.at[:, cols[0]]),
        ring("z", lambda k: out_ref.at[k, yi, :, cols[1]], piece_ref.at[:, cols[1]]),
    ])
    own.wait()
    stage([
        ring("z", lambda k: out_ref.at[k, :, :, cols[0]], out_ref.at[zi, :, :, cols[0]]),
        ring("y", lambda k: out_ref.at[:, k, :, cols[1]], out_ref.at[:, yi, :, cols[1]]),
        ring("t", lambda k: rows_out.at[k], rows_ref),
    ])
    own_rows.wait()
    for send in sends:
        send.wait_send()


def gather_blocks(piece, rows):
    ny, nz, nt = lax.axis_size("cy"), lax.axis_size("cz"), lax.axis_size("tp")
    height, width = piece.shape
    count = sum(sum(2 if both else 1 for _, both in ring_steps(n)) for n in (ny, nz, nz, ny, nt))
    out, rows_out = pl.pallas_call(
        functools.partial(gather_kernel, ny, nz, nt),
        out_shape=(
            jax.ShapeDtypeStruct((nz, ny, height, width), piece.dtype),
            jax.ShapeDtypeStruct((nt,) + rows.shape, rows.dtype),
        ),
        in_specs=[pl.BlockSpec(memory_space=pltpu.VMEM)] * 2,
        out_specs=(pl.BlockSpec(memory_space=pl.ANY), pl.BlockSpec(memory_space=pl.ANY)),
        scratch_shapes=[
            pltpu.SemaphoreType.DMA((2,)),
            pltpu.SemaphoreType.DMA((count,)),
            pltpu.SemaphoreType.DMA((count,)),
        ],
        compiler_params=pltpu.CompilerParams(collective_id=1, has_side_effects=True),
    )(piece, rows)
    return out.reshape(nz * ny * height, width), rows_out.reshape(nt * rows.shape[0], rows.shape[1])


def carried_in(passing, state):
    ny, nz = lax.axis_size("cy"), lax.axis_size("cz")
    if ny * nz == 1:
        return jnp.zeros_like(state)
    zshifts = scan_shifts(nz) if nz > 1 else []
    rows, width = state.shape
    quarter = width // ny
    decay = jnp.broadcast_to(passing.reshape(1, 1), (DECAY_ROWS, width)).astype(jnp.float32)
    message = rows + 2 * DECAY_ROWS
    slots = max(len(zshifts), 1)
    return pl.pallas_call(
        functools.partial(scan_kernel, ny, nz, zshifts),
        out_shape=jax.ShapeDtypeStruct((rows, width), jnp.float32),
        in_specs=[pl.BlockSpec(memory_space=pltpu.VMEM)] * 2,
        out_specs=pl.BlockSpec(memory_space=pltpu.VMEM),
        scratch_shapes=[
            pltpu.VMEM((message, width), jnp.bfloat16),
            pltpu.VMEM((ny, message, width), jnp.bfloat16),
            pltpu.VMEM((slots, message, quarter), jnp.bfloat16),
            pltpu.VMEM((slots, message, quarter), jnp.bfloat16),
            pltpu.VMEM((rows, quarter), jnp.bfloat16),
            pltpu.VMEM((ny, rows, quarter), jnp.bfloat16),
            pltpu.VMEM((rows, width), jnp.float32),
            pltpu.VMEM((DECAY_ROWS, width), jnp.float32),
            pltpu.VMEM((rows, quarter), jnp.float32),
            pltpu.VMEM((DECAY_ROWS, quarter), jnp.float32),
            pltpu.VMEM((rows, quarter), jnp.float32),
            pltpu.VMEM((DECAY_ROWS, quarter), jnp.float32),
            pltpu.SemaphoreType.DMA((ny,)),
            pltpu.SemaphoreType.DMA((ny,)),
            pltpu.SemaphoreType.DMA((slots,)),
            pltpu.SemaphoreType.DMA((slots,)),
            pltpu.SemaphoreType.DMA((ny,)),
            pltpu.SemaphoreType.DMA((ny,)),
        ],
        compiler_params=pltpu.CompilerParams(collective_id=0, has_side_effects=True),
    )(state.astype(jnp.float32), decay)


def rms_rows(embedded_entries, norm_gain):
    token_float = embedded_entries.astype(jnp.float32)
    moment = jnp.mean(token_float * token_float, axis=1, keepdims=True)
    return (token_float * lax.rsqrt(moment + EPSILON) * norm_gain).astype(jnp.bfloat16)


def local_terms(queries, key_rows, values, log_forget, input_gate, starts):
    length = queries.shape[0]
    scaling = queries.shape[1] ** (-0.5)
    segment = jnp.cumsum(starts)
    levels = jnp.cumsum(log_forget)
    position = jnp.arange(length)
    allowed = (position[:, None] >= position[None, :]) & (segment[:, None] == segment[None, :])
    decays = jnp.where(
        allowed,
        jnp.exp(jnp.minimum(levels[:, None] - levels[None, :], 0.0) + input_gate[None, :]),
        0.0,
    )
    scores = jnp.dot(queries, key_rows.T, preferred_element_type=jnp.float32) * scaling
    weights = (scores * decays).astype(jnp.bfloat16)
    inner_part = jnp.dot(weights, values, preferred_element_type=jnp.float32)
    last_level = levels[-1]
    last_seg = segment[-1]
    keeping = jnp.where(segment == last_seg, jnp.exp(last_level - levels + input_gate), 0.0)
    weighted = (key_rows.astype(jnp.float32) * keeping[:, None]).astype(jnp.bfloat16)
    local_state = lax.dot_general(
        weighted, values, (((0,), (0,)), ((), ())), preferred_element_type=jnp.float32
    )
    passing = jnp.where(last_seg == 0, jnp.exp(last_level), 0.0)
    carried = jnp.where(segment == 0, jnp.exp(levels), 0.0) * scaling
    return (inner_part, local_state, passing, carried)


def apply_state(queries, carried, incoming):
    lifted = queries.astype(jnp.float32) * carried[:, None]
    return jnp.dot(
        lifted, incoming, precision=lax.Precision.HIGHEST, preferred_element_type=jnp.float32
    )


def head_norm(head_out, gain):
    centre = jnp.mean(head_out, axis=1, keepdims=True)
    shifted = head_out - centre
    spread = jnp.mean(shifted * shifted, axis=1, keepdims=True)
    return (shifted * lax.rsqrt(spread + EPSILON) * gain).astype(jnp.bfloat16)


def local(
    tokens,
    norm_gain,
    w_qkv,
    w_out,
    head_gain,
    input_codes,
    forget_codes,
    forget_bias,
    document_begin_flags,
):
    normed = rms_rows(tokens, norm_gain)
    width = w_qkv.shape[1]
    both, every_row_list = gather_blocks(jnp.concatenate([w_qkv, w_out.T], axis=1), normed)
    parameter_collection = both[:, :width]
    out_rows = both[:, width:]
    rows_combined = jnp.dot(
        every_row_list, parameter_collection, preferred_element_type=jnp.float32
    )
    rows_combined = rows_combined.astype(jnp.bfloat16)
    heads_here = forget_bias.shape[0]
    stride = 2 * DK + DV
    query_list, inner_list, state_list, passing_list, carried_list = ([], [], [], [], [])
    attention_slot_number = 0
    offset = attention_slot_number * stride
    queries = rows_combined[:, offset : offset + DK]
    key_rows = rows_combined[:, offset + DK : offset + 2 * DK]
    values = rows_combined[:, offset + 2 * DK : offset + stride]
    log_forget = jax.nn.log_sigmoid(
        FORGET_STEP * forget_codes[attention_slot_number].astype(jnp.float32)
        + forget_bias[attention_slot_number]
    )
    input_gate = INPUT_STEP * input_codes[attention_slot_number].astype(jnp.float32)
    inner_part, local_state, passing, carried = local_terms(
        queries, key_rows, values, log_forget, input_gate, document_begin_flags
    )
    query_list.append(queries)
    inner_list.append(inner_part)
    state_list.append(local_state)
    passing_list.append(passing)
    carried_list.append(carried)
    incoming = carried_in(passing_list[0], state_list[0])[None]
    attention_slot_number = 0
    head_out = inner_list[attention_slot_number] + apply_state(
        query_list[attention_slot_number],
        carried_list[attention_slot_number],
        incoming[attention_slot_number],
    )
    normed_heads = head_norm(head_out, head_gain)
    projected = lax.dot_general(
        normed_heads, out_rows, (((1,), (1,)), ((), ())), preferred_element_type=jnp.float32
    )
    summed = lax.psum_scatter(
        projected.astype(jnp.bfloat16),
        "tp",
        scatter_dimension=0,
        tiled=True,
    ).astype(jnp.float32)
    return (tokens.astype(jnp.float32) + summed).astype(jnp.bfloat16)


def solution(mesh):
    z_rows = 4 if mesh.shape["ctx"] % 4 == 0 else 1
    split = jax.sharding.Mesh(
        mesh.devices.reshape(mesh.shape["ctx"] // z_rows, z_rows, mesh.shape["tp"]), ("cz", "cy", "tp")
    )
    blocks = ("cz", "cy")
    placed = (
        P(blocks + ("tp",), None),
        P(),
        P(blocks, "tp"),
        P("tp", blocks),
        P("tp"),
        P("tp", blocks),
        P("tp", blocks),
        P("tp"),
        P(blocks),
    )
    return jax.shard_map(
        local, mesh=split, in_specs=placed, out_specs=P(blocks + ("tp",), None), check_vma=False
    )
```

```python
import functools

import jax
import jax.numpy as jnp
from jax import lax
from jax.experimental import pallas as pl
from jax.experimental.pallas import tpu as pltpu
from jax.sharding import PartitionSpec as P

DK = 256
DV = 512


EPSILON = 1e-06
FORGET_STEP = 0.5
INPUT_STEP = 0.5


MESH_ID = pl.DeviceIdType.MESH
DECAY_ROWS = 16


def scan_shifts(count):
    shifts = [1] + ([2] if count > 2 else [])
    k = 2
    while k < count:
        shifts.append(k)
        k *= 2
    return shifts


def pack(ref, total, decay):
    rows = total.shape[0]
    high = decay.astype(jnp.bfloat16)
    ref[:rows, :] = total.astype(jnp.bfloat16)
    ref[rows : rows + DECAY_ROWS, :] = high
    ref[rows + DECAY_ROWS :, :] = (decay - high.astype(jnp.float32)).astype(jnp.bfloat16)


def absorb(got, rows, acc_total, acc_decay):
    far_total = got[:rows].astype(jnp.float32)
    far_decay = got[rows : rows + DECAY_ROWS].astype(jnp.float32) + got[rows + DECAY_ROWS :].astype(jnp.float32)
    decay = acc_decay[...]
    acc_total[...] = decay[0:1, :] * far_total + acc_total[...]
    acc_decay[...] = decay * far_decay


def scan_kernel(
    ny, nz, zshifts, state_ref, decay_ref, out_ref,
    row_send, row_recv, z_send, z_recv, p_send, p_recv,
    acc_total, acc_decay, quarter_total, quarter_decay, z_total, z_decay,
    row_send_sems, row_recv_sems, z_send_sems, z_recv_sems, p_send_sems, p_recv_sems,
):
    yi = lax.axis_index("cy")
    zi = lax.axis_index("cz")
    tp = lax.axis_index("tp")
    rows, width = state_ref.shape
    quarter = width // ny
    mine = pl.ds(pl.multiple_of(yi * quarter, quarter), quarter)

    barrier = pltpu.get_barrier_semaphore()
    z_partners = sorted(set(zshifts))
    for d in range(1, ny):
        pl.semaphore_signal(barrier, 1, device_id=(zi, lax.rem(yi + d, ny), tp), device_id_type=MESH_ID)
    for s in z_partners:
        for peer in (lax.rem(zi + s, nz), lax.rem(zi + nz - s, nz)):
            pl.semaphore_signal(barrier, 1, device_id=(peer, yi, tp), device_id_type=MESH_ID)
    pl.semaphore_wait(barrier, (ny - 1) + 2 * len(z_partners))

    def row_copy(d, target, slot):
        return pltpu.make_async_remote_copy(
            src_ref=row_send, dst_ref=row_recv.at[slot], send_sem=row_send_sems.at[d],
            recv_sem=row_recv_sems.at[slot], device_id=(zi, target, tp), device_id_type=MESH_ID,
        )

    pack(row_send, state_ref[...], decay_ref[...])
    for d in range(1, ny):
        row_copy(d, lax.rem(yi + d, ny), yi).start()
    for d in range(1, ny):
        source = lax.rem(yi + ny - d, ny)
        row_copy(d, yi, source).wait_recv()

    acc_total[...] = jnp.zeros_like(acc_total)
    acc_decay[...] = jnp.ones_like(acc_decay)
    for d in range(1, ny):
        @pl.when(yi - d >= 0)
        def _():
            absorb(row_recv[yi - d], rows, acc_total, acc_decay)

    quarter_total[...] = jnp.zeros_like(quarter_total)
    quarter_decay[...] = jnp.ones_like(quarter_decay)
    for y in reversed(range(ny)):
        @pl.when(yi == y)
        def _():
            absorb(row_send[:, mine], rows, quarter_total, quarter_decay)

        @pl.when(yi != y)
        def _():
            absorb(row_recv[y, :, mine], rows, quarter_total, quarter_decay)

    def z_copy(j, slot, peer):
        return pltpu.make_async_remote_copy(
            src_ref=z_send.at[slot], dst_ref=z_recv.at[j], send_sem=z_send_sems.at[j],
            recv_sem=z_recv_sems.at[j], device_id=(peer, yi, tp), device_id_type=MESH_ID,
        )

    def z_send_round(j, slot):
        @pl.when(zi + zshifts[j] < nz)
        def _():
            z_copy(j, slot, zi + zshifts[j]).start()

    def z_absorb(j, slot):
        @pl.when(zi - zshifts[j] >= 0)
        def _():
            z_copy(j, slot, zi - zshifts[j]).wait_recv()
            absorb(z_recv[j], rows, z_total, z_decay)

    z_total[...] = jnp.zeros_like(z_total)
    z_decay[...] = jnp.ones_like(z_decay)
    first = min(2, len(zshifts))
    if zshifts:
        pack(z_send.at[0], quarter_total[...], quarter_decay[...])
    for j in range(first):
        z_send_round(j, 0)
    for j in range(first):
        z_absorb(j, 0)
    for j in range(first, len(zshifts)):
        pack(z_send.at[j - 1], z_total[...], z_decay[...])
        z_send_round(j, j - 1)
        z_absorb(j, j - 1)

    def p_copy(d, target, slot):
        return pltpu.make_async_remote_copy(
            src_ref=p_send, dst_ref=p_recv.at[slot], send_sem=p_send_sems.at[d],
            recv_sem=p_recv_sems.at[slot], device_id=(zi, target, tp), device_id_type=MESH_ID,
        )

    p_send[...] = z_total[...].astype(jnp.bfloat16)
    for d in range(1, ny):
        p_copy(d, lax.rem(yi + d, ny), yi).start()
    for d in range(1, ny):
        p_copy(d, yi, lax.rem(yi + ny - d, ny)).wait_recv()
    decay = acc_decay[0:1, :]
    for y in range(ny):
        cols = slice(y * quarter, (y + 1) * quarter)

        @pl.when(yi == y)
        def _():
            out_ref[:, cols] = decay[:, cols] * p_send[...].astype(jnp.float32) + acc_total[:, cols]

        @pl.when(yi != y)
        def _():
            out_ref[:, cols] = decay[:, cols] * p_recv[y].astype(jnp.float32) + acc_total[:, cols]

    for d in range(1, ny):
        row_copy(d, lax.rem(yi + d, ny), yi).wait_send()
        p_copy(d, lax.rem(yi + d, ny), yi).wait_send()
    for j in range(len(zshifts)):
        @pl.when(zi + zshifts[j] < nz)
        def _():
            z_copy(j, 0 if j < first else j - 1, zi + zshifts[j]).wait_send()


def ring_steps(n):
    steps = [(s, True) for s in range(1, (n - 1) // 2 + 1)]
    if n % 2 == 0 and n > 1:
        steps.append((n // 2, False))
    return steps


def gather_kernel(ny, nz, nt, piece_ref, rows_ref, out_ref, rows_out, local_sem, send_sems, recv_sems):
    yi = lax.axis_index("cy")
    zi = lax.axis_index("cz")
    tp = lax.axis_index("tp")
    half = piece_ref.shape[1] // 2
    cols = (pl.ds(0, half), pl.ds(half, half))

    barrier = pltpu.get_barrier_semaphore()
    neighbours = [
        (zi, lax.rem(yi + 1, ny), tp),
        (zi, lax.rem(yi + ny - 1, ny), tp),
        (lax.rem(zi + 1, nz), yi, tp),
        (lax.rem(zi + nz - 1, nz), yi, tp),
        (zi, yi, lax.rem(tp + 1, nt)),
        (zi, yi, lax.rem(tp + nt - 1, nt)),
    ]
    for peer in neighbours:
        pl.semaphore_signal(barrier, 1, device_id=peer, device_id_type=MESH_ID)
    pl.semaphore_wait(barrier, len(neighbours))

    own = pltpu.make_async_copy(piece_ref, out_ref.at[zi, yi], local_sem.at[0])
    own.start()
    own_rows = pltpu.make_async_copy(rows_ref, rows_out.at[tp], local_sem.at[1])
    own_rows.start()
    sends = []

    def ring(along, group_of, first_src):
        n, me = {"y": (ny, yi), "z": (nz, zi), "t": (nt, tp)}[along]
        return dict(n=n, me=me, along=along, group_of=group_of, first_src=first_src, steps=ring_steps(n), last={})

    def device(r, k):
        return {"y": (zi, k, tp), "z": (k, yi, tp), "t": (zi, yi, k)}[r["along"]]

    def step(r, t):
        if t > len(r["steps"]):
            return
        n, me, group_of = r["n"], r["me"], r["group_of"]
        hop, both = r["steps"][t - 1]
        for sign in (1, -1) if both else (1,):
            if t > 1:
                r["last"].pop(sign).wait_recv()
            origin = lax.rem(me + n - sign * (hop - 1), n)
            target = lax.rem(me + n + sign, n)
            source = lax.rem(me + n - sign, n)
            arrived = lax.rem(me + 2 * n - sign * hop, n)
            idx = len(sends)
            send = pltpu.make_async_remote_copy(
                src_ref=r["first_src"] if t == 1 else group_of(origin), dst_ref=group_of(origin),
                send_sem=send_sems.at[idx], recv_sem=recv_sems.at[idx],
                device_id=device(r, target), device_id_type=MESH_ID,
            )
            incoming = pltpu.make_async_remote_copy(
                src_ref=group_of(arrived), dst_ref=group_of(arrived),
                send_sem=send_sems.at[idx], recv_sem=recv_sems.at[idx],
                device_id=device(r, source), device_id_type=MESH_ID,
            )
            send.start()
            sends.append(send)
            r["last"][sign] = incoming

    def stage(rings):
        for t in range(1, max(len(r["steps"]) for r in rings) + 1):
            for r in rings:
                step(r, t)
        for r in rings:
            for incoming in r["last"].values():
                incoming.wait_recv()

    stage([
        ring("y", lambda k: out_ref.at[zi, k, :, cols[0]], piece_ref.at[:, cols[0]]),
        ring("z", lambda k: out_ref.at[k, yi, :, cols[1]], piece_ref.at[:, cols[1]]),
    ])
    own.wait()
    stage([
        ring("z", lambda k: out_ref.at[k, :, :, cols[0]], out_ref.at[zi, :, :, cols[0]]),
        ring("y", lambda k: out_ref.at[:, k, :, cols[1]], out_ref.at[:, yi, :, cols[1]]),
        ring("t", lambda k: rows_out.at[k], rows_ref),
    ])
    own_rows.wait()
    for send in sends:
        send.wait_send()


def gather_blocks(piece, rows):
    ny, nz, nt = lax.axis_size("cy"), lax.axis_size("cz"), lax.axis_size("tp")
    height, width = piece.shape
    count = sum(sum(2 if both else 1 for _, both in ring_steps(n)) for n in (ny, nz, nz, ny, nt))
    out, rows_out = pl.pallas_call(
        functools.partial(gather_kernel, ny, nz, nt),
        out_shape=(
            jax.ShapeDtypeStruct((nz, ny, height, width), piece.dtype),
            jax.ShapeDtypeStruct((nt,) + rows.shape, rows.dtype),
        ),
        in_specs=[pl.BlockSpec(memory_space=pltpu.VMEM)] * 2,
        out_specs=(pl.BlockSpec(memory_space=pl.ANY), pl.BlockSpec(memory_space=pl.ANY)),
        scratch_shapes=[
            pltpu.SemaphoreType.DMA((2,)),
            pltpu.SemaphoreType.DMA((count,)),
            pltpu.SemaphoreType.DMA((count,)),
        ],
        compiler_params=pltpu.CompilerParams(collective_id=1, has_side_effects=True),
    )(piece, rows)
    return out.reshape(nz * ny * height, width), rows_out.reshape(nt * rows.shape[0], rows.shape[1])


def scatter_kernel(nt, part_ref, out_ref, send_buf, recv_buf, send_sems, recv_sems):
    tp = lax.axis_index("tp")
    rows = out_ref.shape[0]
    half = out_ref.shape[1] // 2

    barrier = pltpu.get_barrier_semaphore()
    for peer in (lax.rem(tp + 1, nt), lax.rem(tp + nt - 1, nt)):
        pl.semaphore_signal(barrier, 1, device_id=(lax.axis_index("cz"), lax.axis_index("cy"), peer), device_id_type=MESH_ID)
    pl.semaphore_wait(barrier, 2)

    def own(chunk, side):
        start = pl.multiple_of(chunk * rows, 16)
        return part_ref[pl.ds(start, rows), pl.ds(side * half, half)].astype(jnp.float32)

    def copy(side, step, peer):
        slot = side * nt + step
        return pltpu.make_async_remote_copy(
            src_ref=send_buf.at[slot], dst_ref=recv_buf.at[slot], send_sem=send_sems.at[slot],
            recv_sem=recv_sems.at[slot],
            device_id=(lax.axis_index("cz"), lax.axis_index("cy"), peer), device_id_type=MESH_ID,
        )

    sides = ((0, 1), (1, -1))
    for step in range(1, nt):
        for side, sign in sides:
            chunk = lax.rem(tp + nt * nt - sign * step, nt)
            total = own(chunk, side)
            if step > 1:
                copy(side, step - 1, lax.rem(tp + nt - sign, nt)).wait_recv()
                total = total + recv_buf[side * nt + step - 1].astype(jnp.float32)
            send_buf[side * nt + step] = total.astype(jnp.bfloat16)
            copy(side, step, lax.rem(tp + nt + sign, nt)).start()
    for side, sign in sides:
        copy(side, nt - 1, lax.rem(tp + nt - sign, nt)).wait_recv()
        total = own(tp, side) + recv_buf[side * nt + nt - 1].astype(jnp.float32)
        out_ref[:, side * half : (side + 1) * half] = total.astype(out_ref.dtype)
    for step in range(1, nt):
        for side, sign in sides:
            copy(side, step, lax.rem(tp + nt + sign, nt)).wait_send()


def scatter_rows(part):
    nt = lax.axis_size("tp")
    rows = part.shape[0] // nt
    width = part.shape[1]
    return pl.pallas_call(
        functools.partial(scatter_kernel, nt),
        out_shape=jax.ShapeDtypeStruct((rows, width), part.dtype),
        in_specs=[pl.BlockSpec(memory_space=pltpu.VMEM)],
        out_specs=pl.BlockSpec(memory_space=pltpu.VMEM),
        scratch_shapes=[
            pltpu.VMEM((2 * nt, rows, width // 2), jnp.bfloat16),
            pltpu.VMEM((2 * nt, rows, width // 2), jnp.bfloat16),
            pltpu.SemaphoreType.DMA((2 * nt,)),
            pltpu.SemaphoreType.DMA((2 * nt,)),
        ],
        compiler_params=pltpu.CompilerParams(
            collective_id=2, has_side_effects=True, vmem_limit_bytes=48 * 1024 * 1024
        ),
    )(part)


def carried_in(passing, state):
    ny, nz = lax.axis_size("cy"), lax.axis_size("cz")
    if ny * nz == 1:
        return jnp.zeros_like(state)
    zshifts = scan_shifts(nz) if nz > 1 else []
    rows, width = state.shape
    quarter = width // ny
    decay = jnp.broadcast_to(passing.reshape(1, 1), (DECAY_ROWS, width)).astype(jnp.float32)
    message = rows + 2 * DECAY_ROWS
    slots = max(len(zshifts), 1)
    return pl.pallas_call(
        functools.partial(scan_kernel, ny, nz, zshifts),
        out_shape=jax.ShapeDtypeStruct((rows, width), jnp.float32),
        in_specs=[pl.BlockSpec(memory_space=pltpu.VMEM)] * 2,
        out_specs=pl.BlockSpec(memory_space=pltpu.VMEM),
        scratch_shapes=[
            pltpu.VMEM((message, width), jnp.bfloat16),
            pltpu.VMEM((ny, message, width), jnp.bfloat16),
            pltpu.VMEM((slots, message, quarter), jnp.bfloat16),
            pltpu.VMEM((slots, message, quarter), jnp.bfloat16),
            pltpu.VMEM((rows, quarter), jnp.bfloat16),
            pltpu.VMEM((ny, rows, quarter), jnp.bfloat16),
            pltpu.VMEM((rows, width), jnp.float32),
            pltpu.VMEM((DECAY_ROWS, width), jnp.float32),
            pltpu.VMEM((rows, quarter), jnp.float32),
            pltpu.VMEM((DECAY_ROWS, quarter), jnp.float32),
            pltpu.VMEM((rows, quarter), jnp.float32),
            pltpu.VMEM((DECAY_ROWS, quarter), jnp.float32),
            pltpu.SemaphoreType.DMA((ny,)),
            pltpu.SemaphoreType.DMA((ny,)),
            pltpu.SemaphoreType.DMA((slots,)),
            pltpu.SemaphoreType.DMA((slots,)),
            pltpu.SemaphoreType.DMA((ny,)),
            pltpu.SemaphoreType.DMA((ny,)),
        ],
        compiler_params=pltpu.CompilerParams(collective_id=0, has_side_effects=True),
    )(state.astype(jnp.float32), decay)


def rms_rows(embedded_entries, norm_gain):
    token_float = embedded_entries.astype(jnp.float32)
    moment = jnp.mean(token_float * token_float, axis=1, keepdims=True)
    return (token_float * lax.rsqrt(moment + EPSILON) * norm_gain).astype(jnp.bfloat16)


def local_terms(queries, key_rows, values, log_forget, input_gate, starts):
    length = queries.shape[0]
    scaling = queries.shape[1] ** (-0.5)
    segment = jnp.cumsum(starts)
    levels = jnp.cumsum(log_forget)
    position = jnp.arange(length)
    allowed = (position[:, None] >= position[None, :]) & (segment[:, None] == segment[None, :])
    decays = jnp.where(
        allowed,
        jnp.exp(jnp.minimum(levels[:, None] - levels[None, :], 0.0) + input_gate[None, :]),
        0.0,
    )
    scores = jnp.dot(queries, key_rows.T, preferred_element_type=jnp.float32) * scaling
    weights = (scores * decays).astype(jnp.bfloat16)
    inner_part = jnp.dot(weights, values, preferred_element_type=jnp.float32)
    last_level = levels[-1]
    last_seg = segment[-1]
    keeping = jnp.where(segment == last_seg, jnp.exp(last_level - levels + input_gate), 0.0)
    weighted = (key_rows.astype(jnp.float32) * keeping[:, None]).astype(jnp.bfloat16)
    local_state = lax.dot_general(
        weighted, values, (((0,), (0,)), ((), ())), preferred_element_type=jnp.float32
    )
    passing = jnp.where(last_seg == 0, jnp.exp(last_level), 0.0)
    carried = jnp.where(segment == 0, jnp.exp(levels), 0.0) * scaling
    return (inner_part, local_state, passing, carried)


def apply_state(queries, carried, incoming):
    lifted = queries.astype(jnp.float32) * carried[:, None]
    return jnp.dot(
        lifted, incoming, precision=lax.Precision.HIGHEST, preferred_element_type=jnp.float32
    )


def head_norm(head_out, gain):
    centre = jnp.mean(head_out, axis=1, keepdims=True)
    shifted = head_out - centre
    spread = jnp.mean(shifted * shifted, axis=1, keepdims=True)
    return (shifted * lax.rsqrt(spread + EPSILON) * gain).astype(jnp.bfloat16)


def local(
    tokens,
    norm_gain,
    w_qkv,
    w_out,
    head_gain,
    input_codes,
    forget_codes,
    forget_bias,
    document_begin_flags,
):
    normed = rms_rows(tokens, norm_gain)
    width = w_qkv.shape[1]
    both, every_row_list = gather_blocks(jnp.concatenate([w_qkv, w_out.T], axis=1), normed)
    parameter_collection = both[:, :width]
    out_rows = both[:, width:]
    rows_combined = jnp.dot(
        every_row_list, parameter_collection, preferred_element_type=jnp.float32
    )
    rows_combined = rows_combined.astype(jnp.bfloat16)
    heads_here = forget_bias.shape[0]
    stride = 2 * DK + DV
    query_list, inner_list, state_list, passing_list, carried_list = ([], [], [], [], [])
    attention_slot_number = 0
    offset = attention_slot_number * stride
    queries = rows_combined[:, offset : offset + DK]
    key_rows = rows_combined[:, offset + DK : offset + 2 * DK]
    values = rows_combined[:, offset + 2 * DK : offset + stride]
    log_forget = jax.nn.log_sigmoid(
        FORGET_STEP * forget_codes[attention_slot_number].astype(jnp.float32)
        + forget_bias[attention_slot_number]
    )
    input_gate = INPUT_STEP * input_codes[attention_slot_number].astype(jnp.float32)
    inner_part, local_state, passing, carried = local_terms(
        queries, key_rows, values, log_forget, input_gate, document_begin_flags
    )
    query_list.append(queries)
    inner_list.append(inner_part)
    state_list.append(local_state)
    passing_list.append(passing)
    carried_list.append(carried)
    incoming = carried_in(passing_list[0], state_list[0])[None]
    attention_slot_number = 0
    head_out = inner_list[attention_slot_number] + apply_state(
        query_list[attention_slot_number],
        carried_list[attention_slot_number],
        incoming[attention_slot_number],
    )
    normed_heads = head_norm(head_out, head_gain)
    projected = lax.dot_general(
        normed_heads, out_rows, (((1,), (1,)), ((), ())), preferred_element_type=jnp.float32
    )
    summed = scatter_rows(projected.astype(jnp.bfloat16)).astype(jnp.float32)
    return (tokens.astype(jnp.float32) + summed).astype(jnp.bfloat16)


def solution(mesh):
    z_rows = 4 if mesh.shape["ctx"] % 4 == 0 else 1
    split = jax.sharding.Mesh(
        mesh.devices.reshape(mesh.shape["ctx"] // z_rows, z_rows, mesh.shape["tp"]), ("cz", "cy", "tp")
    )
    blocks = ("cz", "cy")
    placed = (
        P(blocks + ("tp",), None),
        P(),
        P(blocks, "tp"),
        P("tp", blocks),
        P("tp"),
        P("tp", blocks),
        P("tp", blocks),
        P("tp"),
        P(blocks),
    )
    return jax.shard_map(
        local, mesh=split, in_specs=placed, out_specs=P(blocks + ("tp",), None), check_vma=False
    )
```

```python
import functools

import jax
import jax.numpy as jnp
from jax import lax
from jax.experimental import pallas as pl
from jax.experimental.pallas import tpu as pltpu
from jax.sharding import PartitionSpec as P

DK = 256
DV = 512


EPSILON = 1e-06
FORGET_STEP = 0.5
INPUT_STEP = 0.5


MESH_ID = pl.DeviceIdType.MESH
DECAY_ROWS = 16


def scan_shifts(count):
    shifts = [1] + ([2] if count > 2 else [])
    k = 2
    while k < count:
        shifts.append(k)
        k *= 2
    return shifts


def pack(ref, total, decay):
    rows = total.shape[0]
    high = decay.astype(jnp.bfloat16)
    ref[:rows, :] = total.astype(jnp.bfloat16)
    ref[rows : rows + DECAY_ROWS, :] = high
    ref[rows + DECAY_ROWS :, :] = (decay - high.astype(jnp.float32)).astype(jnp.bfloat16)


def absorb(got, rows, acc_total, acc_decay):
    far_total = got[:rows].astype(jnp.float32)
    far_decay = got[rows : rows + DECAY_ROWS].astype(jnp.float32) + got[rows + DECAY_ROWS :].astype(jnp.float32)
    decay = acc_decay[...]
    acc_total[...] = decay[0:1, :] * far_total + acc_total[...]
    acc_decay[...] = decay * far_decay


def scan_kernel(
    ny, nz, zshifts, state_ref, decay_ref, out_ref,
    row_send, row_recv, z_send, z_recv, p_send, p_recv,
    acc_total, acc_decay, quarter_total, quarter_decay, z_total, z_decay,
    row_send_sems, row_recv_sems, z_send_sems, z_recv_sems, p_send_sems, p_recv_sems,
):
    yi = lax.axis_index("cy")
    zi = lax.axis_index("cz")
    tp = lax.axis_index("tp")
    rows, width = state_ref.shape
    quarter = width // ny
    mine = pl.ds(pl.multiple_of(yi * quarter, quarter), quarter)

    barrier = pltpu.get_barrier_semaphore()
    z_partners = sorted(set(zshifts))
    for d in range(1, ny):
        pl.semaphore_signal(barrier, 1, device_id=(zi, lax.rem(yi + d, ny), tp), device_id_type=MESH_ID)
    for s in z_partners:
        for peer in (lax.rem(zi + s, nz), lax.rem(zi + nz - s, nz)):
            pl.semaphore_signal(barrier, 1, device_id=(peer, yi, tp), device_id_type=MESH_ID)
    pl.semaphore_wait(barrier, (ny - 1) + 2 * len(z_partners))

    def row_copy(d, target, slot):
        return pltpu.make_async_remote_copy(
            src_ref=row_send, dst_ref=row_recv.at[slot], send_sem=row_send_sems.at[d],
            recv_sem=row_recv_sems.at[slot], device_id=(zi, target, tp), device_id_type=MESH_ID,
        )

    pack(row_send, state_ref[...], decay_ref[...])
    for d in range(1, ny):
        row_copy(d, lax.rem(yi + d, ny), yi).start()
    for d in range(1, ny):
        source = lax.rem(yi + ny - d, ny)
        row_copy(d, yi, source).wait_recv()

    acc_total[...] = jnp.zeros_like(acc_total)
    acc_decay[...] = jnp.ones_like(acc_decay)
    for d in range(1, ny):
        @pl.when(yi - d >= 0)
        def _():
            absorb(row_recv[yi - d], rows, acc_total, acc_decay)

    quarter_total[...] = jnp.zeros_like(quarter_total)
    quarter_decay[...] = jnp.ones_like(quarter_decay)
    for y in reversed(range(ny)):
        @pl.when(yi == y)
        def _():
            absorb(row_send[:, mine], rows, quarter_total, quarter_decay)

        @pl.when(yi != y)
        def _():
            absorb(row_recv[y, :, mine], rows, quarter_total, quarter_decay)

    def z_copy(j, slot, peer):
        return pltpu.make_async_remote_copy(
            src_ref=z_send.at[slot], dst_ref=z_recv.at[j], send_sem=z_send_sems.at[j],
            recv_sem=z_recv_sems.at[j], device_id=(peer, yi, tp), device_id_type=MESH_ID,
        )

    def z_send_round(j, slot):
        @pl.when(zi + zshifts[j] < nz)
        def _():
            z_copy(j, slot, zi + zshifts[j]).start()

    def z_absorb(j, slot):
        @pl.when(zi - zshifts[j] >= 0)
        def _():
            z_copy(j, slot, zi - zshifts[j]).wait_recv()
            absorb(z_recv[j], rows, z_total, z_decay)

    z_total[...] = jnp.zeros_like(z_total)
    z_decay[...] = jnp.ones_like(z_decay)
    first = min(2, len(zshifts))
    if zshifts:
        pack(z_send.at[0], quarter_total[...], quarter_decay[...])
    for j in range(first):
        z_send_round(j, 0)
    for j in range(first):
        z_absorb(j, 0)
    for j in range(first, len(zshifts)):
        pack(z_send.at[j - 1], z_total[...], z_decay[...])
        z_send_round(j, j - 1)
        z_absorb(j, j - 1)

    def p_copy(d, target, slot):
        return pltpu.make_async_remote_copy(
            src_ref=p_send, dst_ref=p_recv.at[slot], send_sem=p_send_sems.at[d],
            recv_sem=p_recv_sems.at[slot], device_id=(zi, target, tp), device_id_type=MESH_ID,
        )

    p_send[...] = z_total[...].astype(jnp.bfloat16)
    for d in range(1, ny):
        p_copy(d, lax.rem(yi + d, ny), yi).start()
    for d in range(1, ny):
        p_copy(d, yi, lax.rem(yi + ny - d, ny)).wait_recv()
    decay = acc_decay[0:1, :]
    for y in range(ny):
        cols = slice(y * quarter, (y + 1) * quarter)

        @pl.when(yi == y)
        def _():
            out_ref[:, cols] = decay[:, cols] * p_send[...].astype(jnp.float32) + acc_total[:, cols]

        @pl.when(yi != y)
        def _():
            out_ref[:, cols] = decay[:, cols] * p_recv[y].astype(jnp.float32) + acc_total[:, cols]

    for d in range(1, ny):
        row_copy(d, lax.rem(yi + d, ny), yi).wait_send()
        p_copy(d, lax.rem(yi + d, ny), yi).wait_send()
    for j in range(len(zshifts)):
        @pl.when(zi + zshifts[j] < nz)
        def _():
            z_copy(j, 0 if j < first else j - 1, zi + zshifts[j]).wait_send()


def ring_steps(n):
    steps = [(s, True) for s in range(1, (n - 1) // 2 + 1)]
    if n % 2 == 0 and n > 1:
        steps.append((n // 2, False))
    return steps


def gather_kernel(ny, nz, nt, piece_ref, rows_ref, out_ref, rows_out, local_sem, send_sems, recv_sems):
    yi = lax.axis_index("cy")
    zi = lax.axis_index("cz")
    tp = lax.axis_index("tp")
    half = piece_ref.shape[1] // 2
    cols = (pl.ds(0, half), pl.ds(half, half))

    barrier = pltpu.get_barrier_semaphore()
    neighbours = [
        (zi, lax.rem(yi + 1, ny), tp),
        (zi, lax.rem(yi + ny - 1, ny), tp),
        (lax.rem(zi + 1, nz), yi, tp),
        (lax.rem(zi + nz - 1, nz), yi, tp),
        (zi, yi, lax.rem(tp + 1, nt)),
        (zi, yi, lax.rem(tp + nt - 1, nt)),
    ]
    for peer in neighbours:
        pl.semaphore_signal(barrier, 1, device_id=peer, device_id_type=MESH_ID)
    pl.semaphore_wait(barrier, len(neighbours))

    own = pltpu.make_async_copy(piece_ref, out_ref.at[zi, yi], local_sem.at[0])
    own.start()
    own_rows = pltpu.make_async_copy(rows_ref, rows_out.at[tp], local_sem.at[1])
    own_rows.start()
    sends = []

    def ring(along, group_of, first_src):
        n, me = {"y": (ny, yi), "z": (nz, zi), "t": (nt, tp)}[along]
        return dict(n=n, me=me, along=along, group_of=group_of, first_src=first_src, steps=ring_steps(n), last={})

    def device(r, k):
        return {"y": (zi, k, tp), "z": (k, yi, tp), "t": (zi, yi, k)}[r["along"]]

    def step(r, t):
        if t > len(r["steps"]):
            return
        n, me, group_of = r["n"], r["me"], r["group_of"]
        hop, both = r["steps"][t - 1]
        for sign in (1, -1) if both else (1,):
            if t > 1:
                r["last"].pop(sign).wait_recv()
            origin = lax.rem(me + n - sign * (hop - 1), n)
            target = lax.rem(me + n + sign, n)
            source = lax.rem(me + n - sign, n)
            arrived = lax.rem(me + 2 * n - sign * hop, n)
            idx = len(sends)
            send = pltpu.make_async_remote_copy(
                src_ref=r["first_src"] if t == 1 else group_of(origin), dst_ref=group_of(origin),
                send_sem=send_sems.at[idx], recv_sem=recv_sems.at[idx],
                device_id=device(r, target), device_id_type=MESH_ID,
            )
            incoming = pltpu.make_async_remote_copy(
                src_ref=group_of(arrived), dst_ref=group_of(arrived),
                send_sem=send_sems.at[idx], recv_sem=recv_sems.at[idx],
                device_id=device(r, source), device_id_type=MESH_ID,
            )
            send.start()
            sends.append(send)
            r["last"][sign] = incoming

    def stage(rings):
        for t in range(1, max(len(r["steps"]) for r in rings) + 1):
            for r in rings:
                step(r, t)
        for r in rings:
            for incoming in r["last"].values():
                incoming.wait_recv()

    stage([
        ring("y", lambda k: out_ref.at[zi, k, :, cols[0]], piece_ref.at[:, cols[0]]),
        ring("z", lambda k: out_ref.at[k, yi, :, cols[1]], piece_ref.at[:, cols[1]]),
    ])
    own.wait()
    stage([
        ring("z", lambda k: out_ref.at[k, :, :, cols[0]], out_ref.at[zi, :, :, cols[0]]),
        ring("y", lambda k: out_ref.at[:, k, :, cols[1]], out_ref.at[:, yi, :, cols[1]]),
        ring("t", lambda k: rows_out.at[k], rows_ref),
    ])
    own_rows.wait()
    for send in sends:
        send.wait_send()


def gather_blocks(piece, rows):
    ny, nz, nt = lax.axis_size("cy"), lax.axis_size("cz"), lax.axis_size("tp")
    height, width = piece.shape
    count = sum(sum(2 if both else 1 for _, both in ring_steps(n)) for n in (ny, nz, nz, ny, nt))
    out, rows_out = pl.pallas_call(
        functools.partial(gather_kernel, ny, nz, nt),
        out_shape=(
            jax.ShapeDtypeStruct((nz, ny, height, width), piece.dtype),
            jax.ShapeDtypeStruct((nt,) + rows.shape, rows.dtype),
        ),
        in_specs=[pl.BlockSpec(memory_space=pltpu.VMEM)] * 2,
        out_specs=(pl.BlockSpec(memory_space=pl.ANY), pl.BlockSpec(memory_space=pl.ANY)),
        scratch_shapes=[
            pltpu.SemaphoreType.DMA((2,)),
            pltpu.SemaphoreType.DMA((count,)),
            pltpu.SemaphoreType.DMA((count,)),
        ],
        compiler_params=pltpu.CompilerParams(collective_id=1, has_side_effects=True),
    )(piece, rows)
    return out.reshape(nz * ny * height, width), rows_out.reshape(nt * rows.shape[0], rows.shape[1])


def scatter_kernel(nt, heads_ref, weight_ref, out_ref, send_buf, recv_buf, send_sems, recv_sems):
    tp = lax.axis_index("tp")
    rows = out_ref.shape[0]
    half = out_ref.shape[1] // 2

    barrier = pltpu.get_barrier_semaphore()
    for peer in (lax.rem(tp + 1, nt), lax.rem(tp + nt - 1, nt)):
        pl.semaphore_signal(barrier, 1, device_id=(lax.axis_index("cz"), lax.axis_index("cy"), peer), device_id_type=MESH_ID)
    pl.semaphore_wait(barrier, 2)

    def own(chunk, side):
        start = pl.multiple_of(chunk * rows, 16)
        part = lax.dot_general(
            heads_ref[pl.ds(start, rows), :],
            weight_ref[side * half : (side + 1) * half, :],
            (((1,), (1,)), ((), ())),
            preferred_element_type=jnp.float32,
        )
        return part.astype(jnp.bfloat16).astype(jnp.float32)

    def copy(side, step, peer):
        slot = side * nt + step
        return pltpu.make_async_remote_copy(
            src_ref=send_buf.at[slot], dst_ref=recv_buf.at[slot], send_sem=send_sems.at[slot],
            recv_sem=recv_sems.at[slot],
            device_id=(lax.axis_index("cz"), lax.axis_index("cy"), peer), device_id_type=MESH_ID,
        )

    sides = ((0, 1), (1, -1))
    for step in range(1, nt):
        for side, sign in sides:
            chunk = lax.rem(tp + nt * nt - sign * step, nt)
            total = own(chunk, side)
            if step > 1:
                copy(side, step - 1, lax.rem(tp + nt - sign, nt)).wait_recv()
                total = total + recv_buf[side * nt + step - 1].astype(jnp.float32)
            send_buf[side * nt + step] = total.astype(jnp.bfloat16)
            copy(side, step, lax.rem(tp + nt + sign, nt)).start()
    for side, sign in sides:
        copy(side, nt - 1, lax.rem(tp + nt - sign, nt)).wait_recv()
        total = own(tp, side) + recv_buf[side * nt + nt - 1].astype(jnp.float32)
        out_ref[:, side * half : (side + 1) * half] = total.astype(out_ref.dtype)
    for step in range(1, nt):
        for side, sign in sides:
            copy(side, step, lax.rem(tp + nt + sign, nt)).wait_send()


def scatter_rows(heads, weight):
    nt = lax.axis_size("tp")
    rows = heads.shape[0] // nt
    width = weight.shape[0]
    return pl.pallas_call(
        functools.partial(scatter_kernel, nt),
        out_shape=jax.ShapeDtypeStruct((rows, width), jnp.bfloat16),
        in_specs=[pl.BlockSpec(memory_space=pltpu.VMEM)] * 2,
        out_specs=pl.BlockSpec(memory_space=pltpu.VMEM),
        scratch_shapes=[
            pltpu.VMEM((2 * nt, rows, width // 2), jnp.bfloat16),
            pltpu.VMEM((2 * nt, rows, width // 2), jnp.bfloat16),
            pltpu.SemaphoreType.DMA((2 * nt,)),
            pltpu.SemaphoreType.DMA((2 * nt,)),
        ],
        compiler_params=pltpu.CompilerParams(
            collective_id=2, has_side_effects=True, vmem_limit_bytes=48 * 1024 * 1024
        ),
    )(heads, weight)


def carried_in(passing, state):
    ny, nz = lax.axis_size("cy"), lax.axis_size("cz")
    if ny * nz == 1:
        return jnp.zeros_like(state)
    zshifts = scan_shifts(nz) if nz > 1 else []
    rows, width = state.shape
    quarter = width // ny
    decay = jnp.broadcast_to(passing.reshape(1, 1), (DECAY_ROWS, width)).astype(jnp.float32)
    message = rows + 2 * DECAY_ROWS
    slots = max(len(zshifts), 1)
    return pl.pallas_call(
        functools.partial(scan_kernel, ny, nz, zshifts),
        out_shape=jax.ShapeDtypeStruct((rows, width), jnp.float32),
        in_specs=[pl.BlockSpec(memory_space=pltpu.VMEM)] * 2,
        out_specs=pl.BlockSpec(memory_space=pltpu.VMEM),
        scratch_shapes=[
            pltpu.VMEM((message, width), jnp.bfloat16),
            pltpu.VMEM((ny, message, width), jnp.bfloat16),
            pltpu.VMEM((slots, message, quarter), jnp.bfloat16),
            pltpu.VMEM((slots, message, quarter), jnp.bfloat16),
            pltpu.VMEM((rows, quarter), jnp.bfloat16),
            pltpu.VMEM((ny, rows, quarter), jnp.bfloat16),
            pltpu.VMEM((rows, width), jnp.float32),
            pltpu.VMEM((DECAY_ROWS, width), jnp.float32),
            pltpu.VMEM((rows, quarter), jnp.float32),
            pltpu.VMEM((DECAY_ROWS, quarter), jnp.float32),
            pltpu.VMEM((rows, quarter), jnp.float32),
            pltpu.VMEM((DECAY_ROWS, quarter), jnp.float32),
            pltpu.SemaphoreType.DMA((ny,)),
            pltpu.SemaphoreType.DMA((ny,)),
            pltpu.SemaphoreType.DMA((slots,)),
            pltpu.SemaphoreType.DMA((slots,)),
            pltpu.SemaphoreType.DMA((ny,)),
            pltpu.SemaphoreType.DMA((ny,)),
        ],
        compiler_params=pltpu.CompilerParams(collective_id=0, has_side_effects=True),
    )(state.astype(jnp.float32), decay)


def rms_rows(embedded_entries, norm_gain):
    token_float = embedded_entries.astype(jnp.float32)
    moment = jnp.mean(token_float * token_float, axis=1, keepdims=True)
    return (token_float * lax.rsqrt(moment + EPSILON) * norm_gain).astype(jnp.bfloat16)


def local_terms(queries, key_rows, values, log_forget, input_gate, starts):
    length = queries.shape[0]
    scaling = queries.shape[1] ** (-0.5)
    segment = jnp.cumsum(starts)
    levels = jnp.cumsum(log_forget)
    position = jnp.arange(length)
    allowed = (position[:, None] >= position[None, :]) & (segment[:, None] == segment[None, :])
    decays = jnp.where(
        allowed,
        jnp.exp(jnp.minimum(levels[:, None] - levels[None, :], 0.0) + input_gate[None, :]),
        0.0,
    )
    scores = jnp.dot(queries, key_rows.T, preferred_element_type=jnp.float32) * scaling
    weights = (scores * decays).astype(jnp.bfloat16)
    inner_part = jnp.dot(weights, values, preferred_element_type=jnp.float32)
    last_level = levels[-1]
    last_seg = segment[-1]
    keeping = jnp.where(segment == last_seg, jnp.exp(last_level - levels + input_gate), 0.0)
    weighted = (key_rows.astype(jnp.float32) * keeping[:, None]).astype(jnp.bfloat16)
    local_state = lax.dot_general(
        weighted, values, (((0,), (0,)), ((), ())), preferred_element_type=jnp.float32
    )
    passing = jnp.where(last_seg == 0, jnp.exp(last_level), 0.0)
    carried = jnp.where(segment == 0, jnp.exp(levels), 0.0) * scaling
    return (inner_part, local_state, passing, carried)


def apply_state(queries, carried, incoming):
    lifted = queries.astype(jnp.float32) * carried[:, None]
    return jnp.dot(
        lifted, incoming, precision=lax.Precision.HIGHEST, preferred_element_type=jnp.float32
    )


def head_norm(head_out, gain):
    centre = jnp.mean(head_out, axis=1, keepdims=True)
    shifted = head_out - centre
    spread = jnp.mean(shifted * shifted, axis=1, keepdims=True)
    return (shifted * lax.rsqrt(spread + EPSILON) * gain).astype(jnp.bfloat16)


def local(
    tokens,
    norm_gain,
    w_qkv,
    w_out,
    head_gain,
    input_codes,
    forget_codes,
    forget_bias,
    document_begin_flags,
):
    normed = rms_rows(tokens, norm_gain)
    width = w_qkv.shape[1]
    both, every_row_list = gather_blocks(jnp.concatenate([w_qkv, w_out.T], axis=1), normed)
    parameter_collection = both[:, :width]
    out_rows = both[:, width:]
    rows_combined = jnp.dot(
        every_row_list, parameter_collection, preferred_element_type=jnp.float32
    )
    rows_combined = rows_combined.astype(jnp.bfloat16)
    heads_here = forget_bias.shape[0]
    stride = 2 * DK + DV
    query_list, inner_list, state_list, passing_list, carried_list = ([], [], [], [], [])
    attention_slot_number = 0
    offset = attention_slot_number * stride
    queries = rows_combined[:, offset : offset + DK]
    key_rows = rows_combined[:, offset + DK : offset + 2 * DK]
    values = rows_combined[:, offset + 2 * DK : offset + stride]
    log_forget = jax.nn.log_sigmoid(
        FORGET_STEP * forget_codes[attention_slot_number].astype(jnp.float32)
        + forget_bias[attention_slot_number]
    )
    input_gate = INPUT_STEP * input_codes[attention_slot_number].astype(jnp.float32)
    inner_part, local_state, passing, carried = local_terms(
        queries, key_rows, values, log_forget, input_gate, document_begin_flags
    )
    query_list.append(queries)
    inner_list.append(inner_part)
    state_list.append(local_state)
    passing_list.append(passing)
    carried_list.append(carried)
    incoming = carried_in(passing_list[0], state_list[0])[None]
    attention_slot_number = 0
    head_out = inner_list[attention_slot_number] + apply_state(
        query_list[attention_slot_number],
        carried_list[attention_slot_number],
        incoming[attention_slot_number],
    )
    normed_heads = head_norm(head_out, head_gain)
    summed = scatter_rows(normed_heads, out_rows).astype(jnp.float32)
    return (tokens.astype(jnp.float32) + summed).astype(jnp.bfloat16)


def solution(mesh):
    z_rows = 4 if mesh.shape["ctx"] % 4 == 0 else 1
    split = jax.sharding.Mesh(
        mesh.devices.reshape(mesh.shape["ctx"] // z_rows, z_rows, mesh.shape["tp"]), ("cz", "cy", "tp")
    )
    blocks = ("cz", "cy")
    placed = (
        P(blocks + ("tp",), None),
        P(),
        P(blocks, "tp"),
        P("tp", blocks),
        P("tp"),
        P("tp", blocks),
        P("tp", blocks),
        P("tp"),
        P(blocks),
    )
    return jax.shard_map(
        local, mesh=split, in_specs=placed, out_specs=P(blocks + ("tp",), None), check_vma=False
    )
```

```python
import functools

import jax
import jax.numpy as jnp
from jax import lax
from jax.experimental import pallas as pl
from jax.experimental.pallas import tpu as pltpu
from jax.sharding import PartitionSpec as P

DK = 256
DV = 512


EPSILON = 1e-06
FORGET_STEP = 0.5
INPUT_STEP = 0.5


MESH_ID = pl.DeviceIdType.MESH
DECAY_ROWS = 16


def scan_shifts(count):
    shifts = [1] + ([2] if count > 2 else [])
    k = 2
    while k < count:
        shifts.append(k)
        k *= 2
    return shifts


def pack(ref, total, decay):
    rows = total.shape[0]
    high = decay.astype(jnp.bfloat16)
    ref[:rows, :] = total.astype(jnp.bfloat16)
    ref[rows : rows + DECAY_ROWS, :] = high
    ref[rows + DECAY_ROWS :, :] = (decay - high.astype(jnp.float32)).astype(jnp.bfloat16)


def absorb(got, rows, acc_total, acc_decay):
    far_total = got[:rows].astype(jnp.float32)
    far_decay = got[rows : rows + DECAY_ROWS].astype(jnp.float32) + got[rows + DECAY_ROWS :].astype(jnp.float32)
    decay = acc_decay[...]
    acc_total[...] = decay[0:1, :] * far_total + acc_total[...]
    acc_decay[...] = decay * far_decay


def scan_kernel(
    ny, nz, zshifts, state_ref, decay_ref, out_ref,
    row_send, row_recv, z_send, z_recv, p_send, p_recv,
    acc_total, acc_decay, quarter_total, quarter_decay, z_total, z_decay,
    row_send_sems, row_recv_sems, z_send_sems, z_recv_sems, p_send_sems, p_recv_sems,
):
    yi = lax.axis_index("cy")
    zi = lax.axis_index("cz")
    tp = lax.axis_index("tp")
    rows, width = state_ref.shape
    quarter = width // ny
    mine = pl.ds(pl.multiple_of(yi * quarter, quarter), quarter)

    barrier = pltpu.get_barrier_semaphore()
    z_partners = sorted(set(zshifts))
    for d in range(1, ny):
        pl.semaphore_signal(barrier, 1, device_id=(zi, lax.rem(yi + d, ny), tp), device_id_type=MESH_ID)
    for s in z_partners:
        for peer in (lax.rem(zi + s, nz), lax.rem(zi + nz - s, nz)):
            pl.semaphore_signal(barrier, 1, device_id=(peer, yi, tp), device_id_type=MESH_ID)
    pl.semaphore_wait(barrier, (ny - 1) + 2 * len(z_partners))

    def row_copy(d, target, slot):
        return pltpu.make_async_remote_copy(
            src_ref=row_send, dst_ref=row_recv.at[slot], send_sem=row_send_sems.at[d],
            recv_sem=row_recv_sems.at[slot], device_id=(zi, target, tp), device_id_type=MESH_ID,
        )

    pack(row_send, state_ref[...], decay_ref[...])
    for d in range(1, ny):
        row_copy(d, lax.rem(yi + d, ny), yi).start()
    for d in range(1, ny):
        source = lax.rem(yi + ny - d, ny)
        row_copy(d, yi, source).wait_recv()

    acc_total[...] = jnp.zeros_like(acc_total)
    acc_decay[...] = jnp.ones_like(acc_decay)
    for d in range(1, ny):
        @pl.when(yi - d >= 0)
        def _():
            absorb(row_recv[yi - d], rows, acc_total, acc_decay)

    quarter_total[...] = jnp.zeros_like(quarter_total)
    quarter_decay[...] = jnp.ones_like(quarter_decay)
    for y in reversed(range(ny)):
        @pl.when(yi == y)
        def _():
            absorb(row_send[:, mine], rows, quarter_total, quarter_decay)

        @pl.when(yi != y)
        def _():
            absorb(row_recv[y, :, mine], rows, quarter_total, quarter_decay)

    def z_copy(j, slot, peer):
        return pltpu.make_async_remote_copy(
            src_ref=z_send.at[slot], dst_ref=z_recv.at[j], send_sem=z_send_sems.at[j],
            recv_sem=z_recv_sems.at[j], device_id=(peer, yi, tp), device_id_type=MESH_ID,
        )

    def z_send_round(j, slot):
        @pl.when(zi + zshifts[j] < nz)
        def _():
            z_copy(j, slot, zi + zshifts[j]).start()

    def z_absorb(j, slot):
        @pl.when(zi - zshifts[j] >= 0)
        def _():
            z_copy(j, slot, zi - zshifts[j]).wait_recv()
            absorb(z_recv[j], rows, z_total, z_decay)

    z_total[...] = jnp.zeros_like(z_total)
    z_decay[...] = jnp.ones_like(z_decay)
    first = min(2, len(zshifts))
    if zshifts:
        pack(z_send.at[0], quarter_total[...], quarter_decay[...])
    for j in range(first):
        z_send_round(j, 0)
    for j in range(first):
        z_absorb(j, 0)
    for j in range(first, len(zshifts)):
        pack(z_send.at[j - 1], z_total[...], z_decay[...])
        z_send_round(j, j - 1)
        z_absorb(j, j - 1)

    def p_copy(d, target, slot):
        return pltpu.make_async_remote_copy(
            src_ref=p_send, dst_ref=p_recv.at[slot], send_sem=p_send_sems.at[d],
            recv_sem=p_recv_sems.at[slot], device_id=(zi, target, tp), device_id_type=MESH_ID,
        )

    p_send[...] = z_total[...].astype(jnp.bfloat16)
    for d in range(1, ny):
        p_copy(d, lax.rem(yi + d, ny), yi).start()
    for d in range(1, ny):
        p_copy(d, yi, lax.rem(yi + ny - d, ny)).wait_recv()
    decay = acc_decay[0:1, :]
    for y in range(ny):
        cols = slice(y * quarter, (y + 1) * quarter)

        @pl.when(yi == y)
        def _():
            out_ref[:, cols] = decay[:, cols] * p_send[...].astype(jnp.float32) + acc_total[:, cols]

        @pl.when(yi != y)
        def _():
            out_ref[:, cols] = decay[:, cols] * p_recv[y].astype(jnp.float32) + acc_total[:, cols]

    for d in range(1, ny):
        row_copy(d, lax.rem(yi + d, ny), yi).wait_send()
        p_copy(d, lax.rem(yi + d, ny), yi).wait_send()
    for j in range(len(zshifts)):
        @pl.when(zi + zshifts[j] < nz)
        def _():
            z_copy(j, 0 if j < first else j - 1, zi + zshifts[j]).wait_send()


def ring_steps(n):
    steps = [(s, True) for s in range(1, (n - 1) // 2 + 1)]
    if n % 2 == 0 and n > 1:
        steps.append((n // 2, False))
    return steps


def gather_kernel(ny, nz, nt, piece_ref, rows_ref, out_ref, rows_out, local_sem, send_sems, recv_sems):
    yi = lax.axis_index("cy")
    zi = lax.axis_index("cz")
    tp = lax.axis_index("tp")
    half = piece_ref.shape[1] // 2
    cols = (pl.ds(0, half), pl.ds(half, half))

    barrier = pltpu.get_barrier_semaphore()
    neighbours = [
        (zi, lax.rem(yi + 1, ny), tp),
        (zi, lax.rem(yi + ny - 1, ny), tp),
        (lax.rem(zi + 1, nz), yi, tp),
        (lax.rem(zi + nz - 1, nz), yi, tp),
        (zi, yi, lax.rem(tp + 1, nt)),
        (zi, yi, lax.rem(tp + nt - 1, nt)),
    ]
    for peer in neighbours:
        pl.semaphore_signal(barrier, 1, device_id=peer, device_id_type=MESH_ID)
    pl.semaphore_wait(barrier, len(neighbours))

    own = pltpu.make_async_copy(piece_ref, out_ref.at[zi, yi], local_sem.at[0])
    own.start()
    own_rows = pltpu.make_async_copy(rows_ref, rows_out.at[tp], local_sem.at[1])
    own_rows.start()
    sends = []

    def ring(along, group_of, first_src):
        n, me = {"y": (ny, yi), "z": (nz, zi), "t": (nt, tp)}[along]
        return dict(n=n, me=me, along=along, group_of=group_of, first_src=first_src, steps=ring_steps(n), last={})

    def device(r, k):
        return {"y": (zi, k, tp), "z": (k, yi, tp), "t": (zi, yi, k)}[r["along"]]

    def step(r, t):
        if t > len(r["steps"]):
            return
        n, me, group_of = r["n"], r["me"], r["group_of"]
        hop, both = r["steps"][t - 1]
        for sign in (1, -1) if both else (1,):
            if t > 1:
                r["last"].pop(sign).wait_recv()
            origin = lax.rem(me + n - sign * (hop - 1), n)
            target = lax.rem(me + n + sign, n)
            source = lax.rem(me + n - sign, n)
            arrived = lax.rem(me + 2 * n - sign * hop, n)
            idx = len(sends)
            send = pltpu.make_async_remote_copy(
                src_ref=r["first_src"] if t == 1 else group_of(origin), dst_ref=group_of(origin),
                send_sem=send_sems.at[idx], recv_sem=recv_sems.at[idx],
                device_id=device(r, target), device_id_type=MESH_ID,
            )
            incoming = pltpu.make_async_remote_copy(
                src_ref=group_of(arrived), dst_ref=group_of(arrived),
                send_sem=send_sems.at[idx], recv_sem=recv_sems.at[idx],
                device_id=device(r, source), device_id_type=MESH_ID,
            )
            send.start()
            sends.append(send)
            r["last"][sign] = incoming

    def stage(rings):
        for t in range(1, max(len(r["steps"]) for r in rings) + 1):
            for r in rings:
                step(r, t)
        for r in rings:
            for incoming in r["last"].values():
                incoming.wait_recv()

    stage([
        ring("y", lambda k: out_ref.at[zi, k, :, cols[0]], piece_ref.at[:, cols[0]]),
        ring("z", lambda k: out_ref.at[k, yi, :, cols[1]], piece_ref.at[:, cols[1]]),
    ])
    own.wait()
    stage([
        ring("z", lambda k: out_ref.at[k, :, :, cols[0]], out_ref.at[zi, :, :, cols[0]]),
        ring("y", lambda k: out_ref.at[:, k, :, cols[1]], out_ref.at[:, yi, :, cols[1]]),
        ring("t", lambda k: rows_out.at[k], rows_ref),
    ])
    own_rows.wait()
    for send in sends:
        send.wait_send()


def gather_blocks(piece, rows):
    ny, nz, nt = lax.axis_size("cy"), lax.axis_size("cz"), lax.axis_size("tp")
    height, width = piece.shape
    count = sum(sum(2 if both else 1 for _, both in ring_steps(n)) for n in (ny, nz, nz, ny, nt))
    out, rows_out = pl.pallas_call(
        functools.partial(gather_kernel, ny, nz, nt),
        out_shape=(
            jax.ShapeDtypeStruct((nz, ny, height, width), piece.dtype),
            jax.ShapeDtypeStruct((nt,) + rows.shape, rows.dtype),
        ),
        in_specs=[pl.BlockSpec(memory_space=pltpu.VMEM)] * 2,
        out_specs=(pl.BlockSpec(memory_space=pl.ANY), pl.BlockSpec(memory_space=pl.ANY)),
        scratch_shapes=[
            pltpu.SemaphoreType.DMA((2,)),
            pltpu.SemaphoreType.DMA((count,)),
            pltpu.SemaphoreType.DMA((count,)),
        ],
        compiler_params=pltpu.CompilerParams(collective_id=1, has_side_effects=True),
    )(piece, rows)
    return out.reshape(nz * ny * height, width), rows_out.reshape(nt * rows.shape[0], rows.shape[1])


def scatter_kernel(nt, heads_ref, weight_ref, out_ref, send_buf, recv_buf, send_sems, recv_sems):
    tp = lax.axis_index("tp")
    rows = out_ref.shape[0]
    half = out_ref.shape[1] // 2

    barrier = pltpu.get_barrier_semaphore()
    for peer in (lax.rem(tp + 1, nt), lax.rem(tp + nt - 1, nt)):
        pl.semaphore_signal(barrier, 1, device_id=(lax.axis_index("cz"), lax.axis_index("cy"), peer), device_id_type=MESH_ID)

    def own(chunk, side):
        start = pl.multiple_of(chunk * rows, 16)
        part = lax.dot_general(
            heads_ref[pl.ds(start, rows), :],
            weight_ref[side * half : (side + 1) * half, :],
            (((1,), (1,)), ((), ())),
            preferred_element_type=jnp.float32,
        )
        return part.astype(jnp.bfloat16).astype(jnp.float32)

    def copy(side, step, peer):
        slot = side * nt + step
        return pltpu.make_async_remote_copy(
            src_ref=send_buf.at[slot], dst_ref=recv_buf.at[slot], send_sem=send_sems.at[slot],
            recv_sem=recv_sems.at[slot],
            device_id=(lax.axis_index("cz"), lax.axis_index("cy"), peer), device_id_type=MESH_ID,
        )

    sides = ((0, 1), (1, -1))
    first = [own(lax.rem(tp + nt * nt - sign, nt), side) for side, sign in sides]
    pl.semaphore_wait(barrier, 2)
    for step in range(1, nt):
        for side, sign in sides:
            chunk = lax.rem(tp + nt * nt - sign * step, nt)
            total = first[side] if step == 1 else own(chunk, side)
            if step > 1:
                copy(side, step - 1, lax.rem(tp + nt - sign, nt)).wait_recv()
                total = total + recv_buf[side * nt + step - 1].astype(jnp.float32)
            send_buf[side * nt + step] = total.astype(jnp.bfloat16)
            copy(side, step, lax.rem(tp + nt + sign, nt)).start()
    last = [own(tp, side) for side, _ in sides]
    for side, sign in sides:
        copy(side, nt - 1, lax.rem(tp + nt - sign, nt)).wait_recv()
        total = last[side] + recv_buf[side * nt + nt - 1].astype(jnp.float32)
        out_ref[:, side * half : (side + 1) * half] = total.astype(out_ref.dtype)
    for step in range(1, nt):
        for side, sign in sides:
            copy(side, step, lax.rem(tp + nt + sign, nt)).wait_send()


def scatter_rows(heads, weight):
    nt = lax.axis_size("tp")
    rows = heads.shape[0] // nt
    width = weight.shape[0]
    return pl.pallas_call(
        functools.partial(scatter_kernel, nt),
        out_shape=jax.ShapeDtypeStruct((rows, width), jnp.bfloat16),
        in_specs=[pl.BlockSpec(memory_space=pltpu.VMEM)] * 2,
        out_specs=pl.BlockSpec(memory_space=pltpu.VMEM),
        scratch_shapes=[
            pltpu.VMEM((2 * nt, rows, width // 2), jnp.bfloat16),
            pltpu.VMEM((2 * nt, rows, width // 2), jnp.bfloat16),
            pltpu.SemaphoreType.DMA((2 * nt,)),
            pltpu.SemaphoreType.DMA((2 * nt,)),
        ],
        compiler_params=pltpu.CompilerParams(
            collective_id=2, has_side_effects=True, vmem_limit_bytes=48 * 1024 * 1024
        ),
    )(heads, weight)


def carried_in(passing, state):
    ny, nz = lax.axis_size("cy"), lax.axis_size("cz")
    if ny * nz == 1:
        return jnp.zeros_like(state)
    zshifts = scan_shifts(nz) if nz > 1 else []
    rows, width = state.shape
    quarter = width // ny
    decay = jnp.broadcast_to(passing.reshape(1, 1), (DECAY_ROWS, width)).astype(jnp.float32)
    message = rows + 2 * DECAY_ROWS
    slots = max(len(zshifts), 1)
    return pl.pallas_call(
        functools.partial(scan_kernel, ny, nz, zshifts),
        out_shape=jax.ShapeDtypeStruct((rows, width), jnp.float32),
        in_specs=[pl.BlockSpec(memory_space=pltpu.VMEM)] * 2,
        out_specs=pl.BlockSpec(memory_space=pltpu.VMEM),
        scratch_shapes=[
            pltpu.VMEM((message, width), jnp.bfloat16),
            pltpu.VMEM((ny, message, width), jnp.bfloat16),
            pltpu.VMEM((slots, message, quarter), jnp.bfloat16),
            pltpu.VMEM((slots, message, quarter), jnp.bfloat16),
            pltpu.VMEM((rows, quarter), jnp.bfloat16),
            pltpu.VMEM((ny, rows, quarter), jnp.bfloat16),
            pltpu.VMEM((rows, width), jnp.float32),
            pltpu.VMEM((DECAY_ROWS, width), jnp.float32),
            pltpu.VMEM((rows, quarter), jnp.float32),
            pltpu.VMEM((DECAY_ROWS, quarter), jnp.float32),
            pltpu.VMEM((rows, quarter), jnp.float32),
            pltpu.VMEM((DECAY_ROWS, quarter), jnp.float32),
            pltpu.SemaphoreType.DMA((ny,)),
            pltpu.SemaphoreType.DMA((ny,)),
            pltpu.SemaphoreType.DMA((slots,)),
            pltpu.SemaphoreType.DMA((slots,)),
            pltpu.SemaphoreType.DMA((ny,)),
            pltpu.SemaphoreType.DMA((ny,)),
        ],
        compiler_params=pltpu.CompilerParams(collective_id=0, has_side_effects=True),
    )(state.astype(jnp.float32), decay)


def rms_rows(embedded_entries, norm_gain):
    token_float = embedded_entries.astype(jnp.float32)
    moment = jnp.mean(token_float * token_float, axis=1, keepdims=True)
    return (token_float * lax.rsqrt(moment + EPSILON) * norm_gain).astype(jnp.bfloat16)


def local_terms(queries, key_rows, values, log_forget, input_gate, starts):
    length = queries.shape[0]
    scaling = queries.shape[1] ** (-0.5)
    segment = jnp.cumsum(starts)
    levels = jnp.cumsum(log_forget)
    position = jnp.arange(length)
    allowed = (position[:, None] >= position[None, :]) & (segment[:, None] == segment[None, :])
    decays = jnp.where(
        allowed,
        jnp.exp(jnp.minimum(levels[:, None] - levels[None, :], 0.0) + input_gate[None, :]),
        0.0,
    )
    scores = jnp.dot(queries, key_rows.T, preferred_element_type=jnp.float32) * scaling
    weights = (scores * decays).astype(jnp.bfloat16)
    inner_part = jnp.dot(weights, values, preferred_element_type=jnp.float32)
    last_level = levels[-1]
    last_seg = segment[-1]
    keeping = jnp.where(segment == last_seg, jnp.exp(last_level - levels + input_gate), 0.0)
    weighted = (key_rows.astype(jnp.float32) * keeping[:, None]).astype(jnp.bfloat16)
    local_state = lax.dot_general(
        weighted, values, (((0,), (0,)), ((), ())), preferred_element_type=jnp.float32
    )
    passing = jnp.where(last_seg == 0, jnp.exp(last_level), 0.0)
    carried = jnp.where(segment == 0, jnp.exp(levels), 0.0) * scaling
    return (inner_part, local_state, passing, carried)


def apply_state(queries, carried, incoming):
    lifted = queries.astype(jnp.float32) * carried[:, None]
    return jnp.dot(
        lifted, incoming, precision=lax.Precision.HIGHEST, preferred_element_type=jnp.float32
    )


def head_norm(head_out, gain):
    centre = jnp.mean(head_out, axis=1, keepdims=True)
    shifted = head_out - centre
    spread = jnp.mean(shifted * shifted, axis=1, keepdims=True)
    return (shifted * lax.rsqrt(spread + EPSILON) * gain).astype(jnp.bfloat16)


def local(
    tokens,
    norm_gain,
    w_qkv,
    w_out,
    head_gain,
    input_codes,
    forget_codes,
    forget_bias,
    document_begin_flags,
):
    normed = rms_rows(tokens, norm_gain)
    width = w_qkv.shape[1]
    both, every_row_list = gather_blocks(jnp.concatenate([w_qkv, w_out.T], axis=1), normed)
    parameter_collection = both[:, :width]
    out_rows = both[:, width:]
    rows_combined = jnp.dot(
        every_row_list, parameter_collection, preferred_element_type=jnp.float32
    )
    rows_combined = rows_combined.astype(jnp.bfloat16)
    heads_here = forget_bias.shape[0]
    stride = 2 * DK + DV
    query_list, inner_list, state_list, passing_list, carried_list = ([], [], [], [], [])
    attention_slot_number = 0
    offset = attention_slot_number * stride
    queries = rows_combined[:, offset : offset + DK]
    key_rows = rows_combined[:, offset + DK : offset + 2 * DK]
    values = rows_combined[:, offset + 2 * DK : offset + stride]
    log_forget = jax.nn.log_sigmoid(
        FORGET_STEP * forget_codes[attention_slot_number].astype(jnp.float32)
        + forget_bias[attention_slot_number]
    )
    input_gate = INPUT_STEP * input_codes[attention_slot_number].astype(jnp.float32)
    inner_part, local_state, passing, carried = local_terms(
        queries, key_rows, values, log_forget, input_gate, document_begin_flags
    )
    query_list.append(queries)
    inner_list.append(inner_part)
    state_list.append(local_state)
    passing_list.append(passing)
    carried_list.append(carried)
    incoming = carried_in(passing_list[0], state_list[0])[None]
    attention_slot_number = 0
    head_out = inner_list[attention_slot_number] + apply_state(
        query_list[attention_slot_number],
        carried_list[attention_slot_number],
        incoming[attention_slot_number],
    )
    normed_heads = head_norm(head_out, head_gain)
    summed = scatter_rows(normed_heads, out_rows).astype(jnp.float32)
    return (tokens.astype(jnp.float32) + summed).astype(jnp.bfloat16)


def solution(mesh):
    z_rows = 4 if mesh.shape["ctx"] % 4 == 0 else 1
    split = jax.sharding.Mesh(
        mesh.devices.reshape(mesh.shape["ctx"] // z_rows, z_rows, mesh.shape["tp"]), ("cz", "cy", "tp")
    )
    blocks = ("cz", "cy")
    placed = (
        P(blocks + ("tp",), None),
        P(),
        P(blocks, "tp"),
        P("tp", blocks),
        P("tp"),
        P("tp", blocks),
        P("tp", blocks),
        P("tp"),
        P(blocks),
    )
    return jax.shard_map(
        local, mesh=split, in_specs=placed, out_specs=P(blocks + ("tp",), None), check_vma=False
    )
```

```python
import functools

import jax
import jax.numpy as jnp
from jax import lax
from jax.experimental import pallas as pl
from jax.experimental.pallas import tpu as pltpu
from jax.sharding import PartitionSpec as P

DK = 256
DV = 512


EPSILON = 1e-06
FORGET_STEP = 0.5
INPUT_STEP = 0.5


MESH_ID = pl.DeviceIdType.MESH
DECAY_ROWS = 16


def scan_shifts(count):
    shifts = [1] + ([2] if count > 2 else [])
    k = 2
    while k < count:
        shifts.append(k)
        k *= 2
    return shifts


def pack(ref, total, decay):
    rows = total.shape[0]
    high = decay.astype(jnp.bfloat16)
    ref[:rows, :] = total.astype(jnp.bfloat16)
    ref[rows : rows + DECAY_ROWS, :] = high
    ref[rows + DECAY_ROWS :, :] = (decay - high.astype(jnp.float32)).astype(jnp.bfloat16)


def absorb(got, rows, acc_total, acc_decay):
    far_total = got[:rows].astype(jnp.float32)
    far_decay = got[rows : rows + DECAY_ROWS].astype(jnp.float32) + got[rows + DECAY_ROWS :].astype(jnp.float32)
    decay = acc_decay[...]
    acc_total[...] = decay[0:1, :] * far_total + acc_total[...]
    acc_decay[...] = decay * far_decay


def extend(got, rows, acc_total, acc_decay):
    far_total = got[:rows].astype(jnp.float32)
    far_decay = got[rows : rows + DECAY_ROWS].astype(jnp.float32) + got[rows + DECAY_ROWS :].astype(jnp.float32)
    acc_total[...] = far_decay[0:1, :] * acc_total[...] + far_total
    acc_decay[...] = far_decay * acc_decay[...]


def scan_kernel(
    ny, nz, zshifts, state_ref, decay_ref, out_ref,
    row_send, row_recv, z_send, z_recv, c_send, c_recv,
    prefix_total, prefix_decay, quarter_total, quarter_decay, z_total, z_decay,
    row_send_sems, row_recv_sems, z_send_sems, z_recv_sems, c_send_sems, c_recv_sems,
):
    yi = lax.axis_index("cy")
    zi = lax.axis_index("cz")
    tp = lax.axis_index("tp")
    rows, width = state_ref.shape
    quarter = width // ny

    barrier = pltpu.get_barrier_semaphore()
    z_partners = sorted(set(zshifts))
    for d in range(1, ny):
        pl.semaphore_signal(barrier, 1, device_id=(zi, lax.rem(yi + d, ny), tp), device_id_type=MESH_ID)
    for s in z_partners:
        for peer in (lax.rem(zi + s, nz), lax.rem(zi + nz - s, nz)):
            pl.semaphore_signal(barrier, 1, device_id=(peer, yi, tp), device_id_type=MESH_ID)
    pl.semaphore_wait(barrier, (ny - 1) + 2 * len(z_partners))

    def row_copy(d, target, slot, part):
        return pltpu.make_async_remote_copy(
            src_ref=row_send.at[part], dst_ref=row_recv.at[slot], send_sem=row_send_sems.at[d],
            recv_sem=row_recv_sems.at[slot], device_id=(zi, target, tp), device_id_type=MESH_ID,
        )

    for y in range(ny):
        pack(row_send.at[y], state_ref[:, y * quarter : (y + 1) * quarter], decay_ref[:, y * quarter : (y + 1) * quarter])
    for d in range(1, ny):
        target = lax.rem(yi + d, ny)
        row_copy(d, target, yi, target).start()
    for d in range(1, ny):
        row_copy(d, yi, lax.rem(yi + ny - d, ny), yi).wait_recv()

    quarter_total[...] = jnp.zeros_like(quarter_total)
    quarter_decay[...] = jnp.ones_like(quarter_decay)
    for y in range(ny):
        prefix_total[y] = quarter_total[...]
        prefix_decay[y] = quarter_decay[...]

        @pl.when(yi == y)
        def _():
            extend(row_send[y], rows, quarter_total, quarter_decay)

        @pl.when(yi != y)
        def _():
            extend(row_recv[y], rows, quarter_total, quarter_decay)

    def z_copy(j, slot, peer):
        return pltpu.make_async_remote_copy(
            src_ref=z_send.at[slot], dst_ref=z_recv.at[j], send_sem=z_send_sems.at[j],
            recv_sem=z_recv_sems.at[j], device_id=(peer, yi, tp), device_id_type=MESH_ID,
        )

    def z_send_round(j, slot):
        @pl.when(zi + zshifts[j] < nz)
        def _():
            z_copy(j, slot, zi + zshifts[j]).start()

    def z_absorb(j, slot):
        @pl.when(zi - zshifts[j] >= 0)
        def _():
            z_copy(j, slot, zi - zshifts[j]).wait_recv()
            absorb(z_recv[j], rows, z_total, z_decay)

    z_total[...] = jnp.zeros_like(z_total)
    z_decay[...] = jnp.ones_like(z_decay)
    first = min(2, len(zshifts))
    if zshifts:
        pack(z_send.at[0], quarter_total[...], quarter_decay[...])
    for j in range(first):
        z_send_round(j, 0)
    for j in range(first):
        z_absorb(j, 0)
    for j in range(first, len(zshifts)):
        pack(z_send.at[j - 1], z_total[...], z_decay[...])
        z_send_round(j, j - 1)
        z_absorb(j, j - 1)

    def c_copy(y, target, slot):
        return pltpu.make_async_remote_copy(
            src_ref=c_send.at[y], dst_ref=c_recv.at[slot], send_sem=c_send_sems.at[y],
            recv_sem=c_recv_sems.at[slot], device_id=(zi, target, tp), device_id_type=MESH_ID,
        )

    for y in range(ny):
        done = prefix_decay[y][0:1, :] * z_total[...] + prefix_total[y]

        @pl.when(yi == y)
        def _():
            out_ref[:, y * quarter : (y + 1) * quarter] = done

        @pl.when(yi != y)
        def _():
            c_send[y] = done.astype(jnp.bfloat16)
            c_copy(y, y, yi).start()

    for y in range(ny):
        @pl.when(yi != y)
        def _():
            c_copy(y, yi, y).wait_recv()
            out_ref[:, y * quarter : (y + 1) * quarter] = c_recv[y].astype(jnp.float32)

    for d in range(1, ny):
        target = lax.rem(yi + d, ny)
        row_copy(d, target, yi, target).wait_send()
    for y in range(ny):
        @pl.when(yi != y)
        def _():
            c_copy(y, y, yi).wait_send()
    for j in range(len(zshifts)):
        @pl.when(zi + zshifts[j] < nz)
        def _():
            z_copy(j, 0 if j < first else j - 1, zi + zshifts[j]).wait_send()


def carried_in(passing, state):
    ny, nz = lax.axis_size("cy"), lax.axis_size("cz")
    if ny * nz == 1:
        return jnp.zeros_like(state)
    zshifts = scan_shifts(nz) if nz > 1 else []
    rows, width = state.shape
    quarter = width // ny
    decay = jnp.broadcast_to(passing.reshape(1, 1), (DECAY_ROWS, width)).astype(jnp.float32)
    message = rows + 2 * DECAY_ROWS
    slots = max(len(zshifts), 1)
    return pl.pallas_call(
        functools.partial(scan_kernel, ny, nz, zshifts),
        out_shape=jax.ShapeDtypeStruct((rows, width), jnp.float32),
        in_specs=[pl.BlockSpec(memory_space=pltpu.VMEM)] * 2,
        out_specs=pl.BlockSpec(memory_space=pltpu.VMEM),
        scratch_shapes=[
            pltpu.VMEM((ny, message, quarter), jnp.bfloat16),
            pltpu.VMEM((ny, message, quarter), jnp.bfloat16),
            pltpu.VMEM((slots, message, quarter), jnp.bfloat16),
            pltpu.VMEM((slots, message, quarter), jnp.bfloat16),
            pltpu.VMEM((ny, rows, quarter), jnp.bfloat16),
            pltpu.VMEM((ny, rows, quarter), jnp.bfloat16),
            pltpu.VMEM((ny, rows, quarter), jnp.float32),
            pltpu.VMEM((ny, DECAY_ROWS, quarter), jnp.float32),
            pltpu.VMEM((rows, quarter), jnp.float32),
            pltpu.VMEM((DECAY_ROWS, quarter), jnp.float32),
            pltpu.VMEM((rows, quarter), jnp.float32),
            pltpu.VMEM((DECAY_ROWS, quarter), jnp.float32),
            pltpu.SemaphoreType.DMA((ny,)),
            pltpu.SemaphoreType.DMA((ny,)),
            pltpu.SemaphoreType.DMA((slots,)),
            pltpu.SemaphoreType.DMA((slots,)),
            pltpu.SemaphoreType.DMA((ny,)),
            pltpu.SemaphoreType.DMA((ny,)),
        ],
        compiler_params=pltpu.CompilerParams(collective_id=0, has_side_effects=True),
    )(state.astype(jnp.float32), decay)


def ring_steps(n):
    steps = [(s, True) for s in range(1, (n - 1) // 2 + 1)]
    if n % 2 == 0 and n > 1:
        steps.append((n // 2, False))
    return steps


def gather_kernel(ny, nz, nt, piece_ref, rows_ref, out_ref, rows_out, local_sem, send_sems, recv_sems):
    yi = lax.axis_index("cy")
    zi = lax.axis_index("cz")
    tp = lax.axis_index("tp")
    half = piece_ref.shape[1] // 2
    cols = (pl.ds(0, half), pl.ds(half, half))

    barrier = pltpu.get_barrier_semaphore()
    neighbours = [
        (zi, lax.rem(yi + 1, ny), tp),
        (zi, lax.rem(yi + ny - 1, ny), tp),
        (lax.rem(zi + 1, nz), yi, tp),
        (lax.rem(zi + nz - 1, nz), yi, tp),
        (zi, yi, lax.rem(tp + 1, nt)),
        (zi, yi, lax.rem(tp + nt - 1, nt)),
    ]
    for peer in neighbours:
        pl.semaphore_signal(barrier, 1, device_id=peer, device_id_type=MESH_ID)
    pl.semaphore_wait(barrier, len(neighbours))

    own = pltpu.make_async_copy(piece_ref, out_ref.at[zi, yi], local_sem.at[0])
    own.start()
    own_rows = pltpu.make_async_copy(rows_ref, rows_out.at[tp], local_sem.at[1])
    own_rows.start()
    sends = []

    def ring(along, group_of, first_src):
        n, me = {"y": (ny, yi), "z": (nz, zi), "t": (nt, tp)}[along]
        return dict(n=n, me=me, along=along, group_of=group_of, first_src=first_src, steps=ring_steps(n), last={})

    def device(r, k):
        return {"y": (zi, k, tp), "z": (k, yi, tp), "t": (zi, yi, k)}[r["along"]]

    def step(r, t):
        if t > len(r["steps"]):
            return
        n, me, group_of = r["n"], r["me"], r["group_of"]
        hop, both = r["steps"][t - 1]
        for sign in (1, -1) if both else (1,):
            if t > 1:
                r["last"].pop(sign).wait_recv()
            origin = lax.rem(me + n - sign * (hop - 1), n)
            target = lax.rem(me + n + sign, n)
            source = lax.rem(me + n - sign, n)
            arrived = lax.rem(me + 2 * n - sign * hop, n)
            idx = len(sends)
            send = pltpu.make_async_remote_copy(
                src_ref=r["first_src"] if t == 1 else group_of(origin), dst_ref=group_of(origin),
                send_sem=send_sems.at[idx], recv_sem=recv_sems.at[idx],
                device_id=device(r, target), device_id_type=MESH_ID,
            )
            incoming = pltpu.make_async_remote_copy(
                src_ref=group_of(arrived), dst_ref=group_of(arrived),
                send_sem=send_sems.at[idx], recv_sem=recv_sems.at[idx],
                device_id=device(r, source), device_id_type=MESH_ID,
            )
            send.start()
            sends.append(send)
            r["last"][sign] = incoming

    def stage(rings):
        for t in range(1, max(len(r["steps"]) for r in rings) + 1):
            for r in rings:
                step(r, t)
        for r in rings:
            for incoming in r["last"].values():
                incoming.wait_recv()

    stage([
        ring("y", lambda k: out_ref.at[zi, k, :, cols[0]], piece_ref.at[:, cols[0]]),
        ring("z", lambda k: out_ref.at[k, yi, :, cols[1]], piece_ref.at[:, cols[1]]),
    ])
    own.wait()
    stage([
        ring("z", lambda k: out_ref.at[k, :, :, cols[0]], out_ref.at[zi, :, :, cols[0]]),
        ring("y", lambda k: out_ref.at[:, k, :, cols[1]], out_ref.at[:, yi, :, cols[1]]),
        ring("t", lambda k: rows_out.at[k], rows_ref),
    ])
    own_rows.wait()
    for send in sends:
        send.wait_send()


def gather_blocks(piece, rows):
    ny, nz, nt = lax.axis_size("cy"), lax.axis_size("cz"), lax.axis_size("tp")
    height, width = piece.shape
    count = sum(sum(2 if both else 1 for _, both in ring_steps(n)) for n in (ny, nz, nz, ny, nt))
    out, rows_out = pl.pallas_call(
        functools.partial(gather_kernel, ny, nz, nt),
        out_shape=(
            jax.ShapeDtypeStruct((nz, ny, height, width), piece.dtype),
            jax.ShapeDtypeStruct((nt,) + rows.shape, rows.dtype),
        ),
        in_specs=[pl.BlockSpec(memory_space=pltpu.VMEM)] * 2,
        out_specs=(pl.BlockSpec(memory_space=pl.ANY), pl.BlockSpec(memory_space=pl.ANY)),
        scratch_shapes=[
            pltpu.SemaphoreType.DMA((2,)),
            pltpu.SemaphoreType.DMA((count,)),
            pltpu.SemaphoreType.DMA((count,)),
        ],
        compiler_params=pltpu.CompilerParams(collective_id=1, has_side_effects=True),
    )(piece, rows)
    return out.reshape(nz * ny * height, width), rows_out.reshape(nt * rows.shape[0], rows.shape[1])


def scatter_kernel(nt, heads_ref, weight_ref, out_ref, send_buf, recv_buf, send_sems, recv_sems):
    tp = lax.axis_index("tp")
    rows = out_ref.shape[0]
    half = out_ref.shape[1] // 2

    barrier = pltpu.get_barrier_semaphore()
    for peer in (lax.rem(tp + 1, nt), lax.rem(tp + nt - 1, nt)):
        pl.semaphore_signal(barrier, 1, device_id=(lax.axis_index("cz"), lax.axis_index("cy"), peer), device_id_type=MESH_ID)

    def own(chunk, side):
        start = pl.multiple_of(chunk * rows, 16)
        part = lax.dot_general(
            heads_ref[pl.ds(start, rows), :],
            weight_ref[side * half : (side + 1) * half, :],
            (((1,), (1,)), ((), ())),
            preferred_element_type=jnp.float32,
        )
        return part.astype(jnp.bfloat16).astype(jnp.float32)

    def copy(side, step, peer):
        slot = side * nt + step
        return pltpu.make_async_remote_copy(
            src_ref=send_buf.at[slot], dst_ref=recv_buf.at[slot], send_sem=send_sems.at[slot],
            recv_sem=recv_sems.at[slot],
            device_id=(lax.axis_index("cz"), lax.axis_index("cy"), peer), device_id_type=MESH_ID,
        )

    sides = ((0, 1), (1, -1))
    first = [own(lax.rem(tp + nt * nt - sign, nt), side) for side, sign in sides]
    pl.semaphore_wait(barrier, 2)
    for step in range(1, nt):
        for side, sign in sides:
            chunk = lax.rem(tp + nt * nt - sign * step, nt)
            total = first[side] if step == 1 else own(chunk, side)
            if step > 1:
                copy(side, step - 1, lax.rem(tp + nt - sign, nt)).wait_recv()
                total = total + recv_buf[side * nt + step - 1].astype(jnp.float32)
            send_buf[side * nt + step] = total.astype(jnp.bfloat16)
            copy(side, step, lax.rem(tp + nt + sign, nt)).start()
    last = [own(tp, side) for side, _ in sides]
    for side, sign in sides:
        copy(side, nt - 1, lax.rem(tp + nt - sign, nt)).wait_recv()
        total = last[side] + recv_buf[side * nt + nt - 1].astype(jnp.float32)
        out_ref[:, side * half : (side + 1) * half] = total.astype(out_ref.dtype)
    for step in range(1, nt):
        for side, sign in sides:
            copy(side, step, lax.rem(tp + nt + sign, nt)).wait_send()


def scatter_rows(heads, weight):
    nt = lax.axis_size("tp")
    rows = heads.shape[0] // nt
    width = weight.shape[0]
    return pl.pallas_call(
        functools.partial(scatter_kernel, nt),
        out_shape=jax.ShapeDtypeStruct((rows, width), jnp.bfloat16),
        in_specs=[pl.BlockSpec(memory_space=pltpu.VMEM)] * 2,
        out_specs=pl.BlockSpec(memory_space=pltpu.VMEM),
        scratch_shapes=[
            pltpu.VMEM((2 * nt, rows, width // 2), jnp.bfloat16),
            pltpu.VMEM((2 * nt, rows, width // 2), jnp.bfloat16),
            pltpu.SemaphoreType.DMA((2 * nt,)),
            pltpu.SemaphoreType.DMA((2 * nt,)),
        ],
        compiler_params=pltpu.CompilerParams(
            collective_id=2, has_side_effects=True, vmem_limit_bytes=48 * 1024 * 1024
        ),
    )(heads, weight)


def rms_rows(embedded_entries, norm_gain):
    token_float = embedded_entries.astype(jnp.float32)
    moment = jnp.mean(token_float * token_float, axis=1, keepdims=True)
    return (token_float * lax.rsqrt(moment + EPSILON) * norm_gain).astype(jnp.bfloat16)


def local_terms(queries, key_rows, values, log_forget, input_gate, starts):
    length = queries.shape[0]
    scaling = queries.shape[1] ** (-0.5)
    segment = jnp.cumsum(starts)
    levels = jnp.cumsum(log_forget)
    position = jnp.arange(length)
    allowed = (position[:, None] >= position[None, :]) & (segment[:, None] == segment[None, :])
    decays = jnp.where(
        allowed,
        jnp.exp(jnp.minimum(levels[:, None] - levels[None, :], 0.0) + input_gate[None, :]),
        0.0,
    )
    scores = jnp.dot(queries, key_rows.T, preferred_element_type=jnp.float32) * scaling
    weights = (scores * decays).astype(jnp.bfloat16)
    inner_part = jnp.dot(weights, values, preferred_element_type=jnp.float32)
    last_level = levels[-1]
    last_seg = segment[-1]
    keeping = jnp.where(segment == last_seg, jnp.exp(last_level - levels + input_gate), 0.0)
    weighted = (key_rows.astype(jnp.float32) * keeping[:, None]).astype(jnp.bfloat16)
    local_state = lax.dot_general(
        weighted, values, (((0,), (0,)), ((), ())), preferred_element_type=jnp.float32
    )
    passing = jnp.where(last_seg == 0, jnp.exp(last_level), 0.0)
    carried = jnp.where(segment == 0, jnp.exp(levels), 0.0) * scaling
    return (inner_part, local_state, passing, carried)


def apply_state(queries, carried, incoming):
    lifted = queries.astype(jnp.float32) * carried[:, None]
    return jnp.dot(
        lifted, incoming, precision=lax.Precision.HIGHEST, preferred_element_type=jnp.float32
    )


def head_norm(head_out, gain):
    centre = jnp.mean(head_out, axis=1, keepdims=True)
    shifted = head_out - centre
    spread = jnp.mean(shifted * shifted, axis=1, keepdims=True)
    return (shifted * lax.rsqrt(spread + EPSILON) * gain).astype(jnp.bfloat16)


def local(
    tokens,
    norm_gain,
    w_qkv,
    w_out,
    head_gain,
    input_codes,
    forget_codes,
    forget_bias,
    document_begin_flags,
):
    normed = rms_rows(tokens, norm_gain)
    width = w_qkv.shape[1]
    both, every_row_list = gather_blocks(jnp.concatenate([w_qkv, w_out.T], axis=1), normed)
    parameter_collection = both[:, :width]
    out_rows = both[:, width:]
    rows_combined = jnp.dot(
        every_row_list, parameter_collection, preferred_element_type=jnp.float32
    )
    rows_combined = rows_combined.astype(jnp.bfloat16)
    heads_here = forget_bias.shape[0]
    stride = 2 * DK + DV
    query_list, inner_list, state_list, passing_list, carried_list = ([], [], [], [], [])
    attention_slot_number = 0
    offset = attention_slot_number * stride
    queries = rows_combined[:, offset : offset + DK]
    key_rows = rows_combined[:, offset + DK : offset + 2 * DK]
    values = rows_combined[:, offset + 2 * DK : offset + stride]
    log_forget = jax.nn.log_sigmoid(
        FORGET_STEP * forget_codes[attention_slot_number].astype(jnp.float32)
        + forget_bias[attention_slot_number]
    )
    input_gate = INPUT_STEP * input_codes[attention_slot_number].astype(jnp.float32)
    inner_part, local_state, passing, carried = local_terms(
        queries, key_rows, values, log_forget, input_gate, document_begin_flags
    )
    query_list.append(queries)
    inner_list.append(inner_part)
    state_list.append(local_state)
    passing_list.append(passing)
    carried_list.append(carried)
    incoming = carried_in(passing_list[0], state_list[0])[None]
    attention_slot_number = 0
    head_out = inner_list[attention_slot_number] + apply_state(
        query_list[attention_slot_number],
        carried_list[attention_slot_number],
        incoming[attention_slot_number],
    )
    normed_heads = head_norm(head_out, head_gain)
    summed = scatter_rows(normed_heads, out_rows).astype(jnp.float32)
    return (tokens.astype(jnp.float32) + summed).astype(jnp.bfloat16)


def solution(mesh):
    z_rows = 4 if mesh.shape["ctx"] % 4 == 0 else 1
    split = jax.sharding.Mesh(
        mesh.devices.reshape(mesh.shape["ctx"] // z_rows, z_rows, mesh.shape["tp"]), ("cz", "cy", "tp")
    )
    blocks = ("cz", "cy")
    placed = (
        P(blocks + ("tp",), None),
        P(),
        P(blocks, "tp"),
        P("tp", blocks),
        P("tp"),
        P("tp", blocks),
        P("tp", blocks),
        P("tp"),
        P(blocks),
    )
    return jax.shard_map(
        local, mesh=split, in_specs=placed, out_specs=P(blocks + ("tp",), None), check_vma=False
    )
```

```python
import functools

import jax
import jax.numpy as jnp
from jax import lax
from jax.experimental import pallas as pl
from jax.experimental.pallas import tpu as pltpu
from jax.sharding import PartitionSpec as P

DK = 256
DV = 512


EPSILON = 1e-06
FORGET_STEP = 0.5
INPUT_STEP = 0.5


MESH_ID = pl.DeviceIdType.MESH
DECAY_ROWS = 16


def scan_shifts(count):
    shifts = [1] + ([2] if count > 2 else [])
    k = 2
    while k < count:
        shifts.append(k)
        k *= 2
    return shifts


def pack(ref, total, decay):
    rows = total.shape[0]
    high = decay.astype(jnp.bfloat16)
    ref[:rows, :] = total.astype(jnp.bfloat16)
    ref[rows : rows + DECAY_ROWS, :] = high
    ref[rows + DECAY_ROWS :, :] = (decay - high.astype(jnp.float32)).astype(jnp.bfloat16)


def absorb(got, rows, acc_total, acc_decay):
    far_total = got[:rows].astype(jnp.float32)
    far_decay = got[rows : rows + DECAY_ROWS].astype(jnp.float32) + got[rows + DECAY_ROWS :].astype(jnp.float32)
    decay = acc_decay[...]
    acc_total[...] = decay[0:1, :] * far_total + acc_total[...]
    acc_decay[...] = decay * far_decay


def extend(got, rows, acc_total, acc_decay):
    far_total = got[:rows].astype(jnp.float32)
    far_decay = got[rows : rows + DECAY_ROWS].astype(jnp.float32) + got[rows + DECAY_ROWS :].astype(jnp.float32)
    acc_total[...] = far_decay[0:1, :] * acc_total[...] + far_total
    acc_decay[...] = far_decay * acc_decay[...]


def scan_kernel(
    ny, nz, zshifts, state_ref, decay_ref, out_ref,
    row_send, row_recv, z_send, z_recv, c_send, c_recv,
    prefix_total, prefix_decay, quarter_total, quarter_decay, z_total, z_decay,
    row_send_sems, row_recv_sems, z_send_sems, z_recv_sems, c_send_sems, c_recv_sems,
):
    yi = lax.axis_index("cy")
    zi = lax.axis_index("cz")
    tp = lax.axis_index("tp")
    rows, width = state_ref.shape
    quarter = width // ny

    barrier = pltpu.get_barrier_semaphore()
    z_partners = sorted(set(zshifts))
    for d in range(1, ny):
        pl.semaphore_signal(barrier, 1, device_id=(zi, lax.rem(yi + d, ny), tp), device_id_type=MESH_ID)
    for s in z_partners:
        for peer in (lax.rem(zi + s, nz), lax.rem(zi + nz - s, nz)):
            pl.semaphore_signal(barrier, 1, device_id=(peer, yi, tp), device_id_type=MESH_ID)
    pl.semaphore_wait(barrier, (ny - 1) + 2 * len(z_partners))

    def row_copy(d, target, slot, part):
        return pltpu.make_async_remote_copy(
            src_ref=row_send.at[part], dst_ref=row_recv.at[slot], send_sem=row_send_sems.at[d],
            recv_sem=row_recv_sems.at[slot], device_id=(zi, target, tp), device_id_type=MESH_ID,
        )

    for y in range(ny):
        pack(row_send.at[y], state_ref[:, y * quarter : (y + 1) * quarter], decay_ref[:, y * quarter : (y + 1) * quarter])
    for d in range(1, ny):
        target = lax.rem(yi + d, ny)
        row_copy(d, target, yi, target).start()
    for d in range(1, ny):
        row_copy(d, yi, lax.rem(yi + ny - d, ny), yi).wait_recv()

    quarter_total[...] = jnp.zeros_like(quarter_total)
    quarter_decay[...] = jnp.ones_like(quarter_decay)
    for y in range(ny):
        prefix_total[y] = quarter_total[...]
        prefix_decay[y] = quarter_decay[...]

        @pl.when(yi == y)
        def _():
            extend(row_send[y], rows, quarter_total, quarter_decay)

        @pl.when(yi != y)
        def _():
            extend(row_recv[y], rows, quarter_total, quarter_decay)

    def z_copy(j, slot, peer):
        return pltpu.make_async_remote_copy(
            src_ref=z_send.at[slot], dst_ref=z_recv.at[j], send_sem=z_send_sems.at[j],
            recv_sem=z_recv_sems.at[j], device_id=(peer, yi, tp), device_id_type=MESH_ID,
        )

    def z_send_round(j, slot):
        @pl.when(zi + zshifts[j] < nz)
        def _():
            z_copy(j, slot, zi + zshifts[j]).start()

    def z_absorb(j, slot):
        @pl.when(zi - zshifts[j] >= 0)
        def _():
            z_copy(j, slot, zi - zshifts[j]).wait_recv()
            absorb(z_recv[j], rows, z_total, z_decay)

    z_total[...] = jnp.zeros_like(z_total)
    z_decay[...] = jnp.ones_like(z_decay)
    first = min(2, len(zshifts))
    if zshifts:
        pack(z_send.at[0], quarter_total[...], quarter_decay[...])
    for j in range(first):
        z_send_round(j, 0)
    for j in range(first):
        z_absorb(j, 0)
    for j in range(first, len(zshifts)):
        pack(z_send.at[j - 1], z_total[...], z_decay[...])
        z_send_round(j, j - 1)
        z_absorb(j, j - 1)

    def c_copy(y, target, slot):
        return pltpu.make_async_remote_copy(
            src_ref=c_send.at[y], dst_ref=c_recv.at[slot], send_sem=c_send_sems.at[y],
            recv_sem=c_recv_sems.at[slot], device_id=(zi, target, tp), device_id_type=MESH_ID,
        )

    for y in range(ny):
        done = prefix_decay[y][0:1, :] * z_total[...] + prefix_total[y]

        @pl.when(yi == y)
        def _():
            out_ref[:, y * quarter : (y + 1) * quarter] = done

        @pl.when(yi != y)
        def _():
            c_send[y] = done.astype(jnp.bfloat16)
            c_copy(y, y, yi).start()

    for y in range(ny):
        @pl.when(yi != y)
        def _():
            c_copy(y, yi, y).wait_recv()
            out_ref[:, y * quarter : (y + 1) * quarter] = c_recv[y].astype(jnp.float32)

    for d in range(1, ny):
        target = lax.rem(yi + d, ny)
        row_copy(d, target, yi, target).wait_send()
    for y in range(ny):
        @pl.when(yi != y)
        def _():
            c_copy(y, y, yi).wait_send()
    for j in range(len(zshifts)):
        @pl.when(zi + zshifts[j] < nz)
        def _():
            z_copy(j, 0 if j < first else j - 1, zi + zshifts[j]).wait_send()


def carried_in(passing, state):
    ny, nz = lax.axis_size("cy"), lax.axis_size("cz")
    if ny * nz == 1:
        return jnp.zeros_like(state)
    zshifts = scan_shifts(nz) if nz > 1 else []
    rows, width = state.shape
    quarter = width // ny
    decay = jnp.broadcast_to(passing.reshape(1, 1), (DECAY_ROWS, width)).astype(jnp.float32)
    message = rows + 2 * DECAY_ROWS
    slots = max(len(zshifts), 1)
    return pl.pallas_call(
        functools.partial(scan_kernel, ny, nz, zshifts),
        out_shape=jax.ShapeDtypeStruct((rows, width), jnp.float32),
        in_specs=[pl.BlockSpec(memory_space=pltpu.VMEM)] * 2,
        out_specs=pl.BlockSpec(memory_space=pltpu.VMEM),
        scratch_shapes=[
            pltpu.VMEM((ny, message, quarter), jnp.bfloat16),
            pltpu.VMEM((ny, message, quarter), jnp.bfloat16),
            pltpu.VMEM((slots, message, quarter), jnp.bfloat16),
            pltpu.VMEM((slots, message, quarter), jnp.bfloat16),
            pltpu.VMEM((ny, rows, quarter), jnp.bfloat16),
            pltpu.VMEM((ny, rows, quarter), jnp.bfloat16),
            pltpu.VMEM((ny, rows, quarter), jnp.float32),
            pltpu.VMEM((ny, DECAY_ROWS, quarter), jnp.float32),
            pltpu.VMEM((rows, quarter), jnp.float32),
            pltpu.VMEM((DECAY_ROWS, quarter), jnp.float32),
            pltpu.VMEM((rows, quarter), jnp.float32),
            pltpu.VMEM((DECAY_ROWS, quarter), jnp.float32),
            pltpu.SemaphoreType.DMA((ny,)),
            pltpu.SemaphoreType.DMA((ny,)),
            pltpu.SemaphoreType.DMA((slots,)),
            pltpu.SemaphoreType.DMA((slots,)),
            pltpu.SemaphoreType.DMA((ny,)),
            pltpu.SemaphoreType.DMA((ny,)),
        ],
        compiler_params=pltpu.CompilerParams(collective_id=0, has_side_effects=True),
    )(state.astype(jnp.float32), decay)


def ring_steps(n):
    steps = [(s, True) for s in range(1, (n - 1) // 2 + 1)]
    if n % 2 == 0 and n > 1:
        steps.append((n // 2, False))
    return steps


def gather_kernel(ny, nz, nt, piece_ref, rows_ref, out_ref, rows_out, local_sem, send_sems, recv_sems):
    yi = lax.axis_index("cy")
    zi = lax.axis_index("cz")
    tp = lax.axis_index("tp")
    half = piece_ref.shape[1] // 2
    cols = (pl.ds(0, half), pl.ds(half, half))

    barrier = pltpu.get_barrier_semaphore()
    neighbours = [
        (zi, lax.rem(yi + 1, ny), tp),
        (zi, lax.rem(yi + ny - 1, ny), tp),
        (lax.rem(zi + 1, nz), yi, tp),
        (lax.rem(zi + nz - 1, nz), yi, tp),
        (zi, yi, lax.rem(tp + 1, nt)),
        (zi, yi, lax.rem(tp + nt - 1, nt)),
    ]
    for peer in neighbours:
        pl.semaphore_signal(barrier, 1, device_id=peer, device_id_type=MESH_ID)
    pl.semaphore_wait(barrier, len(neighbours))

    own = pltpu.make_async_copy(piece_ref, out_ref.at[zi, yi], local_sem.at[0])
    own.start()
    own_rows = pltpu.make_async_copy(rows_ref, rows_out.at[tp], local_sem.at[1])
    own_rows.start()
    sends = []

    def ring(along, group_of, first_src, height):
        n, me = {"y": (ny, yi), "z": (nz, zi), "t": (nt, tp)}[along]
        return dict(n=n, me=me, along=along, group_of=group_of, first_src=first_src, steps=ring_steps(n), last={}, height=height)

    def device(r, k):
        return {"y": (zi, k, tp), "z": (k, yi, tp), "t": (zi, yi, k)}[r["along"]]

    def step(r, t):
        if t > len(r["steps"]):
            return
        n, me, group_of = r["n"], r["me"], r["group_of"]
        hop, both = r["steps"][t - 1]
        whole = slice(None)
        half_rows = r["height"] // 2
        for sign in (1, -1):
            if both:
                part = whole
            else:
                part = pl.ds(0, half_rows) if sign == 1 else pl.ds(half_rows, half_rows)
            if t > 1:
                r["last"].pop(sign).wait_recv()
            origin = lax.rem(me + 2 * n - sign * (hop - 1), n)
            target = lax.rem(me + n + sign, n)
            source = lax.rem(me + n - sign, n)
            arrived = lax.rem(me + 2 * n - sign * hop, n)
            idx = len(sends)
            send = pltpu.make_async_remote_copy(
                src_ref=r["first_src"](part) if t == 1 else group_of(origin, part), dst_ref=group_of(origin, part),
                send_sem=send_sems.at[idx], recv_sem=recv_sems.at[idx],
                device_id=device(r, target), device_id_type=MESH_ID,
            )
            incoming = pltpu.make_async_remote_copy(
                src_ref=group_of(arrived, part), dst_ref=group_of(arrived, part),
                send_sem=send_sems.at[idx], recv_sem=recv_sems.at[idx],
                device_id=device(r, source), device_id_type=MESH_ID,
            )
            send.start()
            sends.append(send)
            r["last"][sign] = incoming

    def stage(rings):
        for t in range(1, max(len(r["steps"]) for r in rings) + 1):
            for r in rings:
                step(r, t)
        for r in rings:
            for incoming in r["last"].values():
                incoming.wait_recv()

    height = piece_ref.shape[0]
    stage([
        ring("y", lambda k, p: out_ref.at[zi, k, p, cols[0]], lambda p: piece_ref.at[p, cols[0]], height),
        ring("z", lambda k, p: out_ref.at[k, yi, p, cols[1]], lambda p: piece_ref.at[p, cols[1]], height),
    ])
    own.wait()
    stage([
        ring("z", lambda k, p: out_ref.at[k, :, p, cols[0]], lambda p: out_ref.at[zi, :, p, cols[0]], height),
        ring("y", lambda k, p: out_ref.at[:, k, p, cols[1]], lambda p: out_ref.at[:, yi, p, cols[1]], height),
        ring("t", lambda k, p: rows_out.at[k, p, :], lambda p: rows_ref.at[p, :], rows_ref.shape[0]),
    ])
    own_rows.wait()
    for send in sends:
        send.wait_send()


def gather_blocks(piece, rows):
    ny, nz, nt = lax.axis_size("cy"), lax.axis_size("cz"), lax.axis_size("tp")
    height, width = piece.shape
    count = sum(2 * len(ring_steps(n)) for n in (ny, nz, nz, ny, nt))
    out, rows_out = pl.pallas_call(
        functools.partial(gather_kernel, ny, nz, nt),
        out_shape=(
            jax.ShapeDtypeStruct((nz, ny, height, width), piece.dtype),
            jax.ShapeDtypeStruct((nt,) + rows.shape, rows.dtype),
        ),
        in_specs=[pl.BlockSpec(memory_space=pltpu.VMEM)] * 2,
        out_specs=(pl.BlockSpec(memory_space=pl.ANY), pl.BlockSpec(memory_space=pl.ANY)),
        scratch_shapes=[
            pltpu.SemaphoreType.DMA((2,)),
            pltpu.SemaphoreType.DMA((count,)),
            pltpu.SemaphoreType.DMA((count,)),
        ],
        compiler_params=pltpu.CompilerParams(collective_id=1, has_side_effects=True),
    )(piece, rows)
    return out.reshape(nz * ny * height, width), rows_out.reshape(nt * rows.shape[0], rows.shape[1])


def scatter_kernel(nt, heads_ref, weight_ref, out_ref, send_buf, recv_buf, send_sems, recv_sems):
    tp = lax.axis_index("tp")
    rows = out_ref.shape[0]
    half = out_ref.shape[1] // 2

    barrier = pltpu.get_barrier_semaphore()
    for peer in (lax.rem(tp + 1, nt), lax.rem(tp + nt - 1, nt)):
        pl.semaphore_signal(barrier, 1, device_id=(lax.axis_index("cz"), lax.axis_index("cy"), peer), device_id_type=MESH_ID)

    def own(chunk, side):
        start = pl.multiple_of(chunk * rows, 16)
        part = lax.dot_general(
            heads_ref[pl.ds(start, rows), :],
            weight_ref[side * half : (side + 1) * half, :],
            (((1,), (1,)), ((), ())),
            preferred_element_type=jnp.float32,
        )
        return part.astype(jnp.bfloat16).astype(jnp.float32)

    def copy(side, step, peer):
        slot = side * nt + step
        return pltpu.make_async_remote_copy(
            src_ref=send_buf.at[slot], dst_ref=recv_buf.at[slot], send_sem=send_sems.at[slot],
            recv_sem=recv_sems.at[slot],
            device_id=(lax.axis_index("cz"), lax.axis_index("cy"), peer), device_id_type=MESH_ID,
        )

    sides = ((0, 1), (1, -1))
    first = [own(lax.rem(tp + nt * nt - sign, nt), side) for side, sign in sides]
    pl.semaphore_wait(barrier, 2)
    for step in range(1, nt):
        for side, sign in sides:
            chunk = lax.rem(tp + nt * nt - sign * step, nt)
            total = first[side] if step == 1 else own(chunk, side)
            if step > 1:
                copy(side, step - 1, lax.rem(tp + nt - sign, nt)).wait_recv()
                total = total + recv_buf[side * nt + step - 1].astype(jnp.float32)
            send_buf[side * nt + step] = total.astype(jnp.bfloat16)
            copy(side, step, lax.rem(tp + nt + sign, nt)).start()
    last = [own(tp, side) for side, _ in sides]
    for side, sign in sides:
        copy(side, nt - 1, lax.rem(tp + nt - sign, nt)).wait_recv()
        total = last[side] + recv_buf[side * nt + nt - 1].astype(jnp.float32)
        out_ref[:, side * half : (side + 1) * half] = total.astype(out_ref.dtype)
    for step in range(1, nt):
        for side, sign in sides:
            copy(side, step, lax.rem(tp + nt + sign, nt)).wait_send()


def scatter_rows(heads, weight):
    nt = lax.axis_size("tp")
    rows = heads.shape[0] // nt
    width = weight.shape[0]
    return pl.pallas_call(
        functools.partial(scatter_kernel, nt),
        out_shape=jax.ShapeDtypeStruct((rows, width), jnp.bfloat16),
        in_specs=[pl.BlockSpec(memory_space=pltpu.VMEM)] * 2,
        out_specs=pl.BlockSpec(memory_space=pltpu.VMEM),
        scratch_shapes=[
            pltpu.VMEM((2 * nt, rows, width // 2), jnp.bfloat16),
            pltpu.VMEM((2 * nt, rows, width // 2), jnp.bfloat16),
            pltpu.SemaphoreType.DMA((2 * nt,)),
            pltpu.SemaphoreType.DMA((2 * nt,)),
        ],
        compiler_params=pltpu.CompilerParams(
            collective_id=2, has_side_effects=True, vmem_limit_bytes=48 * 1024 * 1024
        ),
    )(heads, weight)


def rms_rows(embedded_entries, norm_gain):
    token_float = embedded_entries.astype(jnp.float32)
    moment = jnp.mean(token_float * token_float, axis=1, keepdims=True)
    return (token_float * lax.rsqrt(moment + EPSILON) * norm_gain).astype(jnp.bfloat16)


def local_terms(queries, key_rows, values, log_forget, input_gate, starts):
    length = queries.shape[0]
    scaling = queries.shape[1] ** (-0.5)
    segment = jnp.cumsum(starts)
    levels = jnp.cumsum(log_forget)
    position = jnp.arange(length)
    allowed = (position[:, None] >= position[None, :]) & (segment[:, None] == segment[None, :])
    decays = jnp.where(
        allowed,
        jnp.exp(jnp.minimum(levels[:, None] - levels[None, :], 0.0) + input_gate[None, :]),
        0.0,
    )
    scores = jnp.dot(queries, key_rows.T, preferred_element_type=jnp.float32) * scaling
    weights = (scores * decays).astype(jnp.bfloat16)
    inner_part = jnp.dot(weights, values, preferred_element_type=jnp.float32)
    last_level = levels[-1]
    last_seg = segment[-1]
    keeping = jnp.where(segment == last_seg, jnp.exp(last_level - levels + input_gate), 0.0)
    weighted = (key_rows.astype(jnp.float32) * keeping[:, None]).astype(jnp.bfloat16)
    local_state = lax.dot_general(
        weighted, values, (((0,), (0,)), ((), ())), preferred_element_type=jnp.float32
    )
    passing = jnp.where(last_seg == 0, jnp.exp(last_level), 0.0)
    carried = jnp.where(segment == 0, jnp.exp(levels), 0.0) * scaling
    return (inner_part, local_state, passing, carried)


def apply_state(queries, carried, incoming):
    lifted = queries.astype(jnp.float32) * carried[:, None]
    return jnp.dot(
        lifted, incoming, precision=lax.Precision.HIGHEST, preferred_element_type=jnp.float32
    )


def head_norm(head_out, gain):
    centre = jnp.mean(head_out, axis=1, keepdims=True)
    shifted = head_out - centre
    spread = jnp.mean(shifted * shifted, axis=1, keepdims=True)
    return (shifted * lax.rsqrt(spread + EPSILON) * gain).astype(jnp.bfloat16)


def local(
    tokens,
    norm_gain,
    w_qkv,
    w_out,
    head_gain,
    input_codes,
    forget_codes,
    forget_bias,
    document_begin_flags,
):
    normed = rms_rows(tokens, norm_gain)
    width = w_qkv.shape[1]
    both, every_row_list = gather_blocks(jnp.concatenate([w_qkv, w_out.T], axis=1), normed)
    parameter_collection = both[:, :width]
    out_rows = both[:, width:]
    rows_combined = jnp.dot(
        every_row_list, parameter_collection, preferred_element_type=jnp.float32
    )
    rows_combined = rows_combined.astype(jnp.bfloat16)
    heads_here = forget_bias.shape[0]
    stride = 2 * DK + DV
    query_list, inner_list, state_list, passing_list, carried_list = ([], [], [], [], [])
    attention_slot_number = 0
    offset = attention_slot_number * stride
    queries = rows_combined[:, offset : offset + DK]
    key_rows = rows_combined[:, offset + DK : offset + 2 * DK]
    values = rows_combined[:, offset + 2 * DK : offset + stride]
    log_forget = jax.nn.log_sigmoid(
        FORGET_STEP * forget_codes[attention_slot_number].astype(jnp.float32)
        + forget_bias[attention_slot_number]
    )
    input_gate = INPUT_STEP * input_codes[attention_slot_number].astype(jnp.float32)
    inner_part, local_state, passing, carried = local_terms(
        queries, key_rows, values, log_forget, input_gate, document_begin_flags
    )
    query_list.append(queries)
    inner_list.append(inner_part)
    state_list.append(local_state)
    passing_list.append(passing)
    carried_list.append(carried)
    incoming = carried_in(passing_list[0], state_list[0])[None]
    attention_slot_number = 0
    head_out = inner_list[attention_slot_number] + apply_state(
        query_list[attention_slot_number],
        carried_list[attention_slot_number],
        incoming[attention_slot_number],
    )
    normed_heads = head_norm(head_out, head_gain)
    summed = scatter_rows(normed_heads, out_rows).astype(jnp.float32)
    return (tokens.astype(jnp.float32) + summed).astype(jnp.bfloat16)


def solution(mesh):
    z_rows = 4 if mesh.shape["ctx"] % 4 == 0 else 1
    split = jax.sharding.Mesh(
        mesh.devices.reshape(mesh.shape["ctx"] // z_rows, z_rows, mesh.shape["tp"]), ("cz", "cy", "tp")
    )
    blocks = ("cz", "cy")
    placed = (
        P(blocks + ("tp",), None),
        P(),
        P(blocks, "tp"),
        P("tp", blocks),
        P("tp"),
        P("tp", blocks),
        P("tp", blocks),
        P("tp"),
        P(blocks),
    )
    return jax.shard_map(
        local, mesh=split, in_specs=placed, out_specs=P(blocks + ("tp",), None), check_vma=False
    )
```

```python
import functools

import jax
import jax.numpy as jnp
from jax import lax
from jax.experimental import pallas as pl
from jax.experimental.pallas import tpu as pltpu
from jax.sharding import PartitionSpec as P

DK = 256
DV = 512


EPSILON = 1e-06
FORGET_STEP = 0.5
INPUT_STEP = 0.5


MESH_ID = pl.DeviceIdType.MESH
DECAY_ROWS = 16


def scan_shifts(count):
    shifts = [1] + ([2] if count > 2 else [])
    k = 2
    while k < count:
        shifts.append(k)
        k *= 2
    return shifts


def pack(ref, total, decay):
    rows = total.shape[0]
    high = decay.astype(jnp.bfloat16)
    ref[:rows, :] = total.astype(jnp.bfloat16)
    ref[rows : rows + DECAY_ROWS, :] = high
    ref[rows + DECAY_ROWS :, :] = (decay - high.astype(jnp.float32)).astype(jnp.bfloat16)


def absorb(got, rows, acc_total, acc_decay):
    far_total = got[:rows].astype(jnp.float32)
    far_decay = got[rows : rows + DECAY_ROWS].astype(jnp.float32) + got[rows + DECAY_ROWS :].astype(jnp.float32)
    decay = acc_decay[...]
    acc_total[...] = decay[0:1, :] * far_total + acc_total[...]
    acc_decay[...] = decay * far_decay


def extend(got, rows, acc_total, acc_decay):
    far_total = got[:rows].astype(jnp.float32)
    far_decay = got[rows : rows + DECAY_ROWS].astype(jnp.float32) + got[rows + DECAY_ROWS :].astype(jnp.float32)
    acc_total[...] = far_decay[0:1, :] * acc_total[...] + far_total
    acc_decay[...] = far_decay * acc_decay[...]


def scan_kernel(
    ny, nz, zshifts, state_ref, decay_ref, out_ref,
    row_send, row_recv, z_send, z_recv, c_send, c_recv,
    prefix_total, prefix_decay, quarter_total, quarter_decay, z_total, z_decay,
    row_send_sems, row_recv_sems, z_send_sems, z_recv_sems, c_send_sems, c_recv_sems,
):
    yi = lax.axis_index("cy")
    zi = lax.axis_index("cz")
    tp = lax.axis_index("tp")
    rows, width = state_ref.shape
    quarter = width // ny

    barrier = pltpu.get_barrier_semaphore()
    z_partners = sorted(set(zshifts))
    for d in range(1, ny):
        pl.semaphore_signal(barrier, 1, device_id=(zi, lax.rem(yi + d, ny), tp), device_id_type=MESH_ID)
    for s in z_partners:
        for peer in (lax.rem(zi + s, nz), lax.rem(zi + nz - s, nz)):
            pl.semaphore_signal(barrier, 1, device_id=(peer, yi, tp), device_id_type=MESH_ID)
    pl.semaphore_wait(barrier, (ny - 1) + 2 * len(z_partners))

    def row_copy(d, target, slot, part):
        return pltpu.make_async_remote_copy(
            src_ref=row_send.at[part], dst_ref=row_recv.at[slot], send_sem=row_send_sems.at[d],
            recv_sem=row_recv_sems.at[slot], device_id=(zi, target, tp), device_id_type=MESH_ID,
        )

    for y in range(ny):
        pack(row_send.at[y], state_ref[:, y * quarter : (y + 1) * quarter], decay_ref[:, y * quarter : (y + 1) * quarter])
    for d in range(1, ny):
        target = lax.rem(yi + d, ny)
        row_copy(d, target, yi, target).start()
    for d in range(1, ny):
        row_copy(d, yi, lax.rem(yi + ny - d, ny), yi).wait_recv()

    quarter_total[...] = jnp.zeros_like(quarter_total)
    quarter_decay[...] = jnp.ones_like(quarter_decay)
    for y in range(ny):
        prefix_total[y] = quarter_total[...]
        prefix_decay[y] = quarter_decay[...]

        @pl.when(yi == y)
        def _():
            extend(row_send[y], rows, quarter_total, quarter_decay)

        @pl.when(yi != y)
        def _():
            extend(row_recv[y], rows, quarter_total, quarter_decay)

    def z_copy(j, slot, peer):
        return pltpu.make_async_remote_copy(
            src_ref=z_send.at[slot], dst_ref=z_recv.at[j], send_sem=z_send_sems.at[j],
            recv_sem=z_recv_sems.at[j], device_id=(peer, yi, tp), device_id_type=MESH_ID,
        )

    def z_send_round(j, slot):
        @pl.when(zi + zshifts[j] < nz)
        def _():
            z_copy(j, slot, zi + zshifts[j]).start()

    def z_absorb(j, slot):
        @pl.when(zi - zshifts[j] >= 0)
        def _():
            z_copy(j, slot, zi - zshifts[j]).wait_recv()
            absorb(z_recv[j], rows, z_total, z_decay)

    z_total[...] = jnp.zeros_like(z_total)
    z_decay[...] = jnp.ones_like(z_decay)
    first = min(2, len(zshifts))
    if zshifts:
        pack(z_send.at[0], quarter_total[...], quarter_decay[...])
    for j in range(first):
        z_send_round(j, 0)
    for j in range(first):
        z_absorb(j, 0)
    for j in range(first, len(zshifts)):
        pack(z_send.at[j - 1], z_total[...], z_decay[...])
        z_send_round(j, j - 1)
        z_absorb(j, j - 1)

    def c_copy(y, target, slot):
        return pltpu.make_async_remote_copy(
            src_ref=c_send.at[y], dst_ref=c_recv.at[slot], send_sem=c_send_sems.at[y],
            recv_sem=c_recv_sems.at[slot], device_id=(zi, target, tp), device_id_type=MESH_ID,
        )

    for y in range(ny):
        done = prefix_decay[y][0:1, :] * z_total[...] + prefix_total[y]

        @pl.when(yi == y)
        def _():
            out_ref[:, y * quarter : (y + 1) * quarter] = done

        @pl.when(yi != y)
        def _():
            c_send[y] = done.astype(jnp.bfloat16)
            c_copy(y, y, yi).start()

    for y in range(ny):
        @pl.when(yi != y)
        def _():
            c_copy(y, yi, y).wait_recv()
            out_ref[:, y * quarter : (y + 1) * quarter] = c_recv[y].astype(jnp.float32)

    for d in range(1, ny):
        target = lax.rem(yi + d, ny)
        row_copy(d, target, yi, target).wait_send()
    for y in range(ny):
        @pl.when(yi != y)
        def _():
            c_copy(y, y, yi).wait_send()
    for j in range(len(zshifts)):
        @pl.when(zi + zshifts[j] < nz)
        def _():
            z_copy(j, 0 if j < first else j - 1, zi + zshifts[j]).wait_send()


def carried_in(passing, state):
    ny, nz = lax.axis_size("cy"), lax.axis_size("cz")
    if ny * nz == 1:
        return jnp.zeros_like(state)
    zshifts = scan_shifts(nz) if nz > 1 else []
    rows, width = state.shape
    quarter = width // ny
    decay = jnp.broadcast_to(passing.reshape(1, 1), (DECAY_ROWS, width)).astype(jnp.float32)
    message = rows + 2 * DECAY_ROWS
    slots = max(len(zshifts), 1)
    return pl.pallas_call(
        functools.partial(scan_kernel, ny, nz, zshifts),
        out_shape=jax.ShapeDtypeStruct((rows, width), jnp.float32),
        in_specs=[pl.BlockSpec(memory_space=pltpu.VMEM)] * 2,
        out_specs=pl.BlockSpec(memory_space=pltpu.VMEM),
        scratch_shapes=[
            pltpu.VMEM((ny, message, quarter), jnp.bfloat16),
            pltpu.VMEM((ny, message, quarter), jnp.bfloat16),
            pltpu.VMEM((slots, message, quarter), jnp.bfloat16),
            pltpu.VMEM((slots, message, quarter), jnp.bfloat16),
            pltpu.VMEM((ny, rows, quarter), jnp.bfloat16),
            pltpu.VMEM((ny, rows, quarter), jnp.bfloat16),
            pltpu.VMEM((ny, rows, quarter), jnp.float32),
            pltpu.VMEM((ny, DECAY_ROWS, quarter), jnp.float32),
            pltpu.VMEM((rows, quarter), jnp.float32),
            pltpu.VMEM((DECAY_ROWS, quarter), jnp.float32),
            pltpu.VMEM((rows, quarter), jnp.float32),
            pltpu.VMEM((DECAY_ROWS, quarter), jnp.float32),
            pltpu.SemaphoreType.DMA((ny,)),
            pltpu.SemaphoreType.DMA((ny,)),
            pltpu.SemaphoreType.DMA((slots,)),
            pltpu.SemaphoreType.DMA((slots,)),
            pltpu.SemaphoreType.DMA((ny,)),
            pltpu.SemaphoreType.DMA((ny,)),
        ],
        compiler_params=pltpu.CompilerParams(collective_id=0, has_side_effects=True),
    )(state.astype(jnp.float32), decay)


def ring_steps(n):
    steps = [(s, True) for s in range(1, (n - 1) // 2 + 1)]
    if n % 2 == 0 and n > 1:
        steps.append((n // 2, False))
    return steps


def gather_kernel(ny, nz, nt, piece_ref, rows_ref, out_ref, rows_out, local_sem, send_sems, recv_sems):
    yi = lax.axis_index("cy")
    zi = lax.axis_index("cz")
    tp = lax.axis_index("tp")
    half = piece_ref.shape[1] // 2
    cols = (pl.ds(0, half), pl.ds(half, half))

    barrier = pltpu.get_barrier_semaphore()
    neighbours = [
        (zi, lax.rem(yi + 1, ny), tp),
        (zi, lax.rem(yi + ny - 1, ny), tp),
        (lax.rem(zi + 1, nz), yi, tp),
        (lax.rem(zi + nz - 1, nz), yi, tp),
        (zi, yi, lax.rem(tp + 1, nt)),
        (zi, yi, lax.rem(tp + nt - 1, nt)),
    ]
    for peer in neighbours:
        pl.semaphore_signal(barrier, 1, device_id=peer, device_id_type=MESH_ID)
    pl.semaphore_wait(barrier, len(neighbours))

    own = pltpu.make_async_copy(piece_ref, out_ref.at[zi, yi], local_sem.at[0])
    own.start()
    own_rows = pltpu.make_async_copy(rows_ref, rows_out.at[tp], local_sem.at[1])
    own_rows.start()
    sends = []

    def ring(along, group_of, first_src, height):
        n, me = {"y": (ny, yi), "z": (nz, zi), "t": (nt, tp)}[along]
        return dict(n=n, me=me, along=along, group_of=group_of, first_src=first_src, steps=ring_steps(n), last={}, height=height)

    def device(r, k):
        return {"y": (zi, k, tp), "z": (k, yi, tp), "t": (zi, yi, k)}[r["along"]]

    def step(r, t):
        if t > len(r["steps"]):
            return
        n, me, group_of = r["n"], r["me"], r["group_of"]
        hop, both = r["steps"][t - 1]
        whole = slice(None)
        half_rows = r["height"] // 2
        for sign in (1, -1):
            if both:
                part = whole
            else:
                part = pl.ds(0, half_rows) if sign == 1 else pl.ds(half_rows, half_rows)
            if t > 1:
                r["last"].pop(sign).wait_recv()
            origin = lax.rem(me + 2 * n - sign * (hop - 1), n)
            target = lax.rem(me + n + sign, n)
            source = lax.rem(me + n - sign, n)
            arrived = lax.rem(me + 2 * n - sign * hop, n)
            idx = len(sends)
            send = pltpu.make_async_remote_copy(
                src_ref=r["first_src"](part) if t == 1 else group_of(origin, part), dst_ref=group_of(origin, part),
                send_sem=send_sems.at[idx], recv_sem=recv_sems.at[idx],
                device_id=device(r, target), device_id_type=MESH_ID,
            )
            incoming = pltpu.make_async_remote_copy(
                src_ref=group_of(arrived, part), dst_ref=group_of(arrived, part),
                send_sem=send_sems.at[idx], recv_sem=recv_sems.at[idx],
                device_id=device(r, source), device_id_type=MESH_ID,
            )
            send.start()
            sends.append(send)
            r["last"][sign] = incoming

    def stage(rings):
        for t in range(1, max(len(r["steps"]) for r in rings) + 1):
            for r in rings:
                step(r, t)
        for r in rings:
            for incoming in r["last"].values():
                incoming.wait_recv()

    height = piece_ref.shape[0]
    a1 = ring("y", lambda k, p: out_ref.at[zi, k, p, cols[0]], lambda p: piece_ref.at[p, cols[0]], height)
    b1 = ring("z", lambda k, p: out_ref.at[k, yi, p, cols[1]], lambda p: piece_ref.at[p, cols[1]], height)
    a2 = ring("z", lambda k, p: out_ref.at[k, :, p, cols[0]], lambda p: out_ref.at[zi, :, p, cols[0]], height)
    b2 = ring("y", lambda k, p: out_ref.at[:, k, p, cols[1]], lambda p: out_ref.at[:, yi, p, cols[1]], height)
    rt = ring("t", lambda k, p: rows_out.at[k, p, :], lambda p: rows_ref.at[p, :], rows_ref.shape[0])

    def finish(r):
        for incoming in r["last"].values():
            incoming.wait_recv()
        r["last"] = {}

    for t in range(1, len(a1["steps"]) + 1):
        step(a1, t)
        step(b1, t)
    finish(a1)
    own.wait()
    step(a2, 1)
    for t in range(len(a1["steps"]) + 1, len(b1["steps"]) + 1):
        step(b1, t)
    finish(b1)
    later = max(len(a2["steps"]), len(b2["steps"]) + 1, len(rt["steps"]) + 1)
    for t in range(1, later + 1):
        step(b2, t)
        step(rt, t)
        step(a2, t + 1)
    for r in (a2, b2, rt):
        finish(r)
    own_rows.wait()
    for send in sends:
        send.wait_send()


def gather_blocks(piece, rows):
    ny, nz, nt = lax.axis_size("cy"), lax.axis_size("cz"), lax.axis_size("tp")
    height, width = piece.shape
    count = sum(2 * len(ring_steps(n)) for n in (ny, nz, nz, ny, nt))
    out, rows_out = pl.pallas_call(
        functools.partial(gather_kernel, ny, nz, nt),
        out_shape=(
            jax.ShapeDtypeStruct((nz, ny, height, width), piece.dtype),
            jax.ShapeDtypeStruct((nt,) + rows.shape, rows.dtype),
        ),
        in_specs=[pl.BlockSpec(memory_space=pltpu.VMEM)] * 2,
        out_specs=(pl.BlockSpec(memory_space=pl.ANY), pl.BlockSpec(memory_space=pl.ANY)),
        scratch_shapes=[
            pltpu.SemaphoreType.DMA((2,)),
            pltpu.SemaphoreType.DMA((count,)),
            pltpu.SemaphoreType.DMA((count,)),
        ],
        compiler_params=pltpu.CompilerParams(collective_id=1, has_side_effects=True),
    )(piece, rows)
    return out.reshape(nz * ny * height, width), rows_out.reshape(nt * rows.shape[0], rows.shape[1])


def scatter_kernel(nt, heads_ref, weight_ref, out_ref, send_buf, recv_buf, send_sems, recv_sems):
    tp = lax.axis_index("tp")
    rows = out_ref.shape[0]
    half = out_ref.shape[1] // 2

    barrier = pltpu.get_barrier_semaphore()
    for peer in (lax.rem(tp + 1, nt), lax.rem(tp + nt - 1, nt)):
        pl.semaphore_signal(barrier, 1, device_id=(lax.axis_index("cz"), lax.axis_index("cy"), peer), device_id_type=MESH_ID)

    def own(chunk, side):
        start = pl.multiple_of(chunk * rows, 16)
        part = lax.dot_general(
            heads_ref[pl.ds(start, rows), :],
            weight_ref[side * half : (side + 1) * half, :],
            (((1,), (1,)), ((), ())),
            preferred_element_type=jnp.float32,
        )
        return part.astype(jnp.bfloat16).astype(jnp.float32)

    def copy(side, step, peer):
        slot = side * nt + step
        return pltpu.make_async_remote_copy(
            src_ref=send_buf.at[slot], dst_ref=recv_buf.at[slot], send_sem=send_sems.at[slot],
            recv_sem=recv_sems.at[slot],
            device_id=(lax.axis_index("cz"), lax.axis_index("cy"), peer), device_id_type=MESH_ID,
        )

    sides = ((0, 1), (1, -1))
    first = [own(lax.rem(tp + nt * nt - sign, nt), side) for side, sign in sides]
    pl.semaphore_wait(barrier, 2)
    for step in range(1, nt):
        for side, sign in sides:
            chunk = lax.rem(tp + nt * nt - sign * step, nt)
            total = first[side] if step == 1 else own(chunk, side)
            if step > 1:
                copy(side, step - 1, lax.rem(tp + nt - sign, nt)).wait_recv()
                total = total + recv_buf[side * nt + step - 1].astype(jnp.float32)
            send_buf[side * nt + step] = total.astype(jnp.bfloat16)
            copy(side, step, lax.rem(tp + nt + sign, nt)).start()
    last = [own(tp, side) for side, _ in sides]
    for side, sign in sides:
        copy(side, nt - 1, lax.rem(tp + nt - sign, nt)).wait_recv()
        total = last[side] + recv_buf[side * nt + nt - 1].astype(jnp.float32)
        out_ref[:, side * half : (side + 1) * half] = total.astype(out_ref.dtype)
    for step in range(1, nt):
        for side, sign in sides:
            copy(side, step, lax.rem(tp + nt + sign, nt)).wait_send()


def scatter_rows(heads, weight):
    nt = lax.axis_size("tp")
    rows = heads.shape[0] // nt
    width = weight.shape[0]
    return pl.pallas_call(
        functools.partial(scatter_kernel, nt),
        out_shape=jax.ShapeDtypeStruct((rows, width), jnp.bfloat16),
        in_specs=[pl.BlockSpec(memory_space=pltpu.VMEM)] * 2,
        out_specs=pl.BlockSpec(memory_space=pltpu.VMEM),
        scratch_shapes=[
            pltpu.VMEM((2 * nt, rows, width // 2), jnp.bfloat16),
            pltpu.VMEM((2 * nt, rows, width // 2), jnp.bfloat16),
            pltpu.SemaphoreType.DMA((2 * nt,)),
            pltpu.SemaphoreType.DMA((2 * nt,)),
        ],
        compiler_params=pltpu.CompilerParams(
            collective_id=2, has_side_effects=True, vmem_limit_bytes=48 * 1024 * 1024
        ),
    )(heads, weight)


def rms_rows(embedded_entries, norm_gain):
    token_float = embedded_entries.astype(jnp.float32)
    moment = jnp.mean(token_float * token_float, axis=1, keepdims=True)
    return (token_float * lax.rsqrt(moment + EPSILON) * norm_gain).astype(jnp.bfloat16)


def local_terms(queries, key_rows, values, log_forget, input_gate, starts):
    length = queries.shape[0]
    scaling = queries.shape[1] ** (-0.5)
    segment = jnp.cumsum(starts)
    levels = jnp.cumsum(log_forget)
    position = jnp.arange(length)
    allowed = (position[:, None] >= position[None, :]) & (segment[:, None] == segment[None, :])
    decays = jnp.where(
        allowed,
        jnp.exp(jnp.minimum(levels[:, None] - levels[None, :], 0.0) + input_gate[None, :]),
        0.0,
    )
    scores = jnp.dot(queries, key_rows.T, preferred_element_type=jnp.float32) * scaling
    weights = (scores * decays).astype(jnp.bfloat16)
    inner_part = jnp.dot(weights, values, preferred_element_type=jnp.float32)
    last_level = levels[-1]
    last_seg = segment[-1]
    keeping = jnp.where(segment == last_seg, jnp.exp(last_level - levels + input_gate), 0.0)
    weighted = (key_rows.astype(jnp.float32) * keeping[:, None]).astype(jnp.bfloat16)
    local_state = lax.dot_general(
        weighted, values, (((0,), (0,)), ((), ())), preferred_element_type=jnp.float32
    )
    passing = jnp.where(last_seg == 0, jnp.exp(last_level), 0.0)
    carried = jnp.where(segment == 0, jnp.exp(levels), 0.0) * scaling
    return (inner_part, local_state, passing, carried)


def apply_state(queries, carried, incoming):
    lifted = queries.astype(jnp.float32) * carried[:, None]
    return jnp.dot(
        lifted, incoming, precision=lax.Precision.HIGHEST, preferred_element_type=jnp.float32
    )


def head_norm(head_out, gain):
    centre = jnp.mean(head_out, axis=1, keepdims=True)
    shifted = head_out - centre
    spread = jnp.mean(shifted * shifted, axis=1, keepdims=True)
    return (shifted * lax.rsqrt(spread + EPSILON) * gain).astype(jnp.bfloat16)


def local(
    tokens,
    norm_gain,
    w_qkv,
    w_out,
    head_gain,
    input_codes,
    forget_codes,
    forget_bias,
    document_begin_flags,
):
    normed = rms_rows(tokens, norm_gain)
    width = w_qkv.shape[1]
    both, every_row_list = gather_blocks(jnp.concatenate([w_qkv, w_out.T], axis=1), normed)
    parameter_collection = both[:, :width]
    out_rows = both[:, width:]
    rows_combined = jnp.dot(
        every_row_list, parameter_collection, preferred_element_type=jnp.float32
    )
    rows_combined = rows_combined.astype(jnp.bfloat16)
    heads_here = forget_bias.shape[0]
    stride = 2 * DK + DV
    query_list, inner_list, state_list, passing_list, carried_list = ([], [], [], [], [])
    attention_slot_number = 0
    offset = attention_slot_number * stride
    queries = rows_combined[:, offset : offset + DK]
    key_rows = rows_combined[:, offset + DK : offset + 2 * DK]
    values = rows_combined[:, offset + 2 * DK : offset + stride]
    log_forget = jax.nn.log_sigmoid(
        FORGET_STEP * forget_codes[attention_slot_number].astype(jnp.float32)
        + forget_bias[attention_slot_number]
    )
    input_gate = INPUT_STEP * input_codes[attention_slot_number].astype(jnp.float32)
    inner_part, local_state, passing, carried = local_terms(
        queries, key_rows, values, log_forget, input_gate, document_begin_flags
    )
    query_list.append(queries)
    inner_list.append(inner_part)
    state_list.append(local_state)
    passing_list.append(passing)
    carried_list.append(carried)
    incoming = carried_in(passing_list[0], state_list[0])[None]
    attention_slot_number = 0
    head_out = inner_list[attention_slot_number] + apply_state(
        query_list[attention_slot_number],
        carried_list[attention_slot_number],
        incoming[attention_slot_number],
    )
    normed_heads = head_norm(head_out, head_gain)
    summed = scatter_rows(normed_heads, out_rows).astype(jnp.float32)
    return (tokens.astype(jnp.float32) + summed).astype(jnp.bfloat16)


def solution(mesh):
    z_rows = 4 if mesh.shape["ctx"] % 4 == 0 else 1
    split = jax.sharding.Mesh(
        mesh.devices.reshape(mesh.shape["ctx"] // z_rows, z_rows, mesh.shape["tp"]), ("cz", "cy", "tp")
    )
    blocks = ("cz", "cy")
    placed = (
        P(blocks + ("tp",), None),
        P(),
        P(blocks, "tp"),
        P("tp", blocks),
        P("tp"),
        P("tp", blocks),
        P("tp", blocks),
        P("tp"),
        P(blocks),
    )
    return jax.shard_map(
        local, mesh=split, in_specs=placed, out_specs=P(blocks + ("tp",), None), check_vma=False
    )
```

```python
import functools

import jax
import jax.numpy as jnp
from jax import lax
from jax.experimental import pallas as pl
from jax.experimental.pallas import tpu as pltpu
from jax.sharding import PartitionSpec as P

DK = 256
DV = 512


EPSILON = 1e-06
FORGET_STEP = 0.5
INPUT_STEP = 0.5


MESH_ID = pl.DeviceIdType.MESH
DECAY_ROWS = 16


def scan_shifts(count):
    shifts = [1] + ([2] if count > 2 else [])
    k = 2
    while k < count:
        shifts.append(k)
        k *= 2
    return shifts


def pack(ref, total, decay):
    rows = total.shape[0]
    high = decay.astype(jnp.bfloat16)
    ref[:rows, :] = total.astype(jnp.bfloat16)
    ref[rows : rows + DECAY_ROWS, :] = high
    ref[rows + DECAY_ROWS :, :] = (decay - high.astype(jnp.float32)).astype(jnp.bfloat16)


def absorb(got, rows, acc_total, acc_decay):
    far_total = got[:rows].astype(jnp.float32)
    far_decay = got[rows : rows + DECAY_ROWS].astype(jnp.float32) + got[rows + DECAY_ROWS :].astype(jnp.float32)
    decay = acc_decay[...]
    acc_total[...] = decay[0:1, :] * far_total + acc_total[...]
    acc_decay[...] = decay * far_decay


def extend(got, rows, acc_total, acc_decay):
    far_total = got[:rows].astype(jnp.float32)
    far_decay = got[rows : rows + DECAY_ROWS].astype(jnp.float32) + got[rows + DECAY_ROWS :].astype(jnp.float32)
    acc_total[...] = far_decay[0:1, :] * acc_total[...] + far_total
    acc_decay[...] = far_decay * acc_decay[...]


def scan_kernel(
    ny, nz, zshifts, state_ref, decay_ref, out_ref,
    row_send, row_recv, z_send, z_recv, c_send, c_recv,
    prefix_total, prefix_decay, quarter_total, quarter_decay, z_total, z_decay,
    row_send_sems, row_recv_sems, z_send_sems, z_recv_sems, c_send_sems, c_recv_sems,
):
    yi = lax.axis_index("cy")
    zi = lax.axis_index("cz")
    tp = lax.axis_index("tp")
    rows, width = state_ref.shape
    quarter = width // ny

    barrier = pltpu.get_barrier_semaphore()
    z_partners = sorted(set(zshifts))
    for d in range(1, ny):
        pl.semaphore_signal(barrier, 1, device_id=(zi, lax.rem(yi + d, ny), tp), device_id_type=MESH_ID)
    for s in z_partners:
        for peer in (lax.rem(zi + s, nz), lax.rem(zi + nz - s, nz)):
            pl.semaphore_signal(barrier, 1, device_id=(peer, yi, tp), device_id_type=MESH_ID)
    pl.semaphore_wait(barrier, (ny - 1) + 2 * len(z_partners))

    def row_copy(d, target, slot, part):
        return pltpu.make_async_remote_copy(
            src_ref=row_send.at[part], dst_ref=row_recv.at[slot], send_sem=row_send_sems.at[d],
            recv_sem=row_recv_sems.at[slot], device_id=(zi, target, tp), device_id_type=MESH_ID,
        )

    for y in range(ny):
        pack(row_send.at[y], state_ref[:, y * quarter : (y + 1) * quarter], decay_ref[:, y * quarter : (y + 1) * quarter])
    for d in range(1, ny):
        target = lax.rem(yi + d, ny)
        row_copy(d, target, yi, target).start()
    for d in range(1, ny):
        row_copy(d, yi, lax.rem(yi + ny - d, ny), yi).wait_recv()

    quarter_total[...] = jnp.zeros_like(quarter_total)
    quarter_decay[...] = jnp.ones_like(quarter_decay)
    for y in range(ny):
        prefix_total[y] = quarter_total[...]
        prefix_decay[y] = quarter_decay[...]

        @pl.when(yi == y)
        def _():
            extend(row_send[y], rows, quarter_total, quarter_decay)

        @pl.when(yi != y)
        def _():
            extend(row_recv[y], rows, quarter_total, quarter_decay)

    def z_copy(j, slot, peer):
        return pltpu.make_async_remote_copy(
            src_ref=z_send.at[slot], dst_ref=z_recv.at[j], send_sem=z_send_sems.at[j],
            recv_sem=z_recv_sems.at[j], device_id=(peer, yi, tp), device_id_type=MESH_ID,
        )

    def z_send_round(j, slot):
        @pl.when(zi + zshifts[j] < nz)
        def _():
            z_copy(j, slot, zi + zshifts[j]).start()

    def z_absorb(j, slot):
        @pl.when(zi - zshifts[j] >= 0)
        def _():
            z_copy(j, slot, zi - zshifts[j]).wait_recv()
            absorb(z_recv[j], rows, z_total, z_decay)

    z_total[...] = jnp.zeros_like(z_total)
    z_decay[...] = jnp.ones_like(z_decay)
    first = min(2, len(zshifts))
    if zshifts:
        pack(z_send.at[0], quarter_total[...], quarter_decay[...])
    for j in range(first):
        z_send_round(j, 0)
    for j in range(first):
        z_absorb(j, 0)
    for j in range(first, len(zshifts)):
        pack(z_send.at[j - 1], z_total[...], z_decay[...])
        z_send_round(j, j - 1)
        z_absorb(j, j - 1)

    def c_copy(y, target, slot):
        return pltpu.make_async_remote_copy(
            src_ref=c_send.at[y], dst_ref=c_recv.at[slot], send_sem=c_send_sems.at[y],
            recv_sem=c_recv_sems.at[slot], device_id=(zi, target, tp), device_id_type=MESH_ID,
        )

    for y in range(ny):
        done = prefix_decay[y][0:1, :] * z_total[...] + prefix_total[y]

        @pl.when(yi == y)
        def _():
            out_ref[:, y * quarter : (y + 1) * quarter] = done

        @pl.when(yi != y)
        def _():
            c_send[y] = done.astype(jnp.bfloat16)
            c_copy(y, y, yi).start()

    for y in range(ny):
        @pl.when(yi != y)
        def _():
            c_copy(y, yi, y).wait_recv()
            out_ref[:, y * quarter : (y + 1) * quarter] = c_recv[y].astype(jnp.float32)

    for d in range(1, ny):
        target = lax.rem(yi + d, ny)
        row_copy(d, target, yi, target).wait_send()
    for y in range(ny):
        @pl.when(yi != y)
        def _():
            c_copy(y, y, yi).wait_send()
    for j in range(len(zshifts)):
        @pl.when(zi + zshifts[j] < nz)
        def _():
            z_copy(j, 0 if j < first else j - 1, zi + zshifts[j]).wait_send()


def carried_in(passing, state):
    ny, nz = lax.axis_size("cy"), lax.axis_size("cz")
    if ny * nz == 1:
        return jnp.zeros_like(state)
    zshifts = scan_shifts(nz) if nz > 1 else []
    rows, width = state.shape
    quarter = width // ny
    decay = jnp.broadcast_to(passing.reshape(1, 1), (DECAY_ROWS, width)).astype(jnp.float32)
    message = rows + 2 * DECAY_ROWS
    slots = max(len(zshifts), 1)
    return pl.pallas_call(
        functools.partial(scan_kernel, ny, nz, zshifts),
        out_shape=jax.ShapeDtypeStruct((rows, width), jnp.float32),
        in_specs=[pl.BlockSpec(memory_space=pltpu.VMEM)] * 2,
        out_specs=pl.BlockSpec(memory_space=pltpu.VMEM),
        scratch_shapes=[
            pltpu.VMEM((ny, message, quarter), jnp.bfloat16),
            pltpu.VMEM((ny, message, quarter), jnp.bfloat16),
            pltpu.VMEM((slots, message, quarter), jnp.bfloat16),
            pltpu.VMEM((slots, message, quarter), jnp.bfloat16),
            pltpu.VMEM((ny, rows, quarter), jnp.bfloat16),
            pltpu.VMEM((ny, rows, quarter), jnp.bfloat16),
            pltpu.VMEM((ny, rows, quarter), jnp.float32),
            pltpu.VMEM((ny, DECAY_ROWS, quarter), jnp.float32),
            pltpu.VMEM((rows, quarter), jnp.float32),
            pltpu.VMEM((DECAY_ROWS, quarter), jnp.float32),
            pltpu.VMEM((rows, quarter), jnp.float32),
            pltpu.VMEM((DECAY_ROWS, quarter), jnp.float32),
            pltpu.SemaphoreType.DMA((ny,)),
            pltpu.SemaphoreType.DMA((ny,)),
            pltpu.SemaphoreType.DMA((slots,)),
            pltpu.SemaphoreType.DMA((slots,)),
            pltpu.SemaphoreType.DMA((ny,)),
            pltpu.SemaphoreType.DMA((ny,)),
        ],
        compiler_params=pltpu.CompilerParams(collective_id=0, has_side_effects=True),
    )(state.astype(jnp.float32), decay)


def ring_steps(n):
    steps = [(s, True) for s in range(1, (n - 1) // 2 + 1)]
    if n % 2 == 0 and n > 1:
        steps.append((n // 2, False))
    return steps


def gather_kernel(ny, nz, nt, piece_ref, rows_ref, out_ref, rows_out, local_sem, send_sems, recv_sems):
    yi = lax.axis_index("cy")
    zi = lax.axis_index("cz")
    tp = lax.axis_index("tp")
    half = piece_ref.shape[1] // 2
    cols = (pl.ds(0, half), pl.ds(half, half))

    barrier = pltpu.get_barrier_semaphore()
    neighbours = [
        (zi, lax.rem(yi + 1, ny), tp),
        (zi, lax.rem(yi + ny - 1, ny), tp),
        (lax.rem(zi + 1, nz), yi, tp),
        (lax.rem(zi + nz - 1, nz), yi, tp),
        (zi, yi, lax.rem(tp + 1, nt)),
        (zi, yi, lax.rem(tp + nt - 1, nt)),
    ]
    for peer in neighbours:
        pl.semaphore_signal(barrier, 1, device_id=peer, device_id_type=MESH_ID)
    pl.semaphore_wait(barrier, len(neighbours))

    own = pltpu.make_async_copy(piece_ref, out_ref.at[zi, yi], local_sem.at[0])
    own.start()
    own_rows = pltpu.make_async_copy(rows_ref, rows_out.at[tp], local_sem.at[1])
    own_rows.start()
    sends = []

    def ring(along, group_of, first_src, height):
        n, me = {"y": (ny, yi), "z": (nz, zi), "t": (nt, tp)}[along]
        return dict(n=n, me=me, along=along, group_of=group_of, first_src=first_src, steps=ring_steps(n), last={}, height=height)

    def device(r, k):
        return {"y": (zi, k, tp), "z": (k, yi, tp), "t": (zi, yi, k)}[r["along"]]

    def step(r, t):
        if t > len(r["steps"]):
            return
        n, me, group_of = r["n"], r["me"], r["group_of"]
        hop, both = r["steps"][t - 1]
        whole = slice(None)
        half_rows = r["height"] // 2
        for sign in (1, -1):
            if both:
                part = whole
            else:
                part = pl.ds(0, half_rows) if sign == 1 else pl.ds(half_rows, half_rows)
            if t > 1:
                r["last"].pop(sign).wait_recv()
            origin = lax.rem(me + 2 * n - sign * (hop - 1), n)
            target = lax.rem(me + n + sign, n)
            source = lax.rem(me + n - sign, n)
            arrived = lax.rem(me + 2 * n - sign * hop, n)
            idx = len(sends)
            send = pltpu.make_async_remote_copy(
                src_ref=r["first_src"](part) if t == 1 else group_of(origin, part), dst_ref=group_of(origin, part),
                send_sem=send_sems.at[idx], recv_sem=recv_sems.at[idx],
                device_id=device(r, target), device_id_type=MESH_ID,
            )
            incoming = pltpu.make_async_remote_copy(
                src_ref=group_of(arrived, part), dst_ref=group_of(arrived, part),
                send_sem=send_sems.at[idx], recv_sem=recv_sems.at[idx],
                device_id=device(r, source), device_id_type=MESH_ID,
            )
            send.start()
            sends.append(send)
            r["last"][sign] = incoming

    def stage(rings):
        for t in range(1, max(len(r["steps"]) for r in rings) + 1):
            for r in rings:
                step(r, t)
        for r in rings:
            for incoming in r["last"].values():
                incoming.wait_recv()

    height = piece_ref.shape[0]
    stage([
        ring("y", lambda k, p: out_ref.at[zi, k, p, cols[0]], lambda p: piece_ref.at[p, cols[0]], height),
        ring("z", lambda k, p: out_ref.at[k, yi, p, cols[1]], lambda p: piece_ref.at[p, cols[1]], height),
    ])
    own.wait()
    stage([
        ring("t", lambda k, p: rows_out.at[k, p, :], lambda p: rows_ref.at[p, :], rows_ref.shape[0]),
        ring("z", lambda k, p: out_ref.at[k, :, p, cols[0]], lambda p: out_ref.at[zi, :, p, cols[0]], height),
        ring("y", lambda k, p: out_ref.at[:, k, p, cols[1]], lambda p: out_ref.at[:, yi, p, cols[1]], height),
    ])
    own_rows.wait()
    for send in sends:
        send.wait_send()


def gather_blocks(piece, rows):
    ny, nz, nt = lax.axis_size("cy"), lax.axis_size("cz"), lax.axis_size("tp")
    height, width = piece.shape
    count = sum(2 * len(ring_steps(n)) for n in (ny, nz, nz, ny, nt))
    out, rows_out = pl.pallas_call(
        functools.partial(gather_kernel, ny, nz, nt),
        out_shape=(
            jax.ShapeDtypeStruct((nz, ny, height, width), piece.dtype),
            jax.ShapeDtypeStruct((nt,) + rows.shape, rows.dtype),
        ),
        in_specs=[pl.BlockSpec(memory_space=pltpu.VMEM)] * 2,
        out_specs=(pl.BlockSpec(memory_space=pl.ANY), pl.BlockSpec(memory_space=pl.ANY)),
        scratch_shapes=[
            pltpu.SemaphoreType.DMA((2,)),
            pltpu.SemaphoreType.DMA((count,)),
            pltpu.SemaphoreType.DMA((count,)),
        ],
        compiler_params=pltpu.CompilerParams(collective_id=1, has_side_effects=True),
    )(piece, rows)
    return out.reshape(nz * ny * height, width), rows_out.reshape(nt * rows.shape[0], rows.shape[1])


def scatter_kernel(nt, heads_ref, weight_ref, out_ref, send_buf, recv_buf, send_sems, recv_sems):
    tp = lax.axis_index("tp")
    rows = out_ref.shape[0]
    half = out_ref.shape[1] // 2

    barrier = pltpu.get_barrier_semaphore()
    for peer in (lax.rem(tp + 1, nt), lax.rem(tp + nt - 1, nt)):
        pl.semaphore_signal(barrier, 1, device_id=(lax.axis_index("cz"), lax.axis_index("cy"), peer), device_id_type=MESH_ID)

    def own(chunk, side):
        start = pl.multiple_of(chunk * rows, 16)
        part = lax.dot_general(
            heads_ref[pl.ds(start, rows), :],
            weight_ref[side * half : (side + 1) * half, :],
            (((1,), (1,)), ((), ())),
            preferred_element_type=jnp.float32,
        )
        return part.astype(jnp.bfloat16).astype(jnp.float32)

    def copy(side, step, peer):
        slot = side * nt + step
        return pltpu.make_async_remote_copy(
            src_ref=send_buf.at[slot], dst_ref=recv_buf.at[slot], send_sem=send_sems.at[slot],
            recv_sem=recv_sems.at[slot],
            device_id=(lax.axis_index("cz"), lax.axis_index("cy"), peer), device_id_type=MESH_ID,
        )

    sides = ((0, 1), (1, -1))
    first = [own(lax.rem(tp + nt * nt - sign, nt), side) for side, sign in sides]
    pl.semaphore_wait(barrier, 2)
    for step in range(1, nt):
        for side, sign in sides:
            chunk = lax.rem(tp + nt * nt - sign * step, nt)
            total = first[side] if step == 1 else own(chunk, side)
            if step > 1:
                copy(side, step - 1, lax.rem(tp + nt - sign, nt)).wait_recv()
                total = total + recv_buf[side * nt + step - 1].astype(jnp.float32)
            send_buf[side * nt + step] = total.astype(jnp.bfloat16)
            copy(side, step, lax.rem(tp + nt + sign, nt)).start()
    last = [own(tp, side) for side, _ in sides]
    for side, sign in sides:
        copy(side, nt - 1, lax.rem(tp + nt - sign, nt)).wait_recv()
        total = last[side] + recv_buf[side * nt + nt - 1].astype(jnp.float32)
        out_ref[:, side * half : (side + 1) * half] = total.astype(out_ref.dtype)
    for step in range(1, nt):
        for side, sign in sides:
            copy(side, step, lax.rem(tp + nt + sign, nt)).wait_send()


def scatter_rows(heads, weight):
    nt = lax.axis_size("tp")
    rows = heads.shape[0] // nt
    width = weight.shape[0]
    return pl.pallas_call(
        functools.partial(scatter_kernel, nt),
        out_shape=jax.ShapeDtypeStruct((rows, width), jnp.bfloat16),
        in_specs=[pl.BlockSpec(memory_space=pltpu.VMEM)] * 2,
        out_specs=pl.BlockSpec(memory_space=pltpu.VMEM),
        scratch_shapes=[
            pltpu.VMEM((2 * nt, rows, width // 2), jnp.bfloat16),
            pltpu.VMEM((2 * nt, rows, width // 2), jnp.bfloat16),
            pltpu.SemaphoreType.DMA((2 * nt,)),
            pltpu.SemaphoreType.DMA((2 * nt,)),
        ],
        compiler_params=pltpu.CompilerParams(
            collective_id=2, has_side_effects=True, vmem_limit_bytes=48 * 1024 * 1024
        ),
    )(heads, weight)


def rms_rows(embedded_entries, norm_gain):
    token_float = embedded_entries.astype(jnp.float32)
    moment = jnp.mean(token_float * token_float, axis=1, keepdims=True)
    return (token_float * lax.rsqrt(moment + EPSILON) * norm_gain).astype(jnp.bfloat16)


def local_terms(queries, key_rows, values, log_forget, input_gate, starts):
    length = queries.shape[0]
    scaling = queries.shape[1] ** (-0.5)
    segment = jnp.cumsum(starts)
    levels = jnp.cumsum(log_forget)
    position = jnp.arange(length)
    allowed = (position[:, None] >= position[None, :]) & (segment[:, None] == segment[None, :])
    decays = jnp.where(
        allowed,
        jnp.exp(jnp.minimum(levels[:, None] - levels[None, :], 0.0) + input_gate[None, :]),
        0.0,
    )
    scores = jnp.dot(queries, key_rows.T, preferred_element_type=jnp.float32) * scaling
    weights = (scores * decays).astype(jnp.bfloat16)
    inner_part = jnp.dot(weights, values, preferred_element_type=jnp.float32)
    last_level = levels[-1]
    last_seg = segment[-1]
    keeping = jnp.where(segment == last_seg, jnp.exp(last_level - levels + input_gate), 0.0)
    weighted = (key_rows.astype(jnp.float32) * keeping[:, None]).astype(jnp.bfloat16)
    local_state = lax.dot_general(
        weighted, values, (((0,), (0,)), ((), ())), preferred_element_type=jnp.float32
    )
    passing = jnp.where(last_seg == 0, jnp.exp(last_level), 0.0)
    carried = jnp.where(segment == 0, jnp.exp(levels), 0.0) * scaling
    return (inner_part, local_state, passing, carried)


def apply_state(queries, carried, incoming):
    lifted = queries.astype(jnp.float32) * carried[:, None]
    return jnp.dot(
        lifted, incoming, precision=lax.Precision.HIGHEST, preferred_element_type=jnp.float32
    )


def head_norm(head_out, gain):
    centre = jnp.mean(head_out, axis=1, keepdims=True)
    shifted = head_out - centre
    spread = jnp.mean(shifted * shifted, axis=1, keepdims=True)
    return (shifted * lax.rsqrt(spread + EPSILON) * gain).astype(jnp.bfloat16)


def local(
    tokens,
    norm_gain,
    w_qkv,
    w_out,
    head_gain,
    input_codes,
    forget_codes,
    forget_bias,
    document_begin_flags,
):
    normed = rms_rows(tokens, norm_gain)
    width = w_qkv.shape[1]
    both, every_row_list = gather_blocks(jnp.concatenate([w_qkv, w_out.T], axis=1), normed)
    parameter_collection = both[:, :width]
    out_rows = both[:, width:]
    rows_combined = jnp.dot(
        every_row_list, parameter_collection, preferred_element_type=jnp.float32
    )
    rows_combined = rows_combined.astype(jnp.bfloat16)
    heads_here = forget_bias.shape[0]
    stride = 2 * DK + DV
    query_list, inner_list, state_list, passing_list, carried_list = ([], [], [], [], [])
    attention_slot_number = 0
    offset = attention_slot_number * stride
    queries = rows_combined[:, offset : offset + DK]
    key_rows = rows_combined[:, offset + DK : offset + 2 * DK]
    values = rows_combined[:, offset + 2 * DK : offset + stride]
    log_forget = jax.nn.log_sigmoid(
        FORGET_STEP * forget_codes[attention_slot_number].astype(jnp.float32)
        + forget_bias[attention_slot_number]
    )
    input_gate = INPUT_STEP * input_codes[attention_slot_number].astype(jnp.float32)
    inner_part, local_state, passing, carried = local_terms(
        queries, key_rows, values, log_forget, input_gate, document_begin_flags
    )
    query_list.append(queries)
    inner_list.append(inner_part)
    state_list.append(local_state)
    passing_list.append(passing)
    carried_list.append(carried)
    incoming = carried_in(passing_list[0], state_list[0])[None]
    attention_slot_number = 0
    head_out = inner_list[attention_slot_number] + apply_state(
        query_list[attention_slot_number],
        carried_list[attention_slot_number],
        incoming[attention_slot_number],
    )
    normed_heads = head_norm(head_out, head_gain)
    summed = scatter_rows(normed_heads, out_rows).astype(jnp.float32)
    return (tokens.astype(jnp.float32) + summed).astype(jnp.bfloat16)


def solution(mesh):
    z_rows = 4 if mesh.shape["ctx"] % 4 == 0 else 1
    split = jax.sharding.Mesh(
        mesh.devices.reshape(mesh.shape["ctx"] // z_rows, z_rows, mesh.shape["tp"]), ("cz", "cy", "tp")
    )
    blocks = ("cz", "cy")
    placed = (
        P(blocks + ("tp",), None),
        P(),
        P(blocks, "tp"),
        P("tp", blocks),
        P("tp"),
        P("tp", blocks),
        P("tp", blocks),
        P("tp"),
        P(blocks),
    )
    return jax.shard_map(
        local, mesh=split, in_specs=placed, out_specs=P(blocks + ("tp",), None), check_vma=False
    )
```

```python
import functools

import jax
import jax.numpy as jnp
from jax import lax
from jax.experimental import pallas as pl
from jax.experimental.pallas import tpu as pltpu
from jax.sharding import PartitionSpec as P

DK = 256
DV = 512


EPSILON = 1e-06
FORGET_STEP = 0.5
INPUT_STEP = 0.5


MESH_ID = pl.DeviceIdType.MESH
DECAY_ROWS = 16


def scan_shifts(count):
    shifts = [1] + ([2] if count > 2 else [])
    k = 2
    while k < count:
        shifts.append(k)
        k *= 2
    return shifts


def pack(ref, total, decay):
    rows = total.shape[0]
    high = decay.astype(jnp.bfloat16)
    ref[:rows, :] = total.astype(jnp.bfloat16)
    ref[rows : rows + DECAY_ROWS, :] = high
    ref[rows + DECAY_ROWS :, :] = (decay - high.astype(jnp.float32)).astype(jnp.bfloat16)


def absorb(got, rows, acc_total, acc_decay):
    far_total = got[:rows].astype(jnp.float32)
    far_decay = got[rows : rows + DECAY_ROWS].astype(jnp.float32) + got[rows + DECAY_ROWS :].astype(jnp.float32)
    decay = acc_decay[...]
    acc_total[...] = decay[0:1, :] * far_total + acc_total[...]
    acc_decay[...] = decay * far_decay


def extend(got, rows, acc_total, acc_decay):
    far_total = got[:rows].astype(jnp.float32)
    far_decay = got[rows : rows + DECAY_ROWS].astype(jnp.float32) + got[rows + DECAY_ROWS :].astype(jnp.float32)
    acc_total[...] = far_decay[0:1, :] * acc_total[...] + far_total
    acc_decay[...] = far_decay * acc_decay[...]


def scan_kernel(
    ny, nz, zshifts, state_ref, decay_ref, out_ref,
    row_send, row_recv, z_send, z_recv, c_send, c_recv,
    prefix_total, prefix_decay, quarter_total, quarter_decay, z_total, z_decay,
    row_send_sems, row_recv_sems, z_send_sems, z_recv_sems, c_send_sems, c_recv_sems,
):
    yi = lax.axis_index("cy")
    zi = lax.axis_index("cz")
    tp = lax.axis_index("tp")
    rows, width = state_ref.shape
    quarter = width // ny

    barrier = pltpu.get_barrier_semaphore()
    z_partners = sorted(set(zshifts))
    for d in range(1, ny):
        pl.semaphore_signal(barrier, 1, device_id=(zi, lax.rem(yi + d, ny), tp), device_id_type=MESH_ID)
    for s in z_partners:
        for peer in (lax.rem(zi + s, nz), lax.rem(zi + nz - s, nz)):
            pl.semaphore_signal(barrier, 1, device_id=(peer, yi, tp), device_id_type=MESH_ID)
    pl.semaphore_wait(barrier, (ny - 1) + 2 * len(z_partners))

    def row_copy(d, target, slot, part):
        return pltpu.make_async_remote_copy(
            src_ref=row_send.at[part], dst_ref=row_recv.at[slot], send_sem=row_send_sems.at[d],
            recv_sem=row_recv_sems.at[slot], device_id=(zi, target, tp), device_id_type=MESH_ID,
        )

    for y in range(ny):
        pack(row_send.at[y], state_ref[:, y * quarter : (y + 1) * quarter], decay_ref[:, y * quarter : (y + 1) * quarter])
    for d in range(1, ny):
        target = lax.rem(yi + d, ny)
        row_copy(d, target, yi, target).start()
    for d in range(1, ny):
        row_copy(d, yi, lax.rem(yi + ny - d, ny), yi).wait_recv()

    quarter_total[...] = jnp.zeros_like(quarter_total)
    quarter_decay[...] = jnp.ones_like(quarter_decay)
    for y in range(ny):
        prefix_total[y] = quarter_total[...]
        prefix_decay[y] = quarter_decay[...]

        @pl.when(yi == y)
        def _():
            extend(row_send[y], rows, quarter_total, quarter_decay)

        @pl.when(yi != y)
        def _():
            extend(row_recv[y], rows, quarter_total, quarter_decay)

    def z_copy(j, slot, peer):
        return pltpu.make_async_remote_copy(
            src_ref=z_send.at[slot], dst_ref=z_recv.at[j], send_sem=z_send_sems.at[j],
            recv_sem=z_recv_sems.at[j], device_id=(peer, yi, tp), device_id_type=MESH_ID,
        )

    def z_send_round(j, slot):
        @pl.when(zi + zshifts[j] < nz)
        def _():
            z_copy(j, slot, zi + zshifts[j]).start()

    def z_absorb(j, slot):
        @pl.when(zi - zshifts[j] >= 0)
        def _():
            z_copy(j, slot, zi - zshifts[j]).wait_recv()
            absorb(z_recv[j], rows, z_total, z_decay)

    z_total[...] = jnp.zeros_like(z_total)
    z_decay[...] = jnp.ones_like(z_decay)
    first = min(2, len(zshifts))
    if zshifts:
        pack(z_send.at[0], quarter_total[...], quarter_decay[...])
    for j in range(first):
        z_send_round(j, 0)
    for j in range(first):
        z_absorb(j, 0)
    for j in range(first, len(zshifts)):
        pack(z_send.at[j - 1], z_total[...], z_decay[...])
        z_send_round(j, j - 1)
        z_absorb(j, j - 1)

    def c_copy(y, target, slot):
        return pltpu.make_async_remote_copy(
            src_ref=c_send.at[y], dst_ref=c_recv.at[slot], send_sem=c_send_sems.at[y],
            recv_sem=c_recv_sems.at[slot], device_id=(zi, target, tp), device_id_type=MESH_ID,
        )

    for y in range(ny):
        done = prefix_decay[y][0:1, :] * z_total[...] + prefix_total[y]

        @pl.when(yi == y)
        def _():
            out_ref[:, y * quarter : (y + 1) * quarter] = done

        @pl.when(yi != y)
        def _():
            c_send[y] = done.astype(jnp.bfloat16)
            c_copy(y, y, yi).start()

    for y in range(ny):
        @pl.when(yi != y)
        def _():
            c_copy(y, yi, y).wait_recv()
            out_ref[:, y * quarter : (y + 1) * quarter] = c_recv[y].astype(jnp.float32)

    for d in range(1, ny):
        target = lax.rem(yi + d, ny)
        row_copy(d, target, yi, target).wait_send()
    for y in range(ny):
        @pl.when(yi != y)
        def _():
            c_copy(y, y, yi).wait_send()
    for j in range(len(zshifts)):
        @pl.when(zi + zshifts[j] < nz)
        def _():
            z_copy(j, 0 if j < first else j - 1, zi + zshifts[j]).wait_send()


def carried_in(passing, state):
    ny, nz = lax.axis_size("cy"), lax.axis_size("cz")
    if ny * nz == 1:
        return jnp.zeros_like(state)
    zshifts = scan_shifts(nz) if nz > 1 else []
    rows, width = state.shape
    quarter = width // ny
    decay = jnp.broadcast_to(passing.reshape(1, 1), (DECAY_ROWS, width)).astype(jnp.float32)
    message = rows + 2 * DECAY_ROWS
    slots = max(len(zshifts), 1)
    return pl.pallas_call(
        functools.partial(scan_kernel, ny, nz, zshifts),
        out_shape=jax.ShapeDtypeStruct((rows, width), jnp.float32),
        in_specs=[pl.BlockSpec(memory_space=pltpu.VMEM)] * 2,
        out_specs=pl.BlockSpec(memory_space=pltpu.VMEM),
        scratch_shapes=[
            pltpu.VMEM((ny, message, quarter), jnp.bfloat16),
            pltpu.VMEM((ny, message, quarter), jnp.bfloat16),
            pltpu.VMEM((slots, message, quarter), jnp.bfloat16),
            pltpu.VMEM((slots, message, quarter), jnp.bfloat16),
            pltpu.VMEM((ny, rows, quarter), jnp.bfloat16),
            pltpu.VMEM((ny, rows, quarter), jnp.bfloat16),
            pltpu.VMEM((ny, rows, quarter), jnp.float32),
            pltpu.VMEM((ny, DECAY_ROWS, quarter), jnp.float32),
            pltpu.VMEM((rows, quarter), jnp.float32),
            pltpu.VMEM((DECAY_ROWS, quarter), jnp.float32),
            pltpu.VMEM((rows, quarter), jnp.float32),
            pltpu.VMEM((DECAY_ROWS, quarter), jnp.float32),
            pltpu.SemaphoreType.DMA((ny,)),
            pltpu.SemaphoreType.DMA((ny,)),
            pltpu.SemaphoreType.DMA((slots,)),
            pltpu.SemaphoreType.DMA((slots,)),
            pltpu.SemaphoreType.DMA((ny,)),
            pltpu.SemaphoreType.DMA((ny,)),
        ],
        compiler_params=pltpu.CompilerParams(collective_id=0, has_side_effects=True),
    )(state.astype(jnp.float32), decay)


def ring_steps(n):
    steps = [(s, True) for s in range(1, (n - 1) // 2 + 1)]
    if n % 2 == 0 and n > 1:
        steps.append((n // 2, False))
    return steps


def gather_kernel(ny, nz, nt, piece_ref, rows_ref, out_ref, rows_out, local_sem, send_sems, recv_sems):
    yi = lax.axis_index("cy")
    zi = lax.axis_index("cz")
    tp = lax.axis_index("tp")
    half = piece_ref.shape[1] // 2
    cols = (pl.ds(0, half), pl.ds(half, half))

    barrier = pltpu.get_barrier_semaphore()
    neighbours = [
        (zi, lax.rem(yi + 1, ny), tp),
        (zi, lax.rem(yi + ny - 1, ny), tp),
        (lax.rem(zi + 1, nz), yi, tp),
        (lax.rem(zi + nz - 1, nz), yi, tp),
        (zi, yi, lax.rem(tp + 1, nt)),
        (zi, yi, lax.rem(tp + nt - 1, nt)),
    ]
    for peer in neighbours:
        pl.semaphore_signal(barrier, 1, device_id=peer, device_id_type=MESH_ID)
    pl.semaphore_wait(barrier, len(neighbours))

    own = pltpu.make_async_copy(piece_ref, out_ref.at[zi, yi], local_sem.at[0])
    own.start()
    own_rows = pltpu.make_async_copy(rows_ref, rows_out.at[tp], local_sem.at[1])
    own_rows.start()
    sends = []

    def ring(along, group_of, first_src, height):
        n, me = {"y": (ny, yi), "z": (nz, zi), "t": (nt, tp)}[along]
        return dict(n=n, me=me, along=along, group_of=group_of, first_src=first_src, steps=ring_steps(n), last={}, height=height)

    def device(r, k):
        return {"y": (zi, k, tp), "z": (k, yi, tp), "t": (zi, yi, k)}[r["along"]]

    def step(r, t):
        if t > len(r["steps"]):
            return
        n, me, group_of = r["n"], r["me"], r["group_of"]
        hop, both = r["steps"][t - 1]
        whole = slice(None)
        half_rows = r["height"] // 2
        for sign in (1, -1):
            if both:
                part = whole
            else:
                part = pl.ds(0, half_rows) if sign == 1 else pl.ds(half_rows, half_rows)
            if t > 1:
                r["last"].pop(sign).wait_recv()
            origin = lax.rem(me + 2 * n - sign * (hop - 1), n)
            target = lax.rem(me + n + sign, n)
            source = lax.rem(me + n - sign, n)
            arrived = lax.rem(me + 2 * n - sign * hop, n)
            idx = len(sends)
            send = pltpu.make_async_remote_copy(
                src_ref=r["first_src"](part) if t == 1 else group_of(origin, part), dst_ref=group_of(origin, part),
                send_sem=send_sems.at[idx], recv_sem=recv_sems.at[idx],
                device_id=device(r, target), device_id_type=MESH_ID,
            )
            incoming = pltpu.make_async_remote_copy(
                src_ref=group_of(arrived, part), dst_ref=group_of(arrived, part),
                send_sem=send_sems.at[idx], recv_sem=recv_sems.at[idx],
                device_id=device(r, source), device_id_type=MESH_ID,
            )
            send.start()
            sends.append(send)
            r["last"][sign] = incoming

    def stage(rings):
        for t in range(1, max(len(r["steps"]) for r in rings) + 1):
            for r in rings:
                step(r, t)
        for r in rings:
            for incoming in r["last"].values():
                incoming.wait_recv()

    height = piece_ref.shape[0]
    stage([
        ring("y", lambda k, p: out_ref.at[zi, k, p, cols[0]], lambda p: piece_ref.at[p, cols[0]], height),
        ring("z", lambda k, p: out_ref.at[k, yi, p, cols[1]], lambda p: piece_ref.at[p, cols[1]], height),
    ])
    own.wait()
    stage([
        ring("t", lambda k, p: rows_out.at[k, p, :], lambda p: rows_ref.at[p, :], rows_ref.shape[0]),
        ring("z", lambda k, p: out_ref.at[k, :, p, cols[0]], lambda p: out_ref.at[zi, :, p, cols[0]], height),
        ring("y", lambda k, p: out_ref.at[:, k, p, cols[1]], lambda p: out_ref.at[:, yi, p, cols[1]], height),
    ])
    own_rows.wait()
    for send in sends:
        send.wait_send()


def gather_blocks(piece, rows):
    ny, nz, nt = lax.axis_size("cy"), lax.axis_size("cz"), lax.axis_size("tp")
    height, width = piece.shape
    count = sum(2 * len(ring_steps(n)) for n in (ny, nz, nz, ny, nt))
    out, rows_out = pl.pallas_call(
        functools.partial(gather_kernel, ny, nz, nt),
        out_shape=(
            jax.ShapeDtypeStruct((nz, ny, height, width), piece.dtype),
            jax.ShapeDtypeStruct((nt,) + rows.shape, rows.dtype),
        ),
        in_specs=[pl.BlockSpec(memory_space=pltpu.VMEM)] * 2,
        out_specs=(pl.BlockSpec(memory_space=pl.ANY), pl.BlockSpec(memory_space=pl.ANY)),
        scratch_shapes=[
            pltpu.SemaphoreType.DMA((2,)),
            pltpu.SemaphoreType.DMA((count,)),
            pltpu.SemaphoreType.DMA((count,)),
        ],
        compiler_params=pltpu.CompilerParams(collective_id=1, has_side_effects=True),
    )(piece, rows)
    return out.reshape(nz * ny * height, width), rows_out.reshape(nt * rows.shape[0], rows.shape[1])


def scatter_kernel(nt, heads_ref, weight_ref, out_ref, send_buf, recv_buf, send_sems, recv_sems):
    tp = lax.axis_index("tp")
    rows = out_ref.shape[0]
    half = out_ref.shape[1] // 2

    barrier = pltpu.get_barrier_semaphore()
    for peer in (lax.rem(tp + 1, nt), lax.rem(tp + nt - 1, nt)):
        pl.semaphore_signal(barrier, 1, device_id=(lax.axis_index("cz"), lax.axis_index("cy"), peer), device_id_type=MESH_ID)

    def own(chunk, side):
        start = pl.multiple_of(chunk * rows, 16)
        part = lax.dot_general(
            heads_ref[pl.ds(start, rows), :],
            weight_ref[side * half : (side + 1) * half, :],
            (((1,), (1,)), ((), ())),
            preferred_element_type=jnp.float32,
        )
        return part.astype(jnp.bfloat16).astype(jnp.float32)

    def copy(side, step, peer):
        slot = side * nt + step
        return pltpu.make_async_remote_copy(
            src_ref=send_buf.at[slot], dst_ref=recv_buf.at[slot], send_sem=send_sems.at[slot],
            recv_sem=recv_sems.at[slot],
            device_id=(lax.axis_index("cz"), lax.axis_index("cy"), peer), device_id_type=MESH_ID,
        )

    sides = ((0, 1), (1, -1))
    first = [own(lax.rem(tp + nt * nt - sign, nt), side) for side, sign in sides]
    pl.semaphore_wait(barrier, 2)
    for step in range(1, nt):
        mine = first if step == 1 else [
            own(lax.rem(tp + nt * nt - sign * step, nt), side) for side, sign in sides
        ]
        for side, sign in sides:
            total = mine[side]
            if step > 1:
                copy(side, step - 1, lax.rem(tp + nt - sign, nt)).wait_recv()
                total = total + recv_buf[side * nt + step - 1].astype(jnp.float32)
            send_buf[side * nt + step] = total.astype(jnp.bfloat16)
            copy(side, step, lax.rem(tp + nt + sign, nt)).start()
    last = [own(tp, side) for side, _ in sides]
    for side, sign in sides:
        copy(side, nt - 1, lax.rem(tp + nt - sign, nt)).wait_recv()
        total = last[side] + recv_buf[side * nt + nt - 1].astype(jnp.float32)
        out_ref[:, side * half : (side + 1) * half] = total.astype(out_ref.dtype)
    for step in range(1, nt):
        for side, sign in sides:
            copy(side, step, lax.rem(tp + nt + sign, nt)).wait_send()


def scatter_rows(heads, weight):
    nt = lax.axis_size("tp")
    rows = heads.shape[0] // nt
    width = weight.shape[0]
    return pl.pallas_call(
        functools.partial(scatter_kernel, nt),
        out_shape=jax.ShapeDtypeStruct((rows, width), jnp.bfloat16),
        in_specs=[pl.BlockSpec(memory_space=pltpu.VMEM)] * 2,
        out_specs=pl.BlockSpec(memory_space=pltpu.VMEM),
        scratch_shapes=[
            pltpu.VMEM((2 * nt, rows, width // 2), jnp.bfloat16),
            pltpu.VMEM((2 * nt, rows, width // 2), jnp.bfloat16),
            pltpu.SemaphoreType.DMA((2 * nt,)),
            pltpu.SemaphoreType.DMA((2 * nt,)),
        ],
        compiler_params=pltpu.CompilerParams(
            collective_id=2, has_side_effects=True, vmem_limit_bytes=48 * 1024 * 1024
        ),
    )(heads, weight)


def rms_rows(embedded_entries, norm_gain):
    token_float = embedded_entries.astype(jnp.float32)
    moment = jnp.mean(token_float * token_float, axis=1, keepdims=True)
    return (token_float * lax.rsqrt(moment + EPSILON) * norm_gain).astype(jnp.bfloat16)


def local_terms(queries, key_rows, values, log_forget, input_gate, starts):
    length = queries.shape[0]
    scaling = queries.shape[1] ** (-0.5)
    segment = jnp.cumsum(starts)
    levels = jnp.cumsum(log_forget)
    position = jnp.arange(length)
    allowed = (position[:, None] >= position[None, :]) & (segment[:, None] == segment[None, :])
    decays = jnp.where(
        allowed,
        jnp.exp(jnp.minimum(levels[:, None] - levels[None, :], 0.0) + input_gate[None, :]),
        0.0,
    )
    scores = jnp.dot(queries, key_rows.T, preferred_element_type=jnp.float32) * scaling
    weights = (scores * decays).astype(jnp.bfloat16)
    inner_part = jnp.dot(weights, values, preferred_element_type=jnp.float32)
    last_level = levels[-1]
    last_seg = segment[-1]
    keeping = jnp.where(segment == last_seg, jnp.exp(last_level - levels + input_gate), 0.0)
    weighted = (key_rows.astype(jnp.float32) * keeping[:, None]).astype(jnp.bfloat16)
    local_state = lax.dot_general(
        weighted, values, (((0,), (0,)), ((), ())), preferred_element_type=jnp.float32
    )
    passing = jnp.where(last_seg == 0, jnp.exp(last_level), 0.0)
    carried = jnp.where(segment == 0, jnp.exp(levels), 0.0) * scaling
    return (inner_part, local_state, passing, carried)


def apply_state(queries, carried, incoming):
    lifted = queries.astype(jnp.float32) * carried[:, None]
    return jnp.dot(
        lifted, incoming, precision=lax.Precision.HIGHEST, preferred_element_type=jnp.float32
    )


def head_norm(head_out, gain):
    centre = jnp.mean(head_out, axis=1, keepdims=True)
    shifted = head_out - centre
    spread = jnp.mean(shifted * shifted, axis=1, keepdims=True)
    return (shifted * lax.rsqrt(spread + EPSILON) * gain).astype(jnp.bfloat16)


def local(
    tokens,
    norm_gain,
    w_qkv,
    w_out,
    head_gain,
    input_codes,
    forget_codes,
    forget_bias,
    document_begin_flags,
):
    normed = rms_rows(tokens, norm_gain)
    width = w_qkv.shape[1]
    both, every_row_list = gather_blocks(jnp.concatenate([w_qkv, w_out.T], axis=1), normed)
    parameter_collection = both[:, :width]
    out_rows = both[:, width:]
    rows_combined = jnp.dot(
        every_row_list, parameter_collection, preferred_element_type=jnp.float32
    )
    rows_combined = rows_combined.astype(jnp.bfloat16)
    heads_here = forget_bias.shape[0]
    stride = 2 * DK + DV
    query_list, inner_list, state_list, passing_list, carried_list = ([], [], [], [], [])
    attention_slot_number = 0
    offset = attention_slot_number * stride
    queries = rows_combined[:, offset : offset + DK]
    key_rows = rows_combined[:, offset + DK : offset + 2 * DK]
    values = rows_combined[:, offset + 2 * DK : offset + stride]
    log_forget = jax.nn.log_sigmoid(
        FORGET_STEP * forget_codes[attention_slot_number].astype(jnp.float32)
        + forget_bias[attention_slot_number]
    )
    input_gate = INPUT_STEP * input_codes[attention_slot_number].astype(jnp.float32)
    inner_part, local_state, passing, carried = local_terms(
        queries, key_rows, values, log_forget, input_gate, document_begin_flags
    )
    query_list.append(queries)
    inner_list.append(inner_part)
    state_list.append(local_state)
    passing_list.append(passing)
    carried_list.append(carried)
    incoming = carried_in(passing_list[0], state_list[0])[None]
    attention_slot_number = 0
    head_out = inner_list[attention_slot_number] + apply_state(
        query_list[attention_slot_number],
        carried_list[attention_slot_number],
        incoming[attention_slot_number],
    )
    normed_heads = head_norm(head_out, head_gain)
    summed = scatter_rows(normed_heads, out_rows).astype(jnp.float32)
    return (tokens.astype(jnp.float32) + summed).astype(jnp.bfloat16)


def solution(mesh):
    z_rows = 4 if mesh.shape["ctx"] % 4 == 0 else 1
    split = jax.sharding.Mesh(
        mesh.devices.reshape(mesh.shape["ctx"] // z_rows, z_rows, mesh.shape["tp"]), ("cz", "cy", "tp")
    )
    blocks = ("cz", "cy")
    placed = (
        P(blocks + ("tp",), None),
        P(),
        P(blocks, "tp"),
        P("tp", blocks),
        P("tp"),
        P("tp", blocks),
        P("tp", blocks),
        P("tp"),
        P(blocks),
    )
    return jax.shard_map(
        local, mesh=split, in_specs=placed, out_specs=P(blocks + ("tp",), None), check_vma=False
    )
```

```python
import functools

import jax
import jax.numpy as jnp
from jax import lax
from jax.experimental import pallas as pl
from jax.experimental.pallas import tpu as pltpu
from jax.sharding import PartitionSpec as P

DK = 256
DV = 512


EPSILON = 1e-06
FORGET_STEP = 0.5
INPUT_STEP = 0.5


MESH_ID = pl.DeviceIdType.MESH
DECAY_ROWS = 16


def scan_shifts(count):
    shifts = [1] + ([2] if count > 2 else [])
    k = 2
    while k < count:
        shifts.append(k)
        k *= 2
    return shifts


def pack(ref, total, decay):
    rows = total.shape[0]
    high = decay.astype(jnp.bfloat16)
    ref[:rows, :] = total.astype(jnp.bfloat16)
    ref[rows : rows + DECAY_ROWS, :] = high
    ref[rows + DECAY_ROWS :, :] = (decay - high.astype(jnp.float32)).astype(jnp.bfloat16)


def absorb(got, rows, acc_total, acc_decay):
    far_total = got[:rows].astype(jnp.float32)
    far_decay = got[rows : rows + DECAY_ROWS].astype(jnp.float32) + got[rows + DECAY_ROWS :].astype(jnp.float32)
    decay = acc_decay[...]
    acc_total[...] = decay[0:1, :] * far_total + acc_total[...]
    acc_decay[...] = decay * far_decay


def extend(got, rows, acc_total, acc_decay):
    far_total = got[:rows].astype(jnp.float32)
    far_decay = got[rows : rows + DECAY_ROWS].astype(jnp.float32) + got[rows + DECAY_ROWS :].astype(jnp.float32)
    acc_total[...] = far_decay[0:1, :] * acc_total[...] + far_total
    acc_decay[...] = far_decay * acc_decay[...]


def scan_kernel(
    ny, nz, zshifts, state_ref, decay_ref, out_ref,
    row_send, row_recv, z_send, z_recv, c_send, c_recv,
    prefix_total, prefix_decay, quarter_total, quarter_decay, z_total, z_decay,
    row_send_sems, row_recv_sems, z_send_sems, z_recv_sems, c_send_sems, c_recv_sems,
):
    yi = lax.axis_index("cy")
    zi = lax.axis_index("cz")
    tp = lax.axis_index("tp")
    rows, width = state_ref.shape
    quarter = width // ny

    barrier = pltpu.get_barrier_semaphore()
    z_partners = sorted(set(zshifts))
    for d in range(1, ny):
        pl.semaphore_signal(barrier, 1, device_id=(zi, lax.rem(yi + d, ny), tp), device_id_type=MESH_ID)
    for s in z_partners:
        for peer in (lax.rem(zi + s, nz), lax.rem(zi + nz - s, nz)):
            pl.semaphore_signal(barrier, 1, device_id=(peer, yi, tp), device_id_type=MESH_ID)
    pl.semaphore_wait(barrier, (ny - 1) + 2 * len(z_partners))

    def row_copy(d, target, slot, part):
        return pltpu.make_async_remote_copy(
            src_ref=row_send.at[part], dst_ref=row_recv.at[slot], send_sem=row_send_sems.at[d],
            recv_sem=row_recv_sems.at[slot], device_id=(zi, target, tp), device_id_type=MESH_ID,
        )

    for y in range(ny):
        pack(row_send.at[y], state_ref[:, y * quarter : (y + 1) * quarter], decay_ref[:, y * quarter : (y + 1) * quarter])
    for d in range(1, ny):
        target = lax.rem(yi + d, ny)
        row_copy(d, target, yi, target).start()
    for d in range(1, ny):
        row_copy(d, yi, lax.rem(yi + ny - d, ny), yi).wait_recv()

    quarter_total[...] = jnp.zeros_like(quarter_total)
    quarter_decay[...] = jnp.ones_like(quarter_decay)
    for y in range(ny):
        prefix_total[y] = quarter_total[...]
        prefix_decay[y] = quarter_decay[...]

        @pl.when(yi == y)
        def _():
            extend(row_send[y], rows, quarter_total, quarter_decay)

        @pl.when(yi != y)
        def _():
            extend(row_recv[y], rows, quarter_total, quarter_decay)

    def z_copy(j, slot, peer):
        return pltpu.make_async_remote_copy(
            src_ref=z_send.at[slot], dst_ref=z_recv.at[j], send_sem=z_send_sems.at[j],
            recv_sem=z_recv_sems.at[j], device_id=(peer, yi, tp), device_id_type=MESH_ID,
        )

    def z_send_round(j, slot):
        @pl.when(zi + zshifts[j] < nz)
        def _():
            z_copy(j, slot, zi + zshifts[j]).start()

    def z_absorb(j, slot):
        @pl.when(zi - zshifts[j] >= 0)
        def _():
            z_copy(j, slot, zi - zshifts[j]).wait_recv()
            absorb(z_recv[j], rows, z_total, z_decay)

    z_total[...] = jnp.zeros_like(z_total)
    z_decay[...] = jnp.ones_like(z_decay)
    first = min(2, len(zshifts))
    if zshifts:
        pack(z_send.at[0], quarter_total[...], quarter_decay[...])
    for j in range(first):
        z_send_round(j, 0)
    for j in range(first):
        z_absorb(j, 0)
    for j in range(first, len(zshifts)):
        pack(z_send.at[j - 1], z_total[...], z_decay[...])
        z_send_round(j, j - 1)
        z_absorb(j, j - 1)

    def c_copy(y, target, slot):
        return pltpu.make_async_remote_copy(
            src_ref=c_send.at[y], dst_ref=c_recv.at[slot], send_sem=c_send_sems.at[y],
            recv_sem=c_recv_sems.at[slot], device_id=(zi, target, tp), device_id_type=MESH_ID,
        )

    for y in range(ny):
        done = prefix_decay[y][0:1, :] * z_total[...] + prefix_total[y]

        @pl.when(yi == y)
        def _():
            out_ref[:, y * quarter : (y + 1) * quarter] = done

        @pl.when(yi != y)
        def _():
            c_send[y] = done.astype(jnp.bfloat16)
            c_copy(y, y, yi).start()

    for y in range(ny):
        @pl.when(yi != y)
        def _():
            c_copy(y, yi, y).wait_recv()
            out_ref[:, y * quarter : (y + 1) * quarter] = c_recv[y].astype(jnp.float32)

    for d in range(1, ny):
        target = lax.rem(yi + d, ny)
        row_copy(d, target, yi, target).wait_send()
    for y in range(ny):
        @pl.when(yi != y)
        def _():
            c_copy(y, y, yi).wait_send()
    for j in range(len(zshifts)):
        @pl.when(zi + zshifts[j] < nz)
        def _():
            z_copy(j, 0 if j < first else j - 1, zi + zshifts[j]).wait_send()


def carried_in(passing, state):
    ny, nz = lax.axis_size("cy"), lax.axis_size("cz")
    if ny * nz == 1:
        return jnp.zeros_like(state)
    zshifts = scan_shifts(nz) if nz > 1 else []
    rows, width = state.shape
    quarter = width // ny
    decay = jnp.broadcast_to(passing.reshape(1, 1), (DECAY_ROWS, width)).astype(jnp.float32)
    message = rows + 2 * DECAY_ROWS
    slots = max(len(zshifts), 1)
    return pl.pallas_call(
        functools.partial(scan_kernel, ny, nz, zshifts),
        out_shape=jax.ShapeDtypeStruct((rows, width), jnp.float32),
        in_specs=[pl.BlockSpec(memory_space=pltpu.VMEM)] * 2,
        out_specs=pl.BlockSpec(memory_space=pltpu.VMEM),
        scratch_shapes=[
            pltpu.VMEM((ny, message, quarter), jnp.bfloat16),
            pltpu.VMEM((ny, message, quarter), jnp.bfloat16),
            pltpu.VMEM((slots, message, quarter), jnp.bfloat16),
            pltpu.VMEM((slots, message, quarter), jnp.bfloat16),
            pltpu.VMEM((ny, rows, quarter), jnp.bfloat16),
            pltpu.VMEM((ny, rows, quarter), jnp.bfloat16),
            pltpu.VMEM((ny, rows, quarter), jnp.float32),
            pltpu.VMEM((ny, DECAY_ROWS, quarter), jnp.float32),
            pltpu.VMEM((rows, quarter), jnp.float32),
            pltpu.VMEM((DECAY_ROWS, quarter), jnp.float32),
            pltpu.VMEM((rows, quarter), jnp.float32),
            pltpu.VMEM((DECAY_ROWS, quarter), jnp.float32),
            pltpu.SemaphoreType.DMA((ny,)),
            pltpu.SemaphoreType.DMA((ny,)),
            pltpu.SemaphoreType.DMA((slots,)),
            pltpu.SemaphoreType.DMA((slots,)),
            pltpu.SemaphoreType.DMA((ny,)),
            pltpu.SemaphoreType.DMA((ny,)),
        ],
        compiler_params=pltpu.CompilerParams(collective_id=0, has_side_effects=True),
    )(state.astype(jnp.float32), decay)


def ring_steps(n):
    steps = [(s, True) for s in range(1, (n - 1) // 2 + 1)]
    if n % 2 == 0 and n > 1:
        steps.append((n // 2, False))
    return steps


def gather_kernel(ny, nz, nt, piece_ref, rows_ref, out_ref, rows_out, local_sem, send_sems, recv_sems):
    yi = lax.axis_index("cy")
    zi = lax.axis_index("cz")
    tp = lax.axis_index("tp")
    half = piece_ref.shape[1] // 2
    cols = (pl.ds(0, half), pl.ds(half, half))

    barrier = pltpu.get_barrier_semaphore()
    neighbours = [
        (zi, lax.rem(yi + 1, ny), tp),
        (zi, lax.rem(yi + ny - 1, ny), tp),
        (lax.rem(zi + 1, nz), yi, tp),
        (lax.rem(zi + nz - 1, nz), yi, tp),
        (zi, yi, lax.rem(tp + 1, nt)),
        (zi, yi, lax.rem(tp + nt - 1, nt)),
    ]
    for peer in neighbours:
        pl.semaphore_signal(barrier, 1, device_id=peer, device_id_type=MESH_ID)
    pl.semaphore_wait(barrier, len(neighbours))

    own = pltpu.make_async_copy(piece_ref, out_ref.at[zi, yi], local_sem.at[0])
    own.start()
    own_rows = pltpu.make_async_copy(rows_ref, rows_out.at[tp], local_sem.at[1])
    own_rows.start()
    sends = []

    def ring(along, group_of, first_src, height):
        n, me = {"y": (ny, yi), "z": (nz, zi), "t": (nt, tp)}[along]
        return dict(n=n, me=me, along=along, group_of=group_of, first_src=first_src, steps=ring_steps(n), last={}, height=height)

    def device(r, k):
        return {"y": (zi, k, tp), "z": (k, yi, tp), "t": (zi, yi, k)}[r["along"]]

    def step(r, t):
        if t > len(r["steps"]):
            return
        n, me, group_of = r["n"], r["me"], r["group_of"]
        hop, both = r["steps"][t - 1]
        whole = slice(None)
        half_rows = r["height"] // 2
        for sign in (1, -1):
            if both:
                part = whole
            else:
                part = pl.ds(0, half_rows) if sign == 1 else pl.ds(half_rows, half_rows)
            if t > 1:
                r["last"].pop(sign).wait_recv()
            origin = lax.rem(me + 2 * n - sign * (hop - 1), n)
            target = lax.rem(me + n + sign, n)
            source = lax.rem(me + n - sign, n)
            arrived = lax.rem(me + 2 * n - sign * hop, n)
            idx = len(sends)
            send = pltpu.make_async_remote_copy(
                src_ref=r["first_src"](part) if t == 1 else group_of(origin, part), dst_ref=group_of(origin, part),
                send_sem=send_sems.at[idx], recv_sem=recv_sems.at[idx],
                device_id=device(r, target), device_id_type=MESH_ID,
            )
            incoming = pltpu.make_async_remote_copy(
                src_ref=group_of(arrived, part), dst_ref=group_of(arrived, part),
                send_sem=send_sems.at[idx], recv_sem=recv_sems.at[idx],
                device_id=device(r, source), device_id_type=MESH_ID,
            )
            send.start()
            sends.append(send)
            r["last"][sign] = incoming

    def stage(rings):
        for t in range(1, max(len(r["steps"]) for r in rings) + 1):
            for r in rings:
                step(r, t)
        for r in rings:
            for incoming in r["last"].values():
                incoming.wait_recv()

    height = piece_ref.shape[0]
    stage([
        ring("y", lambda k, p: out_ref.at[zi, k, p, cols[0]], lambda p: piece_ref.at[p, cols[0]], height),
        ring("z", lambda k, p: out_ref.at[k, yi, p, cols[1]], lambda p: piece_ref.at[p, cols[1]], height),
    ])
    own.wait()
    stage([
        ring("t", lambda k, p: rows_out.at[k, p, :], lambda p: rows_ref.at[p, :], rows_ref.shape[0]),
        ring("z", lambda k, p: out_ref.at[k, :, p, cols[0]], lambda p: out_ref.at[zi, :, p, cols[0]], height),
        ring("y", lambda k, p: out_ref.at[:, k, p, cols[1]], lambda p: out_ref.at[:, yi, p, cols[1]], height),
    ])
    own_rows.wait()
    for send in sends:
        send.wait_send()


def gather_blocks(piece, rows):
    ny, nz, nt = lax.axis_size("cy"), lax.axis_size("cz"), lax.axis_size("tp")
    height, width = piece.shape
    count = sum(2 * len(ring_steps(n)) for n in (ny, nz, nz, ny, nt))
    out, rows_out = pl.pallas_call(
        functools.partial(gather_kernel, ny, nz, nt),
        out_shape=(
            jax.ShapeDtypeStruct((nz, ny, height, width), piece.dtype),
            jax.ShapeDtypeStruct((nt,) + rows.shape, rows.dtype),
        ),
        in_specs=[pl.BlockSpec(memory_space=pltpu.VMEM)] * 2,
        out_specs=(pl.BlockSpec(memory_space=pl.ANY), pl.BlockSpec(memory_space=pl.ANY)),
        scratch_shapes=[
            pltpu.SemaphoreType.DMA((2,)),
            pltpu.SemaphoreType.DMA((count,)),
            pltpu.SemaphoreType.DMA((count,)),
        ],
        compiler_params=pltpu.CompilerParams(collective_id=1, has_side_effects=True),
    )(piece, rows)
    return out.reshape(nz * ny * height, width), rows_out.reshape(nt * rows.shape[0], rows.shape[1])


def scatter_kernel(nt, heads_ref, weight_ref, tokens_ref, out_ref, send_buf, recv_buf, send_sems, recv_sems):
    tp = lax.axis_index("tp")
    rows = out_ref.shape[0]
    half = out_ref.shape[1] // 2

    barrier = pltpu.get_barrier_semaphore()
    for peer in (lax.rem(tp + 1, nt), lax.rem(tp + nt - 1, nt)):
        pl.semaphore_signal(barrier, 1, device_id=(lax.axis_index("cz"), lax.axis_index("cy"), peer), device_id_type=MESH_ID)

    def own(chunk, side):
        start = pl.multiple_of(chunk * rows, 16)
        part = lax.dot_general(
            heads_ref[pl.ds(start, rows), :],
            weight_ref[side * half : (side + 1) * half, :],
            (((1,), (1,)), ((), ())),
            preferred_element_type=jnp.float32,
        )
        return part.astype(jnp.bfloat16).astype(jnp.float32)

    def copy(side, step, peer):
        slot = side * nt + step
        return pltpu.make_async_remote_copy(
            src_ref=send_buf.at[slot], dst_ref=recv_buf.at[slot], send_sem=send_sems.at[slot],
            recv_sem=recv_sems.at[slot],
            device_id=(lax.axis_index("cz"), lax.axis_index("cy"), peer), device_id_type=MESH_ID,
        )

    sides = ((0, 1), (1, -1))
    first = [own(lax.rem(tp + nt * nt - sign, nt), side) for side, sign in sides]
    pl.semaphore_wait(barrier, 2)
    for step in range(1, nt):
        mine = first if step == 1 else [
            own(lax.rem(tp + nt * nt - sign * step, nt), side) for side, sign in sides
        ]
        for side, sign in sides:
            total = mine[side]
            if step > 1:
                copy(side, step - 1, lax.rem(tp + nt - sign, nt)).wait_recv()
                total = total + recv_buf[side * nt + step - 1].astype(jnp.float32)
            send_buf[side * nt + step] = total.astype(jnp.bfloat16)
            copy(side, step, lax.rem(tp + nt + sign, nt)).start()
    last = [own(tp, side) for side, _ in sides]
    for side, sign in sides:
        copy(side, nt - 1, lax.rem(tp + nt - sign, nt)).wait_recv()
        total = last[side] + recv_buf[side * nt + nt - 1].astype(jnp.float32)
        summed = total.astype(jnp.bfloat16).astype(jnp.float32)
        residual = tokens_ref[:, side * half : (side + 1) * half].astype(jnp.float32)
        out_ref[:, side * half : (side + 1) * half] = (residual + summed).astype(out_ref.dtype)
    for step in range(1, nt):
        for side, sign in sides:
            copy(side, step, lax.rem(tp + nt + sign, nt)).wait_send()


def scatter_rows(heads, weight, tokens):
    nt = lax.axis_size("tp")
    rows = heads.shape[0] // nt
    width = weight.shape[0]
    return pl.pallas_call(
        functools.partial(scatter_kernel, nt),
        out_shape=jax.ShapeDtypeStruct((rows, width), jnp.bfloat16),
        in_specs=[pl.BlockSpec(memory_space=pltpu.VMEM)] * 3,
        out_specs=pl.BlockSpec(memory_space=pltpu.VMEM),
        scratch_shapes=[
            pltpu.VMEM((2 * nt, rows, width // 2), jnp.bfloat16),
            pltpu.VMEM((2 * nt, rows, width // 2), jnp.bfloat16),
            pltpu.SemaphoreType.DMA((2 * nt,)),
            pltpu.SemaphoreType.DMA((2 * nt,)),
        ],
        compiler_params=pltpu.CompilerParams(
            collective_id=2, has_side_effects=True, vmem_limit_bytes=48 * 1024 * 1024
        ),
    )(heads, weight, tokens)


def rms_rows(embedded_entries, norm_gain):
    token_float = embedded_entries.astype(jnp.float32)
    moment = jnp.mean(token_float * token_float, axis=1, keepdims=True)
    return (token_float * lax.rsqrt(moment + EPSILON) * norm_gain).astype(jnp.bfloat16)


def local_terms(queries, key_rows, values, log_forget, input_gate, starts):
    length = queries.shape[0]
    scaling = queries.shape[1] ** (-0.5)
    segment = jnp.cumsum(starts)
    levels = jnp.cumsum(log_forget)
    position = jnp.arange(length)
    allowed = (position[:, None] >= position[None, :]) & (segment[:, None] == segment[None, :])
    decays = jnp.where(
        allowed,
        jnp.exp(jnp.minimum(levels[:, None] - levels[None, :], 0.0) + input_gate[None, :]),
        0.0,
    )
    scores = jnp.dot(queries, key_rows.T, preferred_element_type=jnp.float32) * scaling
    weights = (scores * decays).astype(jnp.bfloat16)
    inner_part = jnp.dot(weights, values, preferred_element_type=jnp.float32)
    last_level = levels[-1]
    last_seg = segment[-1]
    keeping = jnp.where(segment == last_seg, jnp.exp(last_level - levels + input_gate), 0.0)
    weighted = (key_rows.astype(jnp.float32) * keeping[:, None]).astype(jnp.bfloat16)
    local_state = lax.dot_general(
        weighted, values, (((0,), (0,)), ((), ())), preferred_element_type=jnp.float32
    )
    passing = jnp.where(last_seg == 0, jnp.exp(last_level), 0.0)
    carried = jnp.where(segment == 0, jnp.exp(levels), 0.0) * scaling
    return (inner_part, local_state, passing, carried)


def apply_state(queries, carried, incoming):
    lifted = queries.astype(jnp.float32) * carried[:, None]
    return jnp.dot(
        lifted, incoming, precision=lax.Precision.HIGHEST, preferred_element_type=jnp.float32
    )


def head_norm(head_out, gain):
    centre = jnp.mean(head_out, axis=1, keepdims=True)
    shifted = head_out - centre
    spread = jnp.mean(shifted * shifted, axis=1, keepdims=True)
    return (shifted * lax.rsqrt(spread + EPSILON) * gain).astype(jnp.bfloat16)


def local(
    tokens,
    norm_gain,
    w_qkv,
    w_out,
    head_gain,
    input_codes,
    forget_codes,
    forget_bias,
    document_begin_flags,
):
    normed = rms_rows(tokens, norm_gain)
    width = w_qkv.shape[1]
    both, every_row_list = gather_blocks(jnp.concatenate([w_qkv, w_out.T], axis=1), normed)
    parameter_collection = both[:, :width]
    out_rows = both[:, width:]
    rows_combined = jnp.dot(
        every_row_list, parameter_collection, preferred_element_type=jnp.float32
    )
    rows_combined = rows_combined.astype(jnp.bfloat16)
    heads_here = forget_bias.shape[0]
    stride = 2 * DK + DV
    query_list, inner_list, state_list, passing_list, carried_list = ([], [], [], [], [])
    attention_slot_number = 0
    offset = attention_slot_number * stride
    queries = rows_combined[:, offset : offset + DK]
    key_rows = rows_combined[:, offset + DK : offset + 2 * DK]
    values = rows_combined[:, offset + 2 * DK : offset + stride]
    log_forget = jax.nn.log_sigmoid(
        FORGET_STEP * forget_codes[attention_slot_number].astype(jnp.float32)
        + forget_bias[attention_slot_number]
    )
    input_gate = INPUT_STEP * input_codes[attention_slot_number].astype(jnp.float32)
    inner_part, local_state, passing, carried = local_terms(
        queries, key_rows, values, log_forget, input_gate, document_begin_flags
    )
    query_list.append(queries)
    inner_list.append(inner_part)
    state_list.append(local_state)
    passing_list.append(passing)
    carried_list.append(carried)
    incoming = carried_in(passing_list[0], state_list[0])[None]
    attention_slot_number = 0
    head_out = inner_list[attention_slot_number] + apply_state(
        query_list[attention_slot_number],
        carried_list[attention_slot_number],
        incoming[attention_slot_number],
    )
    normed_heads = head_norm(head_out, head_gain)
    return scatter_rows(normed_heads, out_rows, tokens)


def solution(mesh):
    z_rows = 4 if mesh.shape["ctx"] % 4 == 0 else 1
    split = jax.sharding.Mesh(
        mesh.devices.reshape(mesh.shape["ctx"] // z_rows, z_rows, mesh.shape["tp"]), ("cz", "cy", "tp")
    )
    blocks = ("cz", "cy")
    placed = (
        P(blocks + ("tp",), None),
        P(),
        P(blocks, "tp"),
        P("tp", blocks),
        P("tp"),
        P("tp", blocks),
        P("tp", blocks),
        P("tp"),
        P(blocks),
    )
    return jax.shard_map(
        local, mesh=split, in_specs=placed, out_specs=P(blocks + ("tp",), None), check_vma=False
    )
```

```python
import functools

import jax
import jax.numpy as jnp
from jax import lax
from jax.experimental import pallas as pl
from jax.experimental.pallas import tpu as pltpu
from jax.sharding import PartitionSpec as P

DK = 256
DV = 512


EPSILON = 1e-06
FORGET_STEP = 0.5
INPUT_STEP = 0.5


MESH_ID = pl.DeviceIdType.MESH
DECAY_ROWS = 16


def scan_shifts(count):
    shifts = [1] + ([2] if count > 2 else [])
    k = 2
    while k < count:
        shifts.append(k)
        k *= 2
    return shifts


def pack(ref, total, decay):
    rows = total.shape[0]
    high = decay.astype(jnp.bfloat16)
    ref[:rows, :] = total.astype(jnp.bfloat16)
    ref[rows : rows + DECAY_ROWS, :] = high
    ref[rows + DECAY_ROWS :, :] = (decay - high.astype(jnp.float32)).astype(jnp.bfloat16)


def absorb(got, rows, acc_total, acc_decay):
    far_total = got[:rows].astype(jnp.float32)
    far_decay = got[rows : rows + DECAY_ROWS].astype(jnp.float32) + got[rows + DECAY_ROWS :].astype(jnp.float32)
    decay = acc_decay[...]
    acc_total[...] = decay[0:1, :] * far_total + acc_total[...]
    acc_decay[...] = decay * far_decay


def extend(got, rows, acc_total, acc_decay):
    far_total = got[:rows].astype(jnp.float32)
    far_decay = got[rows : rows + DECAY_ROWS].astype(jnp.float32) + got[rows + DECAY_ROWS :].astype(jnp.float32)
    acc_total[...] = far_decay[0:1, :] * acc_total[...] + far_total
    acc_decay[...] = far_decay * acc_decay[...]


def scan_kernel(
    ny, nz, zshifts, state_ref, decay_ref, out_ref,
    row_send, row_recv, z_send, z_recv, c_send, c_recv,
    prefix_total, prefix_decay, quarter_total, quarter_decay, z_total, z_decay,
    row_send_sems, row_recv_sems, z_send_sems, z_recv_sems, c_send_sems, c_recv_sems,
):
    yi = lax.axis_index("cy")
    zi = lax.axis_index("cz")
    tp = lax.axis_index("tp")
    rows, width = state_ref.shape
    quarter = width // ny

    barrier = pltpu.get_barrier_semaphore()
    z_partners = sorted(set(zshifts))
    for d in range(1, ny):
        pl.semaphore_signal(barrier, 1, device_id=(zi, lax.rem(yi + d, ny), tp), device_id_type=MESH_ID)
    for s in z_partners:
        for peer in (lax.rem(zi + s, nz), lax.rem(zi + nz - s, nz)):
            pl.semaphore_signal(barrier, 1, device_id=(peer, yi, tp), device_id_type=MESH_ID)
    pl.semaphore_wait(barrier, (ny - 1) + 2 * len(z_partners))

    def row_copy(d, target, slot, part):
        return pltpu.make_async_remote_copy(
            src_ref=row_send.at[part], dst_ref=row_recv.at[slot], send_sem=row_send_sems.at[d],
            recv_sem=row_recv_sems.at[slot], device_id=(zi, target, tp), device_id_type=MESH_ID,
        )

    for y in range(ny):
        pack(row_send.at[y], state_ref[:, y * quarter : (y + 1) * quarter], decay_ref[:, y * quarter : (y + 1) * quarter])
    for d in range(1, ny):
        target = lax.rem(yi + d, ny)
        row_copy(d, target, yi, target).start()
    for d in range(1, ny):
        row_copy(d, yi, lax.rem(yi + ny - d, ny), yi).wait_recv()

    quarter_total[...] = jnp.zeros_like(quarter_total)
    quarter_decay[...] = jnp.ones_like(quarter_decay)
    for y in range(ny):
        prefix_total[y] = quarter_total[...]
        prefix_decay[y] = quarter_decay[...]

        @pl.when(yi == y)
        def _():
            extend(row_send[y], rows, quarter_total, quarter_decay)

        @pl.when(yi != y)
        def _():
            extend(row_recv[y], rows, quarter_total, quarter_decay)

    def z_copy(j, slot, peer):
        return pltpu.make_async_remote_copy(
            src_ref=z_send.at[slot], dst_ref=z_recv.at[j], send_sem=z_send_sems.at[j],
            recv_sem=z_recv_sems.at[j], device_id=(peer, yi, tp), device_id_type=MESH_ID,
        )

    def z_send_round(j, slot):
        @pl.when(zi + zshifts[j] < nz)
        def _():
            z_copy(j, slot, zi + zshifts[j]).start()

    def z_absorb(j, slot):
        @pl.when(zi - zshifts[j] >= 0)
        def _():
            z_copy(j, slot, zi - zshifts[j]).wait_recv()
            absorb(z_recv[j], rows, z_total, z_decay)

    z_total[...] = jnp.zeros_like(z_total)
    z_decay[...] = jnp.ones_like(z_decay)
    first = min(2, len(zshifts))
    if zshifts:
        pack(z_send.at[0], quarter_total[...], quarter_decay[...])
    for j in range(first):
        z_send_round(j, 0)
    for j in range(first):
        z_absorb(j, 0)
    for j in range(first, len(zshifts)):
        pack(z_send.at[j - 1], z_total[...], z_decay[...])
        z_send_round(j, j - 1)
        z_absorb(j, j - 1)

    def c_copy(y, target, slot):
        return pltpu.make_async_remote_copy(
            src_ref=c_send.at[y], dst_ref=c_recv.at[slot], send_sem=c_send_sems.at[y],
            recv_sem=c_recv_sems.at[slot], device_id=(zi, target, tp), device_id_type=MESH_ID,
        )

    for y in range(ny):
        @pl.when(yi != y)
        def _():
            done = prefix_decay[y][0:1, :] * z_total[...] + prefix_total[y]
            c_send[y] = done.astype(jnp.bfloat16)
            c_copy(y, y, yi).start()

    for y in range(ny):
        @pl.when(yi == y)
        def _():
            out_ref[:, y * quarter : (y + 1) * quarter] = prefix_decay[y][0:1, :] * z_total[...] + prefix_total[y]

    for y in range(ny):
        @pl.when(yi != y)
        def _():
            c_copy(y, yi, y).wait_recv()
            out_ref[:, y * quarter : (y + 1) * quarter] = c_recv[y].astype(jnp.float32)

    for d in range(1, ny):
        target = lax.rem(yi + d, ny)
        row_copy(d, target, yi, target).wait_send()
    for y in range(ny):
        @pl.when(yi != y)
        def _():
            c_copy(y, y, yi).wait_send()
    for j in range(len(zshifts)):
        @pl.when(zi + zshifts[j] < nz)
        def _():
            z_copy(j, 0 if j < first else j - 1, zi + zshifts[j]).wait_send()


def carried_in(passing, state):
    ny, nz = lax.axis_size("cy"), lax.axis_size("cz")
    if ny * nz == 1:
        return jnp.zeros_like(state)
    zshifts = scan_shifts(nz) if nz > 1 else []
    rows, width = state.shape
    quarter = width // ny
    decay = jnp.broadcast_to(passing.reshape(1, 1), (DECAY_ROWS, width)).astype(jnp.float32)
    message = rows + 2 * DECAY_ROWS
    slots = max(len(zshifts), 1)
    return pl.pallas_call(
        functools.partial(scan_kernel, ny, nz, zshifts),
        out_shape=jax.ShapeDtypeStruct((rows, width), jnp.float32),
        in_specs=[pl.BlockSpec(memory_space=pltpu.VMEM)] * 2,
        out_specs=pl.BlockSpec(memory_space=pltpu.VMEM),
        scratch_shapes=[
            pltpu.VMEM((ny, message, quarter), jnp.bfloat16),
            pltpu.VMEM((ny, message, quarter), jnp.bfloat16),
            pltpu.VMEM((slots, message, quarter), jnp.bfloat16),
            pltpu.VMEM((slots, message, quarter), jnp.bfloat16),
            pltpu.VMEM((ny, rows, quarter), jnp.bfloat16),
            pltpu.VMEM((ny, rows, quarter), jnp.bfloat16),
            pltpu.VMEM((ny, rows, quarter), jnp.float32),
            pltpu.VMEM((ny, DECAY_ROWS, quarter), jnp.float32),
            pltpu.VMEM((rows, quarter), jnp.float32),
            pltpu.VMEM((DECAY_ROWS, quarter), jnp.float32),
            pltpu.VMEM((rows, quarter), jnp.float32),
            pltpu.VMEM((DECAY_ROWS, quarter), jnp.float32),
            pltpu.SemaphoreType.DMA((ny,)),
            pltpu.SemaphoreType.DMA((ny,)),
            pltpu.SemaphoreType.DMA((slots,)),
            pltpu.SemaphoreType.DMA((slots,)),
            pltpu.SemaphoreType.DMA((ny,)),
            pltpu.SemaphoreType.DMA((ny,)),
        ],
        compiler_params=pltpu.CompilerParams(collective_id=0, has_side_effects=True),
    )(state.astype(jnp.float32), decay)


def ring_steps(n):
    steps = [(s, True) for s in range(1, (n - 1) // 2 + 1)]
    if n % 2 == 0 and n > 1:
        steps.append((n // 2, False))
    return steps


def gather_kernel(ny, nz, nt, piece_ref, rows_ref, out_ref, rows_out, local_sem, send_sems, recv_sems):
    yi = lax.axis_index("cy")
    zi = lax.axis_index("cz")
    tp = lax.axis_index("tp")
    half = piece_ref.shape[1] // 2
    cols = (pl.ds(0, half), pl.ds(half, half))

    barrier = pltpu.get_barrier_semaphore()
    neighbours = [
        (zi, lax.rem(yi + 1, ny), tp),
        (zi, lax.rem(yi + ny - 1, ny), tp),
        (lax.rem(zi + 1, nz), yi, tp),
        (lax.rem(zi + nz - 1, nz), yi, tp),
        (zi, yi, lax.rem(tp + 1, nt)),
        (zi, yi, lax.rem(tp + nt - 1, nt)),
    ]
    for peer in neighbours:
        pl.semaphore_signal(barrier, 1, device_id=peer, device_id_type=MESH_ID)
    pl.semaphore_wait(barrier, len(neighbours))

    own = pltpu.make_async_copy(piece_ref, out_ref.at[zi, yi], local_sem.at[0])
    own.start()
    own_rows = pltpu.make_async_copy(rows_ref, rows_out.at[tp], local_sem.at[1])
    own_rows.start()
    sends = []

    def ring(along, group_of, first_src, height):
        n, me = {"y": (ny, yi), "z": (nz, zi), "t": (nt, tp)}[along]
        return dict(n=n, me=me, along=along, group_of=group_of, first_src=first_src, steps=ring_steps(n), last={}, height=height)

    def device(r, k):
        return {"y": (zi, k, tp), "z": (k, yi, tp), "t": (zi, yi, k)}[r["along"]]

    def step(r, t):
        if t > len(r["steps"]):
            return
        n, me, group_of = r["n"], r["me"], r["group_of"]
        hop, both = r["steps"][t - 1]
        whole = slice(None)
        half_rows = r["height"] // 2
        for sign in (1, -1):
            if both:
                part = whole
            else:
                part = pl.ds(0, half_rows) if sign == 1 else pl.ds(half_rows, half_rows)
            if t > 1:
                r["last"].pop(sign).wait_recv()
            origin = lax.rem(me + 2 * n - sign * (hop - 1), n)
            target = lax.rem(me + n + sign, n)
            source = lax.rem(me + n - sign, n)
            arrived = lax.rem(me + 2 * n - sign * hop, n)
            idx = len(sends)
            send = pltpu.make_async_remote_copy(
                src_ref=r["first_src"](part) if t == 1 else group_of(origin, part), dst_ref=group_of(origin, part),
                send_sem=send_sems.at[idx], recv_sem=recv_sems.at[idx],
                device_id=device(r, target), device_id_type=MESH_ID,
            )
            incoming = pltpu.make_async_remote_copy(
                src_ref=group_of(arrived, part), dst_ref=group_of(arrived, part),
                send_sem=send_sems.at[idx], recv_sem=recv_sems.at[idx],
                device_id=device(r, source), device_id_type=MESH_ID,
            )
            send.start()
            sends.append(send)
            r["last"][sign] = incoming

    def stage(rings):
        for t in range(1, max(len(r["steps"]) for r in rings) + 1):
            for r in rings:
                step(r, t)
        for r in rings:
            for incoming in r["last"].values():
                incoming.wait_recv()

    height = piece_ref.shape[0]
    stage([
        ring("y", lambda k, p: out_ref.at[zi, k, p, cols[0]], lambda p: piece_ref.at[p, cols[0]], height),
        ring("z", lambda k, p: out_ref.at[k, yi, p, cols[1]], lambda p: piece_ref.at[p, cols[1]], height),
    ])
    own.wait()
    stage([
        ring("t", lambda k, p: rows_out.at[k, p, :], lambda p: rows_ref.at[p, :], rows_ref.shape[0]),
        ring("z", lambda k, p: out_ref.at[k, :, p, cols[0]], lambda p: out_ref.at[zi, :, p, cols[0]], height),
        ring("y", lambda k, p: out_ref.at[:, k, p, cols[1]], lambda p: out_ref.at[:, yi, p, cols[1]], height),
    ])
    own_rows.wait()
    for send in sends:
        send.wait_send()


def gather_blocks(piece, rows):
    ny, nz, nt = lax.axis_size("cy"), lax.axis_size("cz"), lax.axis_size("tp")
    height, width = piece.shape
    count = sum(2 * len(ring_steps(n)) for n in (ny, nz, nz, ny, nt))
    out, rows_out = pl.pallas_call(
        functools.partial(gather_kernel, ny, nz, nt),
        out_shape=(
            jax.ShapeDtypeStruct((nz, ny, height, width), piece.dtype),
            jax.ShapeDtypeStruct((nt,) + rows.shape, rows.dtype),
        ),
        in_specs=[pl.BlockSpec(memory_space=pltpu.VMEM)] * 2,
        out_specs=(pl.BlockSpec(memory_space=pl.ANY), pl.BlockSpec(memory_space=pl.ANY)),
        scratch_shapes=[
            pltpu.SemaphoreType.DMA((2,)),
            pltpu.SemaphoreType.DMA((count,)),
            pltpu.SemaphoreType.DMA((count,)),
        ],
        compiler_params=pltpu.CompilerParams(collective_id=1, has_side_effects=True),
    )(piece, rows)
    return out.reshape(nz * ny * height, width), rows_out.reshape(nt * rows.shape[0], rows.shape[1])


def scatter_kernel(nt, heads_ref, weight_ref, out_ref, send_buf, recv_buf, send_sems, recv_sems):
    tp = lax.axis_index("tp")
    rows = out_ref.shape[0]
    half = out_ref.shape[1] // 2

    barrier = pltpu.get_barrier_semaphore()
    for peer in (lax.rem(tp + 1, nt), lax.rem(tp + nt - 1, nt)):
        pl.semaphore_signal(barrier, 1, device_id=(lax.axis_index("cz"), lax.axis_index("cy"), peer), device_id_type=MESH_ID)

    def own(chunk, side):
        start = pl.multiple_of(chunk * rows, 16)
        part = lax.dot_general(
            heads_ref[pl.ds(start, rows), :],
            weight_ref[side * half : (side + 1) * half, :],
            (((1,), (1,)), ((), ())),
            preferred_element_type=jnp.float32,
        )
        return part.astype(jnp.bfloat16).astype(jnp.float32)

    def copy(side, step, peer):
        slot = side * nt + step
        return pltpu.make_async_remote_copy(
            src_ref=send_buf.at[slot], dst_ref=recv_buf.at[slot], send_sem=send_sems.at[slot],
            recv_sem=recv_sems.at[slot],
            device_id=(lax.axis_index("cz"), lax.axis_index("cy"), peer), device_id_type=MESH_ID,
        )

    sides = ((0, 1), (1, -1))
    first = [own(lax.rem(tp + nt * nt - sign, nt), side) for side, sign in sides]
    pl.semaphore_wait(barrier, 2)
    for step in range(1, nt):
        mine = first if step == 1 else [
            own(lax.rem(tp + nt * nt - sign * step, nt), side) for side, sign in sides
        ]
        for side, sign in sides:
            total = mine[side]
            if step > 1:
                copy(side, step - 1, lax.rem(tp + nt - sign, nt)).wait_recv()
                total = total + recv_buf[side * nt + step - 1].astype(jnp.float32)
            send_buf[side * nt + step] = total.astype(jnp.bfloat16)
            copy(side, step, lax.rem(tp + nt + sign, nt)).start()
    last = [own(tp, side) for side, _ in sides]
    for side, sign in sides:
        copy(side, nt - 1, lax.rem(tp + nt - sign, nt)).wait_recv()
        total = last[side] + recv_buf[side * nt + nt - 1].astype(jnp.float32)
        out_ref[:, side * half : (side + 1) * half] = total.astype(out_ref.dtype)
    for step in range(1, nt):
        for side, sign in sides:
            copy(side, step, lax.rem(tp + nt + sign, nt)).wait_send()


def scatter_rows(heads, weight):
    nt = lax.axis_size("tp")
    rows = heads.shape[0] // nt
    width = weight.shape[0]
    return pl.pallas_call(
        functools.partial(scatter_kernel, nt),
        out_shape=jax.ShapeDtypeStruct((rows, width), jnp.bfloat16),
        in_specs=[pl.BlockSpec(memory_space=pltpu.VMEM)] * 2,
        out_specs=pl.BlockSpec(memory_space=pltpu.VMEM),
        scratch_shapes=[
            pltpu.VMEM((2 * nt, rows, width // 2), jnp.bfloat16),
            pltpu.VMEM((2 * nt, rows, width // 2), jnp.bfloat16),
            pltpu.SemaphoreType.DMA((2 * nt,)),
            pltpu.SemaphoreType.DMA((2 * nt,)),
        ],
        compiler_params=pltpu.CompilerParams(
            collective_id=2, has_side_effects=True, vmem_limit_bytes=48 * 1024 * 1024
        ),
    )(heads, weight)


def rms_rows(embedded_entries, norm_gain):
    token_float = embedded_entries.astype(jnp.float32)
    moment = jnp.mean(token_float * token_float, axis=1, keepdims=True)
    return (token_float * lax.rsqrt(moment + EPSILON) * norm_gain).astype(jnp.bfloat16)


def local_terms(queries, key_rows, values, log_forget, input_gate, starts):
    length = queries.shape[0]
    scaling = queries.shape[1] ** (-0.5)
    segment = jnp.cumsum(starts)
    levels = jnp.cumsum(log_forget)
    position = jnp.arange(length)
    allowed = (position[:, None] >= position[None, :]) & (segment[:, None] == segment[None, :])
    decays = jnp.where(
        allowed,
        jnp.exp(jnp.minimum(levels[:, None] - levels[None, :], 0.0) + input_gate[None, :]),
        0.0,
    )
    scores = jnp.dot(queries, key_rows.T, preferred_element_type=jnp.float32) * scaling
    weights = (scores * decays).astype(jnp.bfloat16)
    inner_part = jnp.dot(weights, values, preferred_element_type=jnp.float32)
    last_level = levels[-1]
    last_seg = segment[-1]
    keeping = jnp.where(segment == last_seg, jnp.exp(last_level - levels + input_gate), 0.0)
    weighted = (key_rows.astype(jnp.float32) * keeping[:, None]).astype(jnp.bfloat16)
    local_state = lax.dot_general(
        weighted, values, (((0,), (0,)), ((), ())), preferred_element_type=jnp.float32
    )
    passing = jnp.where(last_seg == 0, jnp.exp(last_level), 0.0)
    carried = jnp.where(segment == 0, jnp.exp(levels), 0.0) * scaling
    return (inner_part, local_state, passing, carried)


def apply_state(queries, carried, incoming):
    lifted = queries.astype(jnp.float32) * carried[:, None]
    return jnp.dot(
        lifted, incoming, precision=lax.Precision.HIGHEST, preferred_element_type=jnp.float32
    )


def head_norm(head_out, gain):
    centre = jnp.mean(head_out, axis=1, keepdims=True)
    shifted = head_out - centre
    spread = jnp.mean(shifted * shifted, axis=1, keepdims=True)
    return (shifted * lax.rsqrt(spread + EPSILON) * gain).astype(jnp.bfloat16)


def local(
    tokens,
    norm_gain,
    w_qkv,
    w_out,
    head_gain,
    input_codes,
    forget_codes,
    forget_bias,
    document_begin_flags,
):
    normed = rms_rows(tokens, norm_gain)
    width = w_qkv.shape[1]
    both, every_row_list = gather_blocks(jnp.concatenate([w_qkv, w_out.T], axis=1), normed)
    parameter_collection = both[:, :width]
    out_rows = both[:, width:]
    rows_combined = jnp.dot(
        every_row_list, parameter_collection, preferred_element_type=jnp.float32
    )
    rows_combined = rows_combined.astype(jnp.bfloat16)
    heads_here = forget_bias.shape[0]
    stride = 2 * DK + DV
    query_list, inner_list, state_list, passing_list, carried_list = ([], [], [], [], [])
    attention_slot_number = 0
    offset = attention_slot_number * stride
    queries = rows_combined[:, offset : offset + DK]
    key_rows = rows_combined[:, offset + DK : offset + 2 * DK]
    values = rows_combined[:, offset + 2 * DK : offset + stride]
    log_forget = jax.nn.log_sigmoid(
        FORGET_STEP * forget_codes[attention_slot_number].astype(jnp.float32)
        + forget_bias[attention_slot_number]
    )
    input_gate = INPUT_STEP * input_codes[attention_slot_number].astype(jnp.float32)
    inner_part, local_state, passing, carried = local_terms(
        queries, key_rows, values, log_forget, input_gate, document_begin_flags
    )
    query_list.append(queries)
    inner_list.append(inner_part)
    state_list.append(local_state)
    passing_list.append(passing)
    carried_list.append(carried)
    incoming = carried_in(passing_list[0], state_list[0])[None]
    attention_slot_number = 0
    head_out = inner_list[attention_slot_number] + apply_state(
        query_list[attention_slot_number],
        carried_list[attention_slot_number],
        incoming[attention_slot_number],
    )
    normed_heads = head_norm(head_out, head_gain)
    summed = scatter_rows(normed_heads, out_rows).astype(jnp.float32)
    return (tokens.astype(jnp.float32) + summed).astype(jnp.bfloat16)


def solution(mesh):
    z_rows = 4 if mesh.shape["ctx"] % 4 == 0 else 1
    split = jax.sharding.Mesh(
        mesh.devices.reshape(mesh.shape["ctx"] // z_rows, z_rows, mesh.shape["tp"]), ("cz", "cy", "tp")
    )
    blocks = ("cz", "cy")
    placed = (
        P(blocks + ("tp",), None),
        P(),
        P(blocks, "tp"),
        P("tp", blocks),
        P("tp"),
        P("tp", blocks),
        P("tp", blocks),
        P("tp"),
        P(blocks),
    )
    return jax.shard_map(
        local, mesh=split, in_specs=placed, out_specs=P(blocks + ("tp",), None), check_vma=False
    )
```
